32 devices in a mesh: shard: 2 (over core), ctx: 4 (over y, x), tp: 4 (over z).
Axes of the slice: x: 2, y: 2, z: 4, core: 2. Of those that a mesh axis runs over, the one named last changes fastest.
Arguments:
- first_half: bfloat16 [4096, 4, 1024], P('ctx', 'shard', 'tp'), may hold values from -6 to 6
- second_half: bfloat16 [4096, 4, 1024], P('ctx', 'shard', 'tp'), may hold values from -6 to 6
- first_cotangent: bfloat16 [4096, 4, 1024], P('ctx', 'shard', 'tp'), may hold values from -6 to 6
- second_cotangent: bfloat16 [4096, 4, 1024], P('ctx', 'shard', 'tp'), may hold values from -6 to 6
- segment_ids: int32 [4, 4096], P('shard', 'ctx'), may hold values from 0 to 3, as said below
- bucket_ids: int32 [4, 4, 4096], P('shard', None, 'ctx'), may hold values from 0 to 63
- positions: int32 [4, 4096], P('shard', 'ctx'), may hold values from 0 to 4095, as said below
- query_weight: bfloat16 [1024, 1024], P('shard', 'tp'), may hold values from -0.1875 to 0.1875
- value_weight: bfloat16 [1024, 1024], P('shard', 'tp'), may hold values from -0.1875 to 0.1875
- output_weight: bfloat16 [1024, 1024], P('tp', 'shard'), may hold values from -0.75 to 0.75
- expand_weight: bfloat16 [1024, 4096], P('shard', 'tp'), may hold values from -0.1875 to 0.1875
- expand_bias: float32 [4096], P('tp'), may hold values from -3 to 3
- shrink_weight: bfloat16 [4096, 1024], P('tp', 'shard'), may hold values from -0.09375 to 0.09375
- shrink_bias: float32 [1024], P('tp'), may hold values from -2 to 2
- attention_gain: float32 [1024], replicated, may hold values from 0.1 to 1.9
- attention_shift: float32 [1024], replicated, may hold values from -2 to 2
- forward_gain: float32 [1024], replicated, may hold values from 0.1 to 1.9
- forward_shift: float32 [1024], replicated, may hold values from -2 to 2
Outputs:
- first_out: bfloat16 [4096, 4, 1024], P('ctx', 'shard', 'tp')
- second_out: bfloat16 [4096, 4, 1024], P('ctx', 'shard', 'tp')
- first_grad: bfloat16 [4096, 4, 1024], P('ctx', 'shard', 'tp')
- second_grad: bfloat16 [4096, 4, 1024], P('ctx', 'shard', 'tp')
- query_grad: float32 [1024, 1024], P('shard', 'tp')
- value_grad: float32 [1024, 1024], P('shard', 'tp')
- output_grad: float32 [1024, 1024], P('tp', 'shard')
- expand_grad: float32 [1024, 4096], P('shard', 'tp')
- expand_bias_grad: float32 [4096], P('tp')
- shrink_grad: float32 [4096, 1024], P('tp', 'shard')
- shrink_bias_grad: float32 [1024], P('tp')
- attention_gain_grad: float32 [1024], P('tp')
- attention_shift_grad: float32 [1024], P('tp')
- forward_gain_grad: float32 [1024], P('tp')
- forward_shift_grad: float32 [1024], P('tp')
The draws below stay inside these ranges and needn't reach their ends.
Inputs may be any that keep to these rules, and one draw needn't show every extreme that they name: `segment_ids`: A document is a run of consecutive positions: ordered by positions, the numbers never fall; every document has a token; a document has at most 2000 tokens, and some document has exactly that many. Within each sequence the positions are a permutation of 0 to 4095.
All inputs are finite; a program needn't handle non-finite values.
Results may differ from the reference program's by a relative error of at most 0.019.
Values may be sent and summed in bfloat16 or wider, within the bound.
No kernel may reach another device: no remote copies, remote signals or barrier semaphores. Data moves between devices by JAX's collectives and lax.ppermute only.
A program may use at most 192 MiB of HBM per device.

```python
import jax
import jax.numpy as jnp
from jax import lax

D = 1024
H = 8
DH = 128
FF = 4096
ROUNDS = 4
NB = 64
LEN = 4096
DOC_MOST = 2000
SEQS = 4


def layout_of(key):

    def one_sequence(seq_key):
        perm_key, length_key, order_key = jax.random.split(seq_key, 3)
        places = jax.random.permutation(perm_key, LEN).astype(jnp.int32)
        rest = LEN - DOC_MOST
        quarter = rest // 3
        moves = jax.random.randint(length_key, (2,), -(quarter // 4), quarter // 4 + 1).astype(jnp.int32)
        lengths = jnp.stack([jnp.int32(DOC_MOST), quarter + moves[0], quarter - moves[0] + moves[1], rest - 2 * quarter - moves[1]]).astype(jnp.int32)
        ordered = lengths[jax.random.permutation(order_key, 4)]
        ends = jnp.cumsum(ordered).astype(jnp.int32)
        slots = jnp.arange(LEN, dtype=jnp.int32)
        by_place = jnp.sum((slots[:, None] >= ends[None, :3]).astype(jnp.int32), 1).astype(jnp.int32)
        return (places, by_place[places])
    keys = jax.random.split(jax.random.fold_in(key, 11), SEQS)
    return jax.vmap(one_sequence)(keys)


def draw_positions(key, part):
    return layout_of(key)[0]


def draw_segment_ids(key, part):
    return layout_of(key)[1]


def plant(array, key, smallest, largest):
    extent = array.shape
    index_at = [jax.random.randint(jax.random.fold_in(key, axis), (), 0, extent[axis]) for axis in range(len(extent))]
    array = array.at[tuple(index_at)].set(smallest)
    longest = extent.index(max(extent))
    index_at[longest] = (index_at[longest] + 1) % extent[longest]
    return array.at[tuple(index_at)].set(largest)


def steps_of(rng, dims, cuts, least, high):
    loudness = 1.0
    for position, shards_of in cuts:
        steps = jax.random.uniform(jax.random.fold_in(jax.random.fold_in(rng, 6), position), (shards_of,), jnp.float32, least / len(cuts), high / len(cuts))
        loudness = loudness * jnp.repeat(jnp.exp(steps), dims[position] // shards_of).reshape((-1,) + (1,) * (len(dims) - 1 - position))
    return loudness


def bell_draw(key, extent, scale, reach, shards=(), held_as=jnp.bfloat16):
    level = steps_of(key, extent, shards, -0.22, 0.18) if shards else 1.0
    result = jax.random.normal(key, extent, jnp.float32) * scale * level
    return jnp.minimum(jnp.maximum(result, -reach), reach).astype(held_as)


def setup_inputs(seed: int = 0) -> dict:
    key_of = jax.random.split(jax.random.key(seed), 19)
    first_half = bell_draw(key_of[0], (LEN, SEQS, D), 1.0, 6.0, ((0, 4), (1, 2), (2, 4)))
    second_half = bell_draw(key_of[1], (LEN, SEQS, D), 1.0, 6.0, ((0, 4), (1, 2), (2, 4)))
    first_cotangent = bell_draw(key_of[2], (LEN, SEQS, D), 1.0, 6.0, ((0, 4), (1, 2), (2, 4)))
    second_cotangent = bell_draw(key_of[3], (LEN, SEQS, D), 1.0, 6.0, ((0, 4), (1, 2), (2, 4)))
    segment_ids = draw_segment_ids(jax.random.fold_in(key_of[18], 71), 0)
    bucket_ids = plant(jax.random.randint(key_of[5], (SEQS, ROUNDS, LEN), 0, NB), jax.random.fold_in(key_of[5], 1), 0, NB - 1).astype(jnp.int32)
    positions = draw_positions(jax.random.fold_in(key_of[18], 71), 0)
    query_weight = bell_draw(key_of[7], (D, H * DH), D ** -0.5, 0.1875, ((0, 2), (1, 4)))
    value_weight = bell_draw(key_of[8], (D, H * DH), D ** -0.5, 0.1875, ((0, 2), (1, 4)))
    output_weight = bell_draw(key_of[9], (H * DH, D), (H * DH // 16) ** -0.5, 0.75, ((0, 4), (1, 2)))
    expand_weight = bell_draw(key_of[10], (D, FF), D ** -0.5, 0.1875, ((0, 2), (1, 4)))
    expand_bias = bell_draw(key_of[11], (FF,), 0.5, 3.0, ((0, 4),), jnp.float32)
    shrink_weight = bell_draw(key_of[12], (FF, D), FF ** -0.5, 0.09375, ((0, 4), (1, 2)))
    shrink_bias = bell_draw(key_of[13], (D,), 0.3, 2.0, ((0, 4),), jnp.float32)
    attention_gain = jnp.clip(1.0 + 0.18 * jax.random.normal(key_of[14], (D,), jnp.float32), 0.1, 1.9)
    attention_shift = bell_draw(key_of[15], (D,), 0.3, 2.0, (), jnp.float32)
    forward_gain = jnp.clip(1.0 + 0.18 * jax.random.normal(key_of[16], (D,), jnp.float32), 0.1, 1.9)
    forward_shift = bell_draw(key_of[17], (D,), 0.3, 2.0, (), jnp.float32)
    return {"first_half": first_half, "second_half": second_half, "first_cotangent": first_cotangent, "second_cotangent": second_cotangent, "segment_ids": segment_ids, "bucket_ids": bucket_ids, "positions": positions, "query_weight": query_weight, "value_weight": value_weight, "output_weight": output_weight, "expand_weight": expand_weight, "expand_bias": expand_bias, "shrink_weight": shrink_weight, "shrink_bias": shrink_bias, "attention_gain": attention_gain, "attention_shift": attention_shift, "forward_gain": forward_gain, "forward_shift": forward_shift}


HIGH = lax.Precision.HIGHEST
SELF_SCORE = -10.0
NEG_FILL = -1e+30

@jax.custom_vjp
def low(v):
    return lax.optimization_barrier(v.astype(jnp.bfloat16)).astype(jnp.float32)

@jax.custom_vjp
def low_back(v):
    return v

def low_keep(v):
    return (low(v), None)

def low_pass(kept, grad):
    return (grad,)

def back_keep(v):
    return (v, None)

def back_low(kept, grad):
    return (low(grad),)
low.defvjp(low_keep, low_pass)
low_back.defvjp(back_keep, back_low)

def layer_norm(rows_in, gain_row, shift_row):
    centre = lax.optimization_barrier(jnp.mean(rows_in, -1, keepdims=True))
    offset = rows_in - centre
    inverse = lax.rsqrt(lax.optimization_barrier(jnp.mean(offset * offset, -1, keepdims=True)) + 1e-05)
    return offset * inverse * gain_row + shift_row

def unit_keys(queries):
    shaped = queries.reshape(queries.shape[:-1] + (queries.shape[-1] // DH, DH))
    factor = lax.rsqrt(lax.optimization_barrier(jnp.mean(shaped * shaped, -1, keepdims=True)) + 1e-06) * DH ** (-0.5)
    return (shaped * factor).reshape(queries.shape)

def attend_sequence(queries, keys, values, segments, buckets, places):
    block = min(512, LEN)

    def one_block(begin_row):
        query_block = lax.dynamic_slice_in_dim(queries, begin_row, block, 0)
        query_seg = lax.dynamic_slice_in_dim(segments, begin_row, block, 0)
        query_buck = lax.dynamic_slice_in_dim(buckets, begin_row, block, 1)
        query_pos = lax.dynamic_slice_in_dim(places, begin_row, block, 0)
        scores = low_back(jnp.einsum('qhd,khd->hqk', query_block, keys, precision=HIGH))
        matches = lax.optimization_barrier(jnp.sum((query_buck[:, :, None] == buckets[:, None, :]).astype(jnp.int32), 0))
        same_doc = query_seg[:, None] == segments[None, :]
        earlier = places[None, :] < query_pos[:, None]
        itself = places[None, :] == query_pos[:, None]
        counts = jnp.where(itself, ROUNDS, jnp.where(earlier & same_doc, matches, 0)).astype(jnp.float32)[None]
        shifted = jnp.where(itself[None], SELF_SCORE, scores)
        usable = counts > 0
        highest = lax.optimization_barrier(jnp.max(jnp.where(usable, shifted, NEG_FILL), -1, keepdims=True))
        summed = lax.optimization_barrier(jnp.sum(jnp.where(usable, counts * jnp.exp(shifted - highest), 0.0), -1, keepdims=True))
        log_total = highest + jnp.log(summed)
        weights = jnp.where(usable, counts * jnp.exp(shifted - log_total), 0.0)
        return jnp.einsum('hqk,khd->qhd', low(weights), values, precision=HIGH)
    starts = jnp.arange(LEN // block, dtype=jnp.int32) * block
    return lax.map(jax.checkpoint(one_block), starts).reshape(LEN, H, DH)

def forward(first_in, second_in, query_w, value_w, output_w, expand_w, expand_b, shrink_w, shrink_b, att_gain, att_shift, ffn_gain, ffn_shift, segment_ids, bucket_ids, positions):
    normed = low(layer_norm(second_in, att_gain, att_shift))
    queries = low(low_back(jnp.einsum('psd,de->pse', normed, query_w, precision=HIGH)))
    keys = low(low_back(unit_keys(queries)))
    values = low(low_back(jnp.einsum('psd,de->pse', normed, value_w, precision=HIGH)))

    def per_sequence(packed):
        query_seq, key_seq, value_seq, seg_seq, buck_seq, pos_seq = packed
        return attend_sequence(query_seq.reshape(LEN, H, DH), key_seq.reshape(LEN, H, DH), value_seq.reshape(LEN, H, DH), seg_seq, buck_seq, pos_seq)
    mixture = lax.map(per_sequence, (queries.transpose(1, 0, 2), keys.transpose(1, 0, 2), values.transpose(1, 0, 2), segment_ids, bucket_ids, positions))
    attention = low(low_back(mixture.reshape(SEQS, LEN, H * DH).transpose(1, 0, 2)))
    branch = jnp.einsum('pse,ed->psd', attention, output_w, precision=HIGH)
    first_out = low(first_in + low_back(branch))
    ffn_in = low(layer_norm(first_out, ffn_gain, ffn_shift))
    pre_act = jnp.einsum('psd,df->psf', ffn_in, expand_w, precision=HIGH) + expand_b
    hidden = low(jax.nn.gelu(low_back(pre_act), approximate=False))
    second_branch = jnp.einsum('psf,fd->psd', hidden, shrink_w, precision=HIGH) + shrink_b
    second_out = low(second_in + low_back(second_branch))
    return (first_out, second_out)

def reference(first_half, second_half, first_cotangent, second_cotangent, segment_ids, bucket_ids, positions, query_weight, value_weight, output_weight, expand_weight, expand_bias, shrink_weight, shrink_bias, attention_gain, attention_shift, forward_gain, forward_shift):
    floats = [array_in.astype(jnp.float32) for array_in in (first_half, second_half, query_weight, value_weight, output_weight, expand_weight, expand_bias, shrink_weight, shrink_bias, attention_gain, attention_shift, forward_gain, forward_shift)]

    def run(*params):
        return forward(*params, segment_ids, bucket_ids, positions)
    outputs, pullback = jax.vjp(run, *floats)
    grads = pullback((first_cotangent.astype(jnp.float32), second_cotangent.astype(jnp.float32)))
    return (outputs[0].astype(jnp.bfloat16), outputs[1].astype(jnp.bfloat16), grads[0].astype(jnp.bfloat16), grads[1].astype(jnp.bfloat16), grads[2], grads[3], grads[4], grads[5], grads[6], grads[7], grads[8], grads[9], grads[10], grads[11], grads[12])
```

```python
import jax
import jax.numpy as jnp
from jax import lax
from jax.experimental import pallas as pl
from jax.experimental.pallas import tpu as pltpu
from jax.sharding import PartitionSpec as P

D = 1024
DH = 128
ROUNDS = 4


SELF_SCORE = -10.0
NEG_FILL = -1e30
BLOCK_ROWS = 512


BUCKETS = 64
HEADS = 8
SEQS = 4
TILE = 256
NT = (((1,), (1,)), ((), ()))
NN = (((1,), (0,)), ((), ()))


def dot(left, right, dims):
    return lax.dot_general(left, right, dims, preferred_element_type=jnp.float32)


def start_of(place, bounds_ref):
    start = jnp.where(place >= bounds_ref[0], bounds_ref[0], 0)
    start = jnp.where(place >= bounds_ref[1], bounds_ref[1], start)
    return jnp.where(place >= bounds_ref[2], bounds_ref[2], start)


def tile_masks(begin_row, bounds_ref):
    query_lane = lax.broadcasted_iota(jnp.int32, (1, TILE), 1)
    doc_start = start_of(query_lane + begin_row, bounds_ref)
    first = start_of(begin_row, bounds_ref) // TILE
    last_start = start_of(begin_row + TILE - 1, bounds_ref)
    full = jnp.minimum((last_start + TILE - 1) // TILE, begin_row // TILE)
    return doc_start, first, full


def rows_at(ref, block):
    return ref[pl.ds(pl.multiple_of(block * TILE, TILE), TILE), :]


def norm_factor(q):
    return lax.rsqrt(jnp.mean(q * q, -1, keepdims=True) + 1e-06)


def attend_kernel(bounds_ref, q_ref, v_ref, hot_ref, out_ref, log_ref, key_sc, vt_sc):
    block = pl.program_id(0)
    blocks = pl.num_programs(0)

    @pl.when(block == 0)
    def _():
        def prep(at, carry):
            q = rows_at(q_ref, at).astype(jnp.float32)
            begin = pl.multiple_of(at * TILE, TILE)
            key_sc[pl.ds(begin, TILE), :] = (q * (norm_factor(q) * DH ** (-0.5))).astype(jnp.bfloat16)
            v = rows_at(v_ref, at).astype(jnp.float32)
            vt_sc[:, pl.ds(begin, TILE)] = v.T.astype(jnp.bfloat16)
            return carry

        lax.fori_loop(0, blocks, prep, 0)

    begin_row = block * TILE
    doc_start, first, full = tile_masks(begin_row, bounds_ref)
    q = rows_at(q_ref, block)
    hot = rows_at(hot_ref, block)
    key_row = lax.broadcasted_iota(jnp.int32, (TILE, 1), 0)
    lane = lax.broadcasted_iota(jnp.int32, (1, TILE), 1)

    def scores(at):
        return dot(rows_at(key_sc, at), q, NT), dot(rows_at(hot_ref, at), hot, NT)

    def vt(at):
        return vt_sc[:, pl.ds(pl.multiple_of(at * TILE, TILE), TILE)]

    s, c = scores(block)
    place = key_row + begin_row
    c = jnp.where((key_row < lane) & (place >= doc_start), c, 0.0)
    itself = key_row == lane
    c = jnp.where(itself, float(ROUNDS), c)
    s = jnp.where(itself, SELF_SCORE, s)
    s = jnp.where(c > 0, s, NEG_FILL)
    high = jnp.max(s, 0, keepdims=True)
    p = c * jnp.exp(s - high)
    total = jnp.sum(p, 0, keepdims=True)
    acc = dot(vt(block), p.astype(jnp.bfloat16), NN)

    def fold(at, carry, masked):
        high, total, acc = carry
        s, c = scores(at)
        if masked:
            c = jnp.where(key_row + at * TILE >= doc_start, c, 0.0)
        s = jnp.where(c > 0, s, NEG_FILL)
        new_high = jnp.maximum(high, jnp.max(s, 0, keepdims=True))
        fade = jnp.exp(high - new_high)
        p = c * jnp.exp(s - new_high)
        total = total * fade + jnp.sum(p, 0, keepdims=True)
        acc = acc * fade + dot(vt(at), p.astype(jnp.bfloat16), NN)
        return new_high, total, acc

    carry = lax.fori_loop(first, full, lambda at, x: fold(at, x, True), (high, total, acc))
    high, total, acc = lax.fori_loop(full, block, lambda at, x: fold(at, x, False), carry)
    out_ref[...] = acc / total
    log_ref[pl.ds(block, 1), :] = high + jnp.log(total)


def attend(bounds, q, v, hot):
    rows = q.shape[0]
    blocks = rows // TILE
    whole = lambda shape: pl.BlockSpec(shape, lambda i, *_: (0,) * len(shape))
    return pl.pallas_call(
        attend_kernel,
        name="attend",
        out_shape=(
            jax.ShapeDtypeStruct((DH, rows), jnp.float32),
            jax.ShapeDtypeStruct((blocks, TILE), jnp.float32),
        ),
        grid_spec=pltpu.PrefetchScalarGridSpec(
            num_scalar_prefetch=1,
            grid=(blocks,),
            in_specs=[whole((rows, DH)), whole((rows, DH)), whole((rows, ROUNDS * BUCKETS))],
            out_specs=[pl.BlockSpec((DH, TILE), lambda i, *_: (0, i)), whole((blocks, TILE))],
            scratch_shapes=[pltpu.VMEM((rows, DH), jnp.bfloat16), pltpu.VMEM((DH, rows), jnp.bfloat16)],
        ),
        compiler_params=pltpu.CompilerParams(
            dimension_semantics=("arbitrary",), vmem_limit_bytes=40 * 2**20
        ),
        cost_estimate=pl.CostEstimate(
            flops=rows * rows * 256, bytes_accessed=rows * DH * 20, transcendentals=rows * rows // 4
        ),
    )(bounds, q, v, hot)


def attend_back_kernel(
    bounds_ref, q_ref, v_ref, hot_ref, grad_ref, out_ref, log_ref,
    q_grad_ref, v_grad_ref, key_sc, kt_sc, dk_sc, dv_sc, dq_sc,
):
    block = pl.program_id(0)
    blocks = pl.num_programs(0)

    @pl.when(block == 0)
    def _():
        def prep(at, carry):
            begin = pl.multiple_of(at * TILE, TILE)
            q = rows_at(q_ref, at).astype(jnp.float32)
            k = q * (norm_factor(q) * DH ** (-0.5))
            key_sc[pl.ds(begin, TILE), :] = k.astype(jnp.bfloat16)
            kt_sc[:, pl.ds(begin, TILE)] = k.T.astype(jnp.bfloat16)
            dk_sc[pl.ds(begin, TILE), :] = jnp.zeros((TILE, DH), jnp.float32)
            dv_sc[pl.ds(begin, TILE), :] = jnp.zeros((TILE, DH), jnp.float32)
            return carry

        lax.fori_loop(0, blocks, prep, 0)

    begin_row = block * TILE
    doc_start, first, full = tile_masks(begin_row, bounds_ref)
    q = rows_at(q_ref, block)
    hot = rows_at(hot_ref, block)
    grad = rows_at(grad_ref, block)
    log_row = log_ref[pl.ds(block, 1), :]
    delta = jnp.sum(grad.astype(jnp.float32).T * out_ref[...], 0, keepdims=True)
    key_row = lax.broadcasted_iota(jnp.int32, (TILE, 1), 0)
    lane = lax.broadcasted_iota(jnp.int32, (1, TILE), 1)

    def fold(at, acc, masked, diagonal=False):
        begin = pl.multiple_of(at * TILE, TILE)
        s = dot(rows_at(key_sc, at), q, NT)
        c = dot(rows_at(hot_ref, at), hot, NT)
        up = dot(rows_at(v_ref, at), grad, NT)
        if diagonal:
            itself = key_row == lane
            c = jnp.where((key_row < lane) & (key_row + begin_row >= doc_start), c, 0.0)
            c = jnp.where(itself, float(ROUNDS), c)
            s = jnp.where(itself, SELF_SCORE, s)
        elif masked:
            c = jnp.where(key_row + begin >= doc_start, c, 0.0)
        s = jnp.where(c > 0, s, NEG_FILL)
        w = c * jnp.exp(s - log_row)
        ds = w * (up - delta)
        if diagonal:
            ds = jnp.where(itself, 0.0, ds)
        w = w.astype(jnp.bfloat16)
        ds = ds.astype(jnp.bfloat16)
        dv_sc[pl.ds(begin, TILE), :] += dot(w, grad, NN)
        dk_sc[pl.ds(begin, TILE), :] += dot(ds, q, NN)
        return acc + dot(kt_sc[:, pl.ds(begin, TILE)], ds, NN)

    acc = fold(block, jnp.zeros((DH, TILE), jnp.float32), True, True)
    acc = lax.fori_loop(first, full, lambda at, x: fold(at, x, True), acc)
    acc = lax.fori_loop(full, block, lambda at, x: fold(at, x, False), acc)
    dq_sc[pl.ds(pl.multiple_of(begin_row, TILE), TILE), :] = acc.T

    @pl.when(block == blocks - 1)
    def _():
        def finish(at, carry):
            begin = pl.multiple_of(at * TILE, TILE)
            q = rows_at(q_ref, at).astype(jnp.float32)
            r = norm_factor(q)
            g = rows_at(dk_sc, at).astype(jnp.bfloat16).astype(jnp.float32)
            back = (r * DH ** (-0.5)) * (g - q * (r * r * jnp.mean(q * g, -1, keepdims=True)))
            q_grad_ref[pl.ds(begin, TILE), :] = (rows_at(dq_sc, at) + back).astype(jnp.bfloat16)
            v_grad_ref[pl.ds(begin, TILE), :] = rows_at(dv_sc, at).astype(jnp.bfloat16)
            return carry

        lax.fori_loop(0, blocks, finish, 0)


def attend_back(bounds, q, v, hot, grad, out, logs):
    rows = q.shape[0]
    blocks = rows // TILE
    whole = lambda shape: pl.BlockSpec(shape, lambda i, *_: (0,) * len(shape))
    return pl.pallas_call(
        attend_back_kernel,
        name="attend_back",
        out_shape=(jax.ShapeDtypeStruct((rows, DH), jnp.bfloat16),) * 2,
        grid_spec=pltpu.PrefetchScalarGridSpec(
            num_scalar_prefetch=1,
            grid=(blocks,),
            in_specs=[
                whole((rows, DH)), whole((rows, DH)), whole((rows, ROUNDS * BUCKETS)), whole((rows, DH)),
                pl.BlockSpec((DH, TILE), lambda i, *_: (0, i)), whole((blocks, TILE)),
            ],
            out_specs=[whole((rows, DH))] * 2,
            scratch_shapes=[
                pltpu.VMEM((rows, DH), jnp.bfloat16),
                pltpu.VMEM((DH, rows), jnp.bfloat16),
                pltpu.VMEM((rows, DH), jnp.float32),
                pltpu.VMEM((rows, DH), jnp.float32),
                pltpu.VMEM((rows, DH), jnp.float32),
            ],
        ),
        compiler_params=pltpu.CompilerParams(
            dimension_semantics=("arbitrary",), vmem_limit_bytes=48 * 2**20
        ),
        cost_estimate=pl.CostEstimate(
            flops=rows * rows * 640, bytes_accessed=rows * DH * 30, transcendentals=rows * rows // 4
        ),
    )(bounds, q, v, hot, grad, out, logs)


def place_matrix(places):
    rows = places.shape[0]
    return (jnp.arange(rows, dtype=jnp.int32)[:, None] == places[None, :]).astype(jnp.bfloat16)


def into_places(places, vectors):
    return jnp.einsum("pa,ad->pd", place_matrix(places), vectors, preferred_element_type=jnp.float32).astype(jnp.bfloat16)


def out_of_places(places, vectors):
    return jnp.einsum("pa,pd->ad", place_matrix(places), vectors, preferred_element_type=jnp.float32).astype(jnp.bfloat16)


def bucket_hot(buckets):
    hot = buckets.T[:, :, None] == jnp.arange(BUCKETS, dtype=jnp.int32)
    return hot.astype(jnp.bfloat16).reshape(buckets.shape[1], ROUNDS * BUCKETS)


def doc_bounds(segments):
    return jnp.sum((segments[None, :] < jnp.arange(1, 4, dtype=jnp.int32)[:, None]).astype(jnp.int32), 1)


def smooth_unit(values_in):
    return jax.nn.gelu(values_in, approximate=False)


def norm_rows(rows_wide, gain_row, shift_row):
    centre = jnp.mean(rows_wide, -1, keepdims=True)
    offset = rows_wide - centre
    inverse = lax.rsqrt(jnp.mean(offset * offset, -1, keepdims=True) + 1e-05)
    scaled = offset * inverse
    return (scaled * gain_row + shift_row, scaled, inverse)


def unit_keys(queries):
    shaped = queries.reshape(queries.shape[:-1] + (queries.shape[-1] // DH, DH))
    factor = lax.rsqrt(jnp.mean(shaped * shaped, -1, keepdims=True) + 1e-06) * DH ** (-0.5)
    return (shaped * factor).reshape(queries.shape)


def heads_view(vectors):
    return vectors.reshape(vectors.shape[0], vectors.shape[1], vectors.shape[2] // DH, DH)


def full_rows(sliced):
    return lax.all_gather(sliced, "tp", axis=2, tiled=True)


def branch_sum(partial_value):
    return lax.psum_scatter(partial_value, "tp", scatter_dimension=2, tiled=True)


def norm_back(grad_slice, scaled_slice, inverse, gain_slice):
    weighted = grad_slice * gain_slice
    first_sum, second_sum = lax.psum(
        (jnp.sum(weighted, -1, keepdims=True), jnp.sum(weighted * scaled_slice, -1, keepdims=True)),
        "tp",
    )
    inner = inverse * (weighted - first_sum / D - scaled_slice * (second_sum / D))
    return (inner, jnp.sum(grad_slice * scaled_slice, (0, 1)), jnp.sum(grad_slice, (0, 1)))


def label_rows(all_labels, begin_row, extent):
    all_segments, all_buckets, all_positions = all_labels
    return (
        lax.dynamic_slice_in_dim(all_segments, begin_row, extent, 1),
        lax.dynamic_slice_in_dim(all_buckets, begin_row, extent, 2),
        lax.dynamic_slice_in_dim(all_positions, begin_row, extent, 1),
    )


def block_weights(query_heads, query_labels, key_heads, key_labels):
    query_seg, query_buck, query_pos = query_labels
    key_seg, key_buck, key_pos = key_labels
    scores = jnp.einsum(
        "pshd,kshd->shpk", query_heads, key_heads, preferred_element_type=jnp.float32
    )
    matches = jnp.sum((query_buck[:, :, :, None] == key_buck[:, :, None, :]).astype(jnp.int32), 1)
    same_doc = query_seg[:, :, None] == key_seg[:, None, :]
    earlier = key_pos[:, None, :] < query_pos[:, :, None]
    itself = key_pos[:, None, :] == query_pos[:, :, None]
    counts = jnp.where(itself, ROUNDS, jnp.where(earlier & same_doc, matches, 0)).astype(
        jnp.float32
    )[:, None]
    shifted = jnp.where(itself[:, None], SELF_SCORE, scores)
    return (shifted, counts, itself[:, None])


def weights_of(shifted, counts, log_total):
    return jnp.where(counts > 0, counts * jnp.exp(shifted - log_total[..., None]), 0.0)


def blockwise(advance, running, row_count):
    extent = BLOCK_ROWS

    def turn(state_now, block_index):
        return (advance(state_now, block_index * extent, extent), None)

    return lax.scan(turn, running, jnp.arange(row_count // extent, dtype=jnp.int32))[0]


def over_keys(key_vectors, value_vectors, folder, initial):
    return folder(
        initial,
        (
            lax.all_gather(key_vectors, "ctx", axis=0, tiled=True),
            lax.all_gather(value_vectors, "ctx", axis=0, tiled=True),
        ),
        jnp.int32(0),
    )


def over_context(first_part, second_part, third_part, fourth_part, fifth_part):
    return (
        lax.psum(first_part.astype(jnp.bfloat16), "ctx").astype(jnp.float32),
        lax.psum(second_part.astype(jnp.bfloat16), "ctx").astype(jnp.float32),
        lax.psum(third_part.astype(jnp.bfloat16), "ctx").astype(jnp.float32),
        lax.psum(fourth_part.astype(jnp.bfloat16), "ctx").astype(jnp.float32),
        lax.psum(fifth_part.astype(jnp.bfloat16), "ctx").astype(jnp.float32),
    )


def to_row_owners(first_part, second_part, third_part):
    return (
        lax.psum_scatter(
            first_part.astype(jnp.bfloat16), "shard", scatter_dimension=0, tiled=True
        ).astype(jnp.float32),
        lax.psum_scatter(
            second_part.astype(jnp.bfloat16), "shard", scatter_dimension=0, tiled=True
        ).astype(jnp.float32),
        lax.psum_scatter(
            third_part.astype(jnp.bfloat16), "shard", scatter_dimension=0, tiled=True
        ).astype(jnp.float32),
    )


def to_col_owners(first_part, second_part):
    return (
        lax.psum_scatter(
            first_part.astype(jnp.bfloat16), "shard", scatter_dimension=1, tiled=True
        ).astype(jnp.float32),
        lax.psum_scatter(
            second_part.astype(jnp.bfloat16), "shard", scatter_dimension=1, tiled=True
        ).astype(jnp.float32),
    )


def general_device(
    first_half,
    second_half,
    first_cotangent,
    second_cotangent,
    segment_ids,
    bucket_ids,
    positions,
    query_weight,
    value_weight,
    output_weight,
    expand_weight,
    expand_bias,
    shrink_weight,
    shrink_bias,
    attention_gain,
    attention_shift,
    forward_gain,
    forward_shift,
):
    rows_here, seqs_here, slice_width = first_half.shape
    width_heads = query_weight.shape[1]
    heads_here = width_heads // DH
    tp_start = lax.axis_index("tp") * slice_width
    ctx_start = lax.axis_index("ctx") * rows_here
    bf16 = jnp.bfloat16
    f32 = jnp.float32

    def columns(wide):
        return lax.dynamic_slice_in_dim(wide, tp_start, slice_width, wide.ndim - 1)

    full_query, full_value, full_expand = (
        lax.all_gather(query_weight, "shard", axis=0, tiled=True),
        lax.all_gather(value_weight, "shard", axis=0, tiled=True),
        lax.all_gather(expand_weight, "shard", axis=0, tiled=True),
    )
    full_output, full_shrink = (
        lax.all_gather(output_weight, "shard", axis=1, tiled=True),
        lax.all_gather(shrink_weight, "shard", axis=1, tiled=True),
    )
    all_labels = (
        lax.all_gather(segment_ids, "ctx", axis=1, tiled=True),
        lax.all_gather(bucket_ids, "ctx", axis=2, tiled=True),
        lax.all_gather(positions, "ctx", axis=1, tiled=True),
    )
    local_labels = label_rows(all_labels, ctx_start, rows_here)
    second_wide = full_rows(second_half)
    normed, attn_scaled, attn_inverse = norm_rows(
        second_wide.astype(f32), attention_gain, attention_shift
    )
    normed = normed.astype(bf16)
    queries = jnp.einsum("psd,de->pse", normed, full_query, preferred_element_type=f32).astype(bf16)
    key_vectors = unit_keys(queries.astype(f32)).astype(bf16)
    value_vectors = jnp.einsum(
        "psd,de->pse", normed, full_value, preferred_element_type=f32
    ).astype(bf16)
    query_heads = heads_view(queries)
    stat_shape = (seqs_here, heads_here, rows_here)
    head_zero = jnp.zeros((rows_here, seqs_here, heads_here, DH), f32)

    def norm_fold(running, pieces, begin_row):
        key_piece = pieces[0]

        def advance(state_now, offset, extent):
            highest, summed = state_now
            key_heads = heads_view(lax.dynamic_slice_in_dim(key_piece, offset, extent, 0))
            shifted, counts, _ = block_weights(
                query_heads, local_labels, key_heads, label_rows(all_labels, offset, extent)
            )
            usable = counts > 0
            new_high = jnp.maximum(highest, jnp.max(jnp.where(usable, shifted, NEG_FILL), -1))
            summed = summed * jnp.exp(highest - new_high) + jnp.sum(
                jnp.where(usable, counts * jnp.exp(shifted - new_high[..., None]), 0.0), -1
            )
            return (new_high, summed)

        return blockwise(advance, running, key_piece.shape[0])

    highest, summed = over_keys(
        key_vectors,
        value_vectors,
        norm_fold,
        (jnp.full(stat_shape, NEG_FILL, f32), jnp.zeros(stat_shape, f32)),
    )
    log_total = highest + jnp.log(summed)

    def key_block(pieces, offset, extent):
        key_heads = heads_view(lax.dynamic_slice_in_dim(pieces[0], offset, extent, 0))
        value_heads = heads_view(lax.dynamic_slice_in_dim(pieces[1], offset, extent, 0))
        shifted, counts, itself = block_weights(
            query_heads, local_labels, key_heads, label_rows(all_labels, offset, extent)
        )
        return (key_heads, value_heads, weights_of(shifted, counts, log_total), itself)

    def mix_fold(running, pieces, begin_row):

        def advance(state_now, offset, extent):
            key_heads, value_heads, weights, itself = key_block(pieces, offset, extent)
            return state_now + jnp.einsum(
                "shpk,kshd->pshd", weights.astype(bf16), value_heads, preferred_element_type=f32
            )

        return blockwise(advance, running, pieces[0].shape[0])

    head_mix = over_keys(key_vectors, value_vectors, mix_fold, head_zero)
    attention = head_mix.reshape(rows_here, seqs_here, width_heads).astype(bf16)
    branch = branch_sum(
        jnp.einsum("pse,ed->psd", attention, full_output, preferred_element_type=f32)
    )
    first_out = (first_half.astype(f32) + branch).astype(bf16)
    first_wide = full_rows(first_out)
    ffn_in, ffn_scaled, ffn_inverse = norm_rows(first_wide.astype(f32), forward_gain, forward_shift)
    ffn_in = ffn_in.astype(bf16)
    pre_act = (
        jnp.einsum("psd,df->psf", ffn_in, full_expand, preferred_element_type=f32) + expand_bias
    )
    hidden_exact, unit_pull = jax.vjp(smooth_unit, pre_act)
    hidden = hidden_exact.astype(bf16)
    second_branch = (
        branch_sum(jnp.einsum("psf,fd->psd", hidden, full_shrink, preferred_element_type=f32))
        + shrink_bias
    )
    second_out = (second_half.astype(f32) + second_branch).astype(bf16)
    cotangent_wide = full_rows(second_cotangent)
    hidden_grad = jnp.einsum("psd,fd->psf", cotangent_wide, full_shrink, preferred_element_type=f32)
    pre_grad = unit_pull(hidden_grad)[0].astype(bf16)
    shrink_grad = jnp.einsum("psf,psd->fd", hidden, cotangent_wide, preferred_element_type=f32)
    shrink_bias_grad = jnp.sum(second_cotangent.astype(f32), (0, 1))
    expand_grad = jnp.einsum("psd,psf->df", ffn_in, pre_grad, preferred_element_type=f32)
    expand_bias_grad = jnp.sum(pre_grad.astype(f32), (0, 1))
    ffn_grad = branch_sum(
        jnp.einsum("psf,df->psd", pre_grad, full_expand, preferred_element_type=f32)
    )
    ffn_back, forward_gain_grad, forward_shift_grad = norm_back(
        ffn_grad, columns(ffn_scaled), ffn_inverse, columns(forward_gain)
    )
    first_grad = (first_cotangent.astype(f32) + ffn_back).astype(bf16)
    grad_wide = full_rows(first_grad)
    output_grad = jnp.einsum("pse,psd->ed", attention, grad_wide, preferred_element_type=f32)
    attention_grad = jnp.einsum(
        "psd,ed->pse", grad_wide, full_output, preferred_element_type=f32
    ).astype(bf16)
    grad_heads = heads_view(attention_grad)

    def delta_fold(running, pieces, begin_row):

        def advance(state_now, offset, extent):
            key_heads, value_heads, weights, itself = key_block(pieces, offset, extent)
            upstream = jnp.einsum(
                "pshd,kshd->shpk", grad_heads, value_heads, preferred_element_type=f32
            )
            return state_now + jnp.sum(weights * upstream, -1)

        return blockwise(advance, running, pieces[0].shape[0])

    row_delta = over_keys(key_vectors, value_vectors, delta_fold, jnp.zeros(stat_shape, f32))

    def query_fold(running, pieces, begin_row):

        def advance(state_now, offset, extent):
            key_heads, value_heads, weights, itself = key_block(pieces, offset, extent)
            upstream = jnp.einsum(
                "pshd,kshd->shpk", grad_heads, value_heads, preferred_element_type=f32
            )
            score_grad = jnp.where(itself, 0.0, weights * (upstream - row_delta[..., None])).astype(
                bf16
            )
            return state_now + jnp.einsum(
                "shpk,kshd->pshd", score_grad, key_heads, preferred_element_type=f32
            )

        return blockwise(advance, running, pieces[0].shape[0])

    query_part = over_keys(key_vectors, value_vectors, query_fold, head_zero)
    query_lse, query_delta = (
        lax.all_gather(log_total, "ctx", axis=2, tiled=True),
        lax.all_gather(row_delta, "ctx", axis=2, tiled=True),
    )
    local_keys = heads_view(key_vectors)
    local_values = heads_view(value_vectors)
    query_piece = lax.all_gather(queries, "ctx", axis=0, tiled=True)
    grad_piece = lax.all_gather(attention_grad, "ctx", axis=0, tiled=True)

    def advance(state_now, offset, extent):
        remote_queries = heads_view(lax.dynamic_slice_in_dim(query_piece, offset, extent, 0))
        remote_grads = heads_view(lax.dynamic_slice_in_dim(grad_piece, offset, extent, 0))
        lse_rows = lax.dynamic_slice_in_dim(query_lse, offset, extent, 2)
        delta_rows = lax.dynamic_slice_in_dim(query_delta, offset, extent, 2)
        shifted, counts, itself = block_weights(
            remote_queries, label_rows(all_labels, offset, extent), local_keys, local_labels
        )
        weights = weights_of(shifted, counts, lse_rows)
        upstream = jnp.einsum(
            "pshd,kshd->shpk", remote_grads, local_values, preferred_element_type=f32
        )
        score_grad = jnp.where(itself, 0.0, weights * (upstream - delta_rows[..., None])).astype(
            bf16
        )
        key_now = state_now[0] + jnp.einsum(
            "shpk,pshd->kshd", score_grad, remote_queries, preferred_element_type=f32
        )
        value_now = state_now[1] + jnp.einsum(
            "shpk,pshd->kshd", weights.astype(bf16), remote_grads, preferred_element_type=f32
        )
        return (key_now, value_now)

    key_part, value_part = blockwise(advance, (head_zero, head_zero), query_piece.shape[0])
    keys_grad = key_part.reshape(rows_here, seqs_here, width_heads).astype(bf16)
    values_grad = value_part.reshape(rows_here, seqs_here, width_heads).astype(bf16)
    unit_back = jax.vjp(unit_keys, queries.astype(f32))[1]
    queries_total = (
        query_part.reshape(rows_here, seqs_here, width_heads) + unit_back(keys_grad.astype(f32))[0]
    ).astype(bf16)
    query_grad = jnp.einsum("psd,pse->de", normed, queries_total, preferred_element_type=f32)
    value_grad = jnp.einsum("psd,pse->de", normed, values_grad, preferred_element_type=f32)
    normed_grad = branch_sum(
        jnp.einsum("pse,de->psd", queries_total, full_query, preferred_element_type=f32)
        + jnp.einsum("pse,de->psd", values_grad, full_value, preferred_element_type=f32)
    )
    attn_back, attention_gain_grad, attention_shift_grad = norm_back(
        normed_grad, columns(attn_scaled), attn_inverse, columns(attention_gain)
    )
    second_grad = (second_cotangent.astype(f32) + attn_back).astype(bf16)
    expand_bias_sum, shrink_bias_sum, attn_gain_sum, attn_shift_sum, ffn_gain_sum, ffn_shift_sum = (
        lax.psum(
            (
                expand_bias_grad,
                shrink_bias_grad,
                attention_gain_grad,
                attention_shift_grad,
                forward_gain_grad,
                forward_shift_grad,
            ),
            ("shard", "ctx"),
        )
    )
    query_sum, value_sum, expand_sum, output_sum, shrink_sum = over_context(
        query_grad, value_grad, expand_grad, output_grad, shrink_grad
    )
    query_own, value_own, expand_own = to_row_owners(query_sum, value_sum, expand_sum)
    output_own, shrink_own = to_col_owners(output_sum, shrink_sum)
    return (
        first_out,
        second_out,
        first_grad,
        second_grad,
        query_own,
        value_own,
        output_own,
        expand_own,
        expand_bias_sum,
        shrink_own,
        shrink_bias_sum,
        attn_gain_sum,
        attn_shift_sum,
        ffn_gain_sum,
        ffn_shift_sum,
    )


def branch_sum_low(partial_value):
    summed = lax.psum_scatter(
        partial_value.astype(jnp.bfloat16), "tp", scatter_dimension=2, tiled=True
    )
    return summed.astype(jnp.float32)


def sequence_labels(segment_ids, bucket_ids, positions, heads_here):
    seqs_here, rows_here = positions.shape
    packed = jnp.concatenate([positions[:, None], segment_ids[:, None], bucket_ids], 1)
    gathered = lax.all_gather(packed, "ctx", axis=2, tiled=True)
    mine = lax.dynamic_index_in_dim(gathered, lax.axis_index("ctx") // heads_here, 0, False)
    places = mine[0]
    return places, doc_bounds(mine[1]), into_places(places, bucket_hot(mine[2:]))


def to_heads(vectors):
    rows_here, seqs_here, width = vectors[0].shape
    heads = width // DH
    stacked = jnp.concatenate(
        [item.reshape(rows_here, seqs_here * heads, 1, DH) for item in vectors], 2
    )
    sent = stacked.transpose(1, 0, 2, 3).reshape(seqs_here * heads, rows_here, -1)
    landed = lax.all_to_all(sent, "ctx", split_axis=0, concat_axis=0, tiled=True)
    return landed.reshape(-1, landed.shape[2])


def from_heads(vectors, seqs_here, count):
    pairs = lax.axis_size("ctx")
    sent = vectors.reshape(pairs, vectors.shape[0] // pairs, vectors.shape[1])
    landed = lax.all_to_all(sent, "ctx", split_axis=0, concat_axis=0, tiled=True)
    shaped = landed.reshape(seqs_here, pairs // seqs_here, -1, count, DH).transpose(2, 0, 1, 3, 4)
    rows_here = shaped.shape[0]
    return tuple(shaped[:, :, :, at].reshape(rows_here, seqs_here, -1) for at in range(count))


def per_device(
    first_half,
    second_half,
    first_cotangent,
    second_cotangent,
    segment_ids,
    bucket_ids,
    positions,
    query_weight,
    value_weight,
    output_weight,
    expand_weight,
    expand_bias,
    shrink_weight,
    shrink_bias,
    attention_gain,
    attention_shift,
    forward_gain,
    forward_shift,
):
    rows_here, seqs_here, slice_width = first_half.shape
    width_heads = query_weight.shape[1]
    heads_here = width_heads // DH
    tp_start = lax.axis_index("tp") * slice_width
    ctx_start = lax.axis_index("ctx") * rows_here
    bf16 = jnp.bfloat16
    f32 = jnp.float32

    def columns(wide):
        return lax.dynamic_slice_in_dim(wide, tp_start, slice_width, wide.ndim - 1)

    full_query, full_value, full_expand = (
        lax.all_gather(query_weight, "shard", axis=0, tiled=True),
        lax.all_gather(value_weight, "shard", axis=0, tiled=True),
        lax.all_gather(expand_weight, "shard", axis=0, tiled=True),
    )
    full_output, full_shrink = (
        lax.all_gather(output_weight, "shard", axis=1, tiled=True),
        lax.all_gather(shrink_weight, "shard", axis=1, tiled=True),
    )
    places, bounds, hot = sequence_labels(segment_ids, bucket_ids, positions, heads_here)
    second_wide = full_rows(second_half)
    normed, attn_scaled, attn_inverse = norm_rows(
        second_wide.astype(f32), attention_gain, attention_shift
    )
    normed = normed.astype(bf16)
    queries = jnp.einsum("psd,de->pse", normed, full_query, preferred_element_type=f32).astype(bf16)
    value_vectors = jnp.einsum(
        "psd,de->pse", normed, full_value, preferred_element_type=f32
    ).astype(bf16)
    sorted_pair = into_places(places, to_heads((queries, value_vectors)))
    query_sorted, value_sorted = sorted_pair[:, :DH], sorted_pair[:, DH:]
    mix, logs = attend(bounds, query_sorted, value_sorted, hot)
    (attention,) = from_heads(out_of_places(places, mix.T.astype(bf16)), seqs_here, 1)
    branch = branch_sum_low(
        jnp.einsum("pse,ed->psd", attention, full_output, preferred_element_type=f32)
    )
    first_out = (first_half.astype(f32) + branch).astype(bf16)
    first_wide = full_rows(first_out)
    ffn_in, ffn_scaled, ffn_inverse = norm_rows(first_wide.astype(f32), forward_gain, forward_shift)
    ffn_in = ffn_in.astype(bf16)
    pre_act = (
        jnp.einsum("psd,df->psf", ffn_in, full_expand, preferred_element_type=f32) + expand_bias
    )
    hidden_exact, unit_pull = jax.vjp(smooth_unit, pre_act)
    hidden = hidden_exact.astype(bf16)
    second_branch = (
        branch_sum_low(jnp.einsum("psf,fd->psd", hidden, full_shrink, preferred_element_type=f32))
        + shrink_bias
    )
    second_out = (second_half.astype(f32) + second_branch).astype(bf16)
    cotangent_wide = full_rows(second_cotangent)
    hidden_grad = jnp.einsum("psd,fd->psf", cotangent_wide, full_shrink, preferred_element_type=f32)
    pre_grad = unit_pull(hidden_grad)[0].astype(bf16)
    shrink_grad = jnp.einsum("psf,psd->fd", hidden, cotangent_wide, preferred_element_type=f32)
    shrink_bias_grad = jnp.sum(second_cotangent.astype(f32), (0, 1))
    expand_grad = jnp.einsum("psd,psf->df", ffn_in, pre_grad, preferred_element_type=f32)
    expand_bias_grad = jnp.sum(pre_grad.astype(f32), (0, 1))
    ffn_grad = branch_sum_low(
        jnp.einsum("psf,df->psd", pre_grad, full_expand, preferred_element_type=f32)
    )
    ffn_back, forward_gain_grad, forward_shift_grad = norm_back(
        ffn_grad, columns(ffn_scaled), ffn_inverse, columns(forward_gain)
    )
    first_grad = (first_cotangent.astype(f32) + ffn_back).astype(bf16)
    grad_wide = full_rows(first_grad)
    output_grad = jnp.einsum("pse,psd->ed", attention, grad_wide, preferred_element_type=f32)
    attention_grad = jnp.einsum(
        "psd,ed->pse", grad_wide, full_output, preferred_element_type=f32
    ).astype(bf16)
    grad_sorted = into_places(places, to_heads((attention_grad,)))
    parts = attend_back(bounds, query_sorted, value_sorted, hot, grad_sorted, mix, logs)
    queries_total, values_grad = from_heads(
        out_of_places(places, jnp.concatenate(parts, 1)), seqs_here, 2
    )
    query_grad = jnp.einsum("psd,pse->de", normed, queries_total, preferred_element_type=f32)
    value_grad = jnp.einsum("psd,pse->de", normed, values_grad, preferred_element_type=f32)
    normed_grad = branch_sum_low(
        jnp.einsum("pse,de->psd", queries_total, full_query, preferred_element_type=f32)
        + jnp.einsum("pse,de->psd", values_grad, full_value, preferred_element_type=f32)
    )
    attn_back, attention_gain_grad, attention_shift_grad = norm_back(
        normed_grad, columns(attn_scaled), attn_inverse, columns(attention_gain)
    )
    second_grad = (second_cotangent.astype(f32) + attn_back).astype(bf16)
    expand_bias_sum, shrink_bias_sum, attn_gain_sum, attn_shift_sum, ffn_gain_sum, ffn_shift_sum = (
        lax.psum(
            (
                expand_bias_grad,
                shrink_bias_grad,
                attention_gain_grad,
                attention_shift_grad,
                forward_gain_grad,
                forward_shift_grad,
            ),
            ("shard", "ctx"),
        )
    )
    query_sum, value_sum, expand_sum, output_sum, shrink_sum = over_context(
        query_grad, value_grad, expand_grad, output_grad, shrink_grad
    )
    query_own, value_own, expand_own = to_row_owners(query_sum, value_sum, expand_sum)
    output_own, shrink_own = to_col_owners(output_sum, shrink_sum)
    return (
        first_out,
        second_out,
        first_grad,
        second_grad,
        query_own,
        value_own,
        output_own,
        expand_own,
        expand_bias_sum,
        shrink_own,
        shrink_bias_sum,
        attn_gain_sum,
        attn_shift_sum,
        ffn_gain_sum,
        ffn_shift_sum,
    )


def paired(mesh):
    heads_here = HEADS // mesh.shape["tp"]
    seqs_here = SEQS // mesh.shape["shard"]
    return mesh.shape["ctx"] == heads_here * seqs_here


def solution(mesh):
    return jax.shard_map(
        per_device if paired(mesh) else general_device,
        mesh=mesh,
        in_specs=(
            P("ctx", "shard", "tp"),
            P("ctx", "shard", "tp"),
            P("ctx", "shard", "tp"),
            P("ctx", "shard", "tp"),
            P("shard", "ctx"),
            P("shard", None, "ctx"),
            P("shard", "ctx"),
            P("shard", "tp"),
            P("shard", "tp"),
            P("tp", "shard"),
            P("shard", "tp"),
            P("tp"),
            P("tp", "shard"),
            P("tp"),
            P(),
            P(),
            P(),
            P(),
        ),
        out_specs=(
            P("ctx", "shard", "tp"),
            P("ctx", "shard", "tp"),
            P("ctx", "shard", "tp"),
            P("ctx", "shard", "tp"),
            P("shard", "tp"),
            P("shard", "tp"),
            P("tp", "shard"),
            P("shard", "tp"),
            P("tp"),
            P("tp", "shard"),
            P("tp"),
            P("tp"),
            P("tp"),
            P("tp"),
            P("tp"),
        ),
        check_vma=False,
    )
```

```python
import jax
import jax.numpy as jnp
from jax import lax
from jax.experimental import pallas as pl
from jax.experimental.pallas import tpu as pltpu
from jax.sharding import PartitionSpec as P

D = 1024
DH = 128
ROUNDS = 4


SELF_SCORE = -10.0
NEG_FILL = -1e30
BLOCK_ROWS = 512


BUCKETS = 64
HEADS = 8
SEQS = 4
TILE = 256
NT = (((1,), (1,)), ((), ()))
NN = (((1,), (0,)), ((), ()))


def dot(left, right, dims):
    return lax.dot_general(left, right, dims, preferred_element_type=jnp.float32)


def start_of(place, bounds_ref):
    start = jnp.where(place >= bounds_ref[0], bounds_ref[0], 0)
    start = jnp.where(place >= bounds_ref[1], bounds_ref[1], start)
    return jnp.where(place >= bounds_ref[2], bounds_ref[2], start)


def tile_masks(begin_row, bounds_ref):
    query_lane = lax.broadcasted_iota(jnp.int32, (1, TILE), 1)
    doc_start = start_of(query_lane + begin_row, bounds_ref)
    first = start_of(begin_row, bounds_ref) // TILE
    last_start = start_of(begin_row + TILE - 1, bounds_ref)
    full = jnp.minimum((last_start + TILE - 1) // TILE, begin_row // TILE)
    return doc_start, first, full


def rows_at(ref, block):
    return ref[pl.ds(pl.multiple_of(block * TILE, TILE), TILE), :]


def norm_factor(q):
    return lax.rsqrt(jnp.mean(q * q, -1, keepdims=True) + 1e-06)


def attend_kernel(bounds_ref, q_ref, v_ref, hot_ref, out_ref, log_ref, key_sc, vt_sc):
    block = pl.program_id(0)
    blocks = pl.num_programs(0)

    @pl.when(block == 0)
    def _():
        def prep(at, carry):
            q = rows_at(q_ref, at).astype(jnp.float32)
            begin = pl.multiple_of(at * TILE, TILE)
            key_sc[pl.ds(begin, TILE), :] = (q * (norm_factor(q) * DH ** (-0.5))).astype(jnp.bfloat16)
            v = rows_at(v_ref, at).astype(jnp.float32)
            vt_sc[:, pl.ds(begin, TILE)] = v.T.astype(jnp.bfloat16)
            return carry

        lax.fori_loop(0, blocks, prep, 0)

    begin_row = block * TILE
    doc_start, first, full = tile_masks(begin_row, bounds_ref)
    q = rows_at(q_ref, block)
    hot = rows_at(hot_ref, block)
    key_row = lax.broadcasted_iota(jnp.int32, (TILE, 1), 0)
    lane = lax.broadcasted_iota(jnp.int32, (1, TILE), 1)

    def scores(at):
        return dot(rows_at(key_sc, at), q, NT), dot(rows_at(hot_ref, at), hot, NT)

    def vt(at):
        return vt_sc[:, pl.ds(pl.multiple_of(at * TILE, TILE), TILE)]

    s, c = scores(block)
    place = key_row + begin_row
    c = jnp.where((key_row < lane) & (place >= doc_start), c, 0.0)
    itself = key_row == lane
    c = jnp.where(itself, float(ROUNDS), c)
    s = jnp.where(itself, SELF_SCORE, s)
    s = jnp.where(c > 0, s, NEG_FILL)
    high = jnp.max(s, 0, keepdims=True)
    p = c * jnp.exp(s - high)
    total = jnp.sum(p, 0, keepdims=True)
    acc = dot(vt(block), p.astype(jnp.bfloat16), NN)

    def fold(at, carry, masked):
        high, total, acc = carry
        s, c = scores(at)
        if masked:
            c = jnp.where(key_row + at * TILE >= doc_start, c, 0.0)
        s = jnp.where(c > 0, s, NEG_FILL)
        new_high = jnp.maximum(high, jnp.max(s, 0, keepdims=True))
        fade = jnp.exp(high - new_high)
        p = c * jnp.exp(s - new_high)
        total = total * fade + jnp.sum(p, 0, keepdims=True)
        acc = acc * fade + dot(vt(at), p.astype(jnp.bfloat16), NN)
        return new_high, total, acc

    carry = lax.fori_loop(first, full, lambda at, x: fold(at, x, True), (high, total, acc))
    high, total, acc = lax.fori_loop(full, block, lambda at, x: fold(at, x, False), carry)
    out_ref[...] = acc / total
    log_ref[pl.ds(block, 1), :] = high + jnp.log(total)


def attend(bounds, q, v, hot):
    rows = q.shape[0]
    blocks = rows // TILE
    whole = lambda shape: pl.BlockSpec(shape, lambda i, *_: (0,) * len(shape))
    return pl.pallas_call(
        attend_kernel,
        name="attend",
        out_shape=(
            jax.ShapeDtypeStruct((DH, rows), jnp.float32),
            jax.ShapeDtypeStruct((blocks, TILE), jnp.float32),
        ),
        grid_spec=pltpu.PrefetchScalarGridSpec(
            num_scalar_prefetch=1,
            grid=(blocks,),
            in_specs=[whole((rows, DH)), whole((rows, DH)), whole((rows, ROUNDS * BUCKETS))],
            out_specs=[pl.BlockSpec((DH, TILE), lambda i, *_: (0, i)), whole((blocks, TILE))],
            scratch_shapes=[pltpu.VMEM((rows, DH), jnp.bfloat16), pltpu.VMEM((DH, rows), jnp.bfloat16)],
        ),
        compiler_params=pltpu.CompilerParams(
            dimension_semantics=("arbitrary",), vmem_limit_bytes=40 * 2**20
        ),
        cost_estimate=pl.CostEstimate(
            flops=rows * rows * 256, bytes_accessed=rows * DH * 20, transcendentals=rows * rows // 4
        ),
    )(bounds, q, v, hot)


def attend_back_kernel(
    bounds_ref, q_ref, v_ref, hot_ref, grad_ref, out_ref, log_ref,
    q_grad_ref, v_grad_ref, key_sc, kt_sc, dk_sc, dv_sc, dq_sc,
):
    block = pl.program_id(0)
    blocks = pl.num_programs(0)

    @pl.when(block == 0)
    def _():
        def prep(at, carry):
            begin = pl.multiple_of(at * TILE, TILE)
            q = rows_at(q_ref, at).astype(jnp.float32)
            k = q * (norm_factor(q) * DH ** (-0.5))
            key_sc[pl.ds(begin, TILE), :] = k.astype(jnp.bfloat16)
            kt_sc[:, pl.ds(begin, TILE)] = k.T.astype(jnp.bfloat16)
            dk_sc[pl.ds(begin, TILE), :] = jnp.zeros((TILE, DH), jnp.float32)
            dv_sc[pl.ds(begin, TILE), :] = jnp.zeros((TILE, DH), jnp.float32)
            return carry

        lax.fori_loop(0, blocks, prep, 0)

    begin_row = block * TILE
    doc_start, first, full = tile_masks(begin_row, bounds_ref)
    q = rows_at(q_ref, block)
    hot = rows_at(hot_ref, block)
    grad = rows_at(grad_ref, block)
    log_row = log_ref[pl.ds(block, 1), :]
    delta = jnp.sum(grad.astype(jnp.float32).T * out_ref[...], 0, keepdims=True)
    key_row = lax.broadcasted_iota(jnp.int32, (TILE, 1), 0)
    lane = lax.broadcasted_iota(jnp.int32, (1, TILE), 1)

    def fold(at, acc, masked, diagonal=False):
        begin = pl.multiple_of(at * TILE, TILE)
        s = dot(rows_at(key_sc, at), q, NT)
        c = dot(rows_at(hot_ref, at), hot, NT)
        up = dot(rows_at(v_ref, at), grad, NT)
        if diagonal:
            itself = key_row == lane
            c = jnp.where((key_row < lane) & (key_row + begin_row >= doc_start), c, 0.0)
            c = jnp.where(itself, float(ROUNDS), c)
            s = jnp.where(itself, SELF_SCORE, s)
        elif masked:
            c = jnp.where(key_row + begin >= doc_start, c, 0.0)
        s = jnp.where(c > 0, s, NEG_FILL)
        w = c * jnp.exp(s - log_row)
        ds = w * (up - delta)
        if diagonal:
            ds = jnp.where(itself, 0.0, ds)
        w = w.astype(jnp.bfloat16)
        ds = ds.astype(jnp.bfloat16)
        dv_sc[pl.ds(begin, TILE), :] += dot(w, grad, NN)
        dk_sc[pl.ds(begin, TILE), :] += dot(ds, q, NN)
        return acc + dot(kt_sc[:, pl.ds(begin, TILE)], ds, NN)

    acc = fold(block, jnp.zeros((DH, TILE), jnp.float32), True, True)
    acc = lax.fori_loop(first, full, lambda at, x: fold(at, x, True), acc)
    acc = lax.fori_loop(full, block, lambda at, x: fold(at, x, False), acc)
    dq_sc[pl.ds(pl.multiple_of(begin_row, TILE), TILE), :] = acc.T

    @pl.when(block == blocks - 1)
    def _():
        def finish(at, carry):
            begin = pl.multiple_of(at * TILE, TILE)
            q = rows_at(q_ref, at).astype(jnp.float32)
            r = norm_factor(q)
            g = rows_at(dk_sc, at).astype(jnp.bfloat16).astype(jnp.float32)
            back = (r * DH ** (-0.5)) * (g - q * (r * r * jnp.mean(q * g, -1, keepdims=True)))
            q_grad_ref[pl.ds(begin, TILE), :] = (rows_at(dq_sc, at) + back).astype(jnp.bfloat16)
            v_grad_ref[pl.ds(begin, TILE), :] = rows_at(dv_sc, at).astype(jnp.bfloat16)
            return carry

        lax.fori_loop(0, blocks, finish, 0)


def attend_back(bounds, q, v, hot, grad, out, logs):
    rows = q.shape[0]
    blocks = rows // TILE
    whole = lambda shape: pl.BlockSpec(shape, lambda i, *_: (0,) * len(shape))
    return pl.pallas_call(
        attend_back_kernel,
        name="attend_back",
        out_shape=(jax.ShapeDtypeStruct((rows, DH), jnp.bfloat16),) * 2,
        grid_spec=pltpu.PrefetchScalarGridSpec(
            num_scalar_prefetch=1,
            grid=(blocks,),
            in_specs=[
                whole((rows, DH)), whole((rows, DH)), whole((rows, ROUNDS * BUCKETS)), whole((rows, DH)),
                pl.BlockSpec((DH, TILE), lambda i, *_: (0, i)), whole((blocks, TILE)),
            ],
            out_specs=[whole((rows, DH))] * 2,
            scratch_shapes=[
                pltpu.VMEM((rows, DH), jnp.bfloat16),
                pltpu.VMEM((DH, rows), jnp.bfloat16),
                pltpu.VMEM((rows, DH), jnp.float32),
                pltpu.VMEM((rows, DH), jnp.float32),
                pltpu.VMEM((rows, DH), jnp.float32),
            ],
        ),
        compiler_params=pltpu.CompilerParams(
            dimension_semantics=("arbitrary",), vmem_limit_bytes=48 * 2**20
        ),
        cost_estimate=pl.CostEstimate(
            flops=rows * rows * 640, bytes_accessed=rows * DH * 30, transcendentals=rows * rows // 4
        ),
    )(bounds, q, v, hot, grad, out, logs)


def place_matrix(places):
    rows = places.shape[0]
    return (jnp.arange(rows, dtype=jnp.int32)[:, None] == places[None, :]).astype(jnp.bfloat16)


def into_places(places, vectors):
    return jnp.einsum("pa,ad->pd", place_matrix(places), vectors, preferred_element_type=jnp.float32).astype(jnp.bfloat16)


def out_of_places(places, vectors):
    return jnp.einsum("pa,pd->ad", place_matrix(places), vectors, preferred_element_type=jnp.float32).astype(jnp.bfloat16)


def bucket_hot(buckets):
    hot = buckets.T[:, :, None] == jnp.arange(BUCKETS, dtype=jnp.int32)
    return hot.astype(jnp.bfloat16).reshape(buckets.shape[1], ROUNDS * BUCKETS)


def doc_bounds(segments):
    return jnp.sum((segments[None, :] < jnp.arange(1, 4, dtype=jnp.int32)[:, None]).astype(jnp.int32), 1)


def smooth_unit(values_in):
    return jax.nn.gelu(values_in, approximate=False)


def norm_rows(rows_wide, gain_row, shift_row):
    centre = jnp.mean(rows_wide, -1, keepdims=True)
    offset = rows_wide - centre
    inverse = lax.rsqrt(jnp.mean(offset * offset, -1, keepdims=True) + 1e-05)
    scaled = offset * inverse
    return (scaled * gain_row + shift_row, scaled, inverse)


def unit_keys(queries):
    shaped = queries.reshape(queries.shape[:-1] + (queries.shape[-1] // DH, DH))
    factor = lax.rsqrt(jnp.mean(shaped * shaped, -1, keepdims=True) + 1e-06) * DH ** (-0.5)
    return (shaped * factor).reshape(queries.shape)


def heads_view(vectors):
    return vectors.reshape(vectors.shape[0], vectors.shape[1], vectors.shape[2] // DH, DH)


def full_rows(sliced):
    return lax.all_gather(sliced, "tp", axis=2, tiled=True)


def branch_sum(partial_value):
    return lax.psum_scatter(partial_value, "tp", scatter_dimension=2, tiled=True)


def norm_back(grad_slice, scaled_slice, inverse, gain_slice):
    weighted = grad_slice * gain_slice
    first_sum, second_sum = lax.psum(
        (jnp.sum(weighted, -1, keepdims=True), jnp.sum(weighted * scaled_slice, -1, keepdims=True)),
        "tp",
    )
    inner = inverse * (weighted - first_sum / D - scaled_slice * (second_sum / D))
    return (inner, jnp.sum(grad_slice * scaled_slice, (0, 1)), jnp.sum(grad_slice, (0, 1)))


def label_rows(all_labels, begin_row, extent):
    all_segments, all_buckets, all_positions = all_labels
    return (
        lax.dynamic_slice_in_dim(all_segments, begin_row, extent, 1),
        lax.dynamic_slice_in_dim(all_buckets, begin_row, extent, 2),
        lax.dynamic_slice_in_dim(all_positions, begin_row, extent, 1),
    )


def block_weights(query_heads, query_labels, key_heads, key_labels):
    query_seg, query_buck, query_pos = query_labels
    key_seg, key_buck, key_pos = key_labels
    scores = jnp.einsum(
        "pshd,kshd->shpk", query_heads, key_heads, preferred_element_type=jnp.float32
    )
    matches = jnp.sum((query_buck[:, :, :, None] == key_buck[:, :, None, :]).astype(jnp.int32), 1)
    same_doc = query_seg[:, :, None] == key_seg[:, None, :]
    earlier = key_pos[:, None, :] < query_pos[:, :, None]
    itself = key_pos[:, None, :] == query_pos[:, :, None]
    counts = jnp.where(itself, ROUNDS, jnp.where(earlier & same_doc, matches, 0)).astype(
        jnp.float32
    )[:, None]
    shifted = jnp.where(itself[:, None], SELF_SCORE, scores)
    return (shifted, counts, itself[:, None])


def weights_of(shifted, counts, log_total):
    return jnp.where(counts > 0, counts * jnp.exp(shifted - log_total[..., None]), 0.0)


def blockwise(advance, running, row_count):
    extent = BLOCK_ROWS

    def turn(state_now, block_index):
        return (advance(state_now, block_index * extent, extent), None)

    return lax.scan(turn, running, jnp.arange(row_count // extent, dtype=jnp.int32))[0]


def over_keys(key_vectors, value_vectors, folder, initial):
    return folder(
        initial,
        (
            lax.all_gather(key_vectors, "ctx", axis=0, tiled=True),
            lax.all_gather(value_vectors, "ctx", axis=0, tiled=True),
        ),
        jnp.int32(0),
    )


def over_context(first_part, second_part, third_part, fourth_part, fifth_part):
    return (
        lax.psum(first_part.astype(jnp.bfloat16), "ctx").astype(jnp.float32),
        lax.psum(second_part.astype(jnp.bfloat16), "ctx").astype(jnp.float32),
        lax.psum(third_part.astype(jnp.bfloat16), "ctx").astype(jnp.float32),
        lax.psum(fourth_part.astype(jnp.bfloat16), "ctx").astype(jnp.float32),
        lax.psum(fifth_part.astype(jnp.bfloat16), "ctx").astype(jnp.float32),
    )


def to_row_owners(first_part, second_part, third_part):
    return (
        lax.psum_scatter(
            first_part.astype(jnp.bfloat16), "shard", scatter_dimension=0, tiled=True
        ).astype(jnp.float32),
        lax.psum_scatter(
            second_part.astype(jnp.bfloat16), "shard", scatter_dimension=0, tiled=True
        ).astype(jnp.float32),
        lax.psum_scatter(
            third_part.astype(jnp.bfloat16), "shard", scatter_dimension=0, tiled=True
        ).astype(jnp.float32),
    )


def to_col_owners(first_part, second_part):
    return (
        lax.psum_scatter(
            first_part.astype(jnp.bfloat16), "shard", scatter_dimension=1, tiled=True
        ).astype(jnp.float32),
        lax.psum_scatter(
            second_part.astype(jnp.bfloat16), "shard", scatter_dimension=1, tiled=True
        ).astype(jnp.float32),
    )


def general_device(
    first_half,
    second_half,
    first_cotangent,
    second_cotangent,
    segment_ids,
    bucket_ids,
    positions,
    query_weight,
    value_weight,
    output_weight,
    expand_weight,
    expand_bias,
    shrink_weight,
    shrink_bias,
    attention_gain,
    attention_shift,
    forward_gain,
    forward_shift,
):
    rows_here, seqs_here, slice_width = first_half.shape
    width_heads = query_weight.shape[1]
    heads_here = width_heads // DH
    tp_start = lax.axis_index("tp") * slice_width
    ctx_start = lax.axis_index("ctx") * rows_here
    bf16 = jnp.bfloat16
    f32 = jnp.float32

    def columns(wide):
        return lax.dynamic_slice_in_dim(wide, tp_start, slice_width, wide.ndim - 1)

    full_query, full_value, full_expand = (
        lax.all_gather(query_weight, "shard", axis=0, tiled=True),
        lax.all_gather(value_weight, "shard", axis=0, tiled=True),
        lax.all_gather(expand_weight, "shard", axis=0, tiled=True),
    )
    full_output, full_shrink = (
        lax.all_gather(output_weight, "shard", axis=1, tiled=True),
        lax.all_gather(shrink_weight, "shard", axis=1, tiled=True),
    )
    all_labels = (
        lax.all_gather(segment_ids, "ctx", axis=1, tiled=True),
        lax.all_gather(bucket_ids, "ctx", axis=2, tiled=True),
        lax.all_gather(positions, "ctx", axis=1, tiled=True),
    )
    local_labels = label_rows(all_labels, ctx_start, rows_here)
    second_wide = full_rows(second_half)
    normed, attn_scaled, attn_inverse = norm_rows(
        second_wide.astype(f32), attention_gain, attention_shift
    )
    normed = normed.astype(bf16)
    queries = jnp.einsum("psd,de->pse", normed, full_query, preferred_element_type=f32).astype(bf16)
    key_vectors = unit_keys(queries.astype(f32)).astype(bf16)
    value_vectors = jnp.einsum(
        "psd,de->pse", normed, full_value, preferred_element_type=f32
    ).astype(bf16)
    query_heads = heads_view(queries)
    stat_shape = (seqs_here, heads_here, rows_here)
    head_zero = jnp.zeros((rows_here, seqs_here, heads_here, DH), f32)

    def norm_fold(running, pieces, begin_row):
        key_piece = pieces[0]

        def advance(state_now, offset, extent):
            highest, summed = state_now
            key_heads = heads_view(lax.dynamic_slice_in_dim(key_piece, offset, extent, 0))
            shifted, counts, _ = block_weights(
                query_heads, local_labels, key_heads, label_rows(all_labels, offset, extent)
            )
            usable = counts > 0
            new_high = jnp.maximum(highest, jnp.max(jnp.where(usable, shifted, NEG_FILL), -1))
            summed = summed * jnp.exp(highest - new_high) + jnp.sum(
                jnp.where(usable, counts * jnp.exp(shifted - new_high[..., None]), 0.0), -1
            )
            return (new_high, summed)

        return blockwise(advance, running, key_piece.shape[0])

    highest, summed = over_keys(
        key_vectors,
        value_vectors,
        norm_fold,
        (jnp.full(stat_shape, NEG_FILL, f32), jnp.zeros(stat_shape, f32)),
    )
    log_total = highest + jnp.log(summed)

    def key_block(pieces, offset, extent):
        key_heads = heads_view(lax.dynamic_slice_in_dim(pieces[0], offset, extent, 0))
        value_heads = heads_view(lax.dynamic_slice_in_dim(pieces[1], offset, extent, 0))
        shifted, counts, itself = block_weights(
            query_heads, local_labels, key_heads, label_rows(all_labels, offset, extent)
        )
        return (key_heads, value_heads, weights_of(shifted, counts, log_total), itself)

    def mix_fold(running, pieces, begin_row):

        def advance(state_now, offset, extent):
            key_heads, value_heads, weights, itself = key_block(pieces, offset, extent)
            return state_now + jnp.einsum(
                "shpk,kshd->pshd", weights.astype(bf16), value_heads, preferred_element_type=f32
            )

        return blockwise(advance, running, pieces[0].shape[0])

    head_mix = over_keys(key_vectors, value_vectors, mix_fold, head_zero)
    attention = head_mix.reshape(rows_here, seqs_here, width_heads).astype(bf16)
    branch = branch_sum(
        jnp.einsum("pse,ed->psd", attention, full_output, preferred_element_type=f32)
    )
    first_out = (first_half.astype(f32) + branch).astype(bf16)
    first_wide = full_rows(first_out)
    ffn_in, ffn_scaled, ffn_inverse = norm_rows(first_wide.astype(f32), forward_gain, forward_shift)
    ffn_in = ffn_in.astype(bf16)
    pre_act = (
        jnp.einsum("psd,df->psf", ffn_in, full_expand, preferred_element_type=f32) + expand_bias
    )
    hidden_exact, unit_pull = jax.vjp(smooth_unit, pre_act)
    hidden = hidden_exact.astype(bf16)
    second_branch = (
        branch_sum(jnp.einsum("psf,fd->psd", hidden, full_shrink, preferred_element_type=f32))
        + shrink_bias
    )
    second_out = (second_half.astype(f32) + second_branch).astype(bf16)
    cotangent_wide = full_rows(second_cotangent)
    hidden_grad = jnp.einsum("psd,fd->psf", cotangent_wide, full_shrink, preferred_element_type=f32)
    pre_grad = unit_pull(hidden_grad)[0].astype(bf16)
    shrink_grad = jnp.einsum("psf,psd->fd", hidden, cotangent_wide, preferred_element_type=f32)
    shrink_bias_grad = jnp.sum(second_cotangent.astype(f32), (0, 1))
    expand_grad = jnp.einsum("psd,psf->df", ffn_in, pre_grad, preferred_element_type=f32)
    expand_bias_grad = jnp.sum(pre_grad.astype(f32), (0, 1))
    ffn_grad = branch_sum(
        jnp.einsum("psf,df->psd", pre_grad, full_expand, preferred_element_type=f32)
    )
    ffn_back, forward_gain_grad, forward_shift_grad = norm_back(
        ffn_grad, columns(ffn_scaled), ffn_inverse, columns(forward_gain)
    )
    first_grad = (first_cotangent.astype(f32) + ffn_back).astype(bf16)
    grad_wide = full_rows(first_grad)
    output_grad = jnp.einsum("pse,psd->ed", attention, grad_wide, preferred_element_type=f32)
    attention_grad = jnp.einsum(
        "psd,ed->pse", grad_wide, full_output, preferred_element_type=f32
    ).astype(bf16)
    grad_heads = heads_view(attention_grad)

    def delta_fold(running, pieces, begin_row):

        def advance(state_now, offset, extent):
            key_heads, value_heads, weights, itself = key_block(pieces, offset, extent)
            upstream = jnp.einsum(
                "pshd,kshd->shpk", grad_heads, value_heads, preferred_element_type=f32
            )
            return state_now + jnp.sum(weights * upstream, -1)

        return blockwise(advance, running, pieces[0].shape[0])

    row_delta = over_keys(key_vectors, value_vectors, delta_fold, jnp.zeros(stat_shape, f32))

    def query_fold(running, pieces, begin_row):

        def advance(state_now, offset, extent):
            key_heads, value_heads, weights, itself = key_block(pieces, offset, extent)
            upstream = jnp.einsum(
                "pshd,kshd->shpk", grad_heads, value_heads, preferred_element_type=f32
            )
            score_grad = jnp.where(itself, 0.0, weights * (upstream - row_delta[..., None])).astype(
                bf16
            )
            return state_now + jnp.einsum(
                "shpk,kshd->pshd", score_grad, key_heads, preferred_element_type=f32
            )

        return blockwise(advance, running, pieces[0].shape[0])

    query_part = over_keys(key_vectors, value_vectors, query_fold, head_zero)
    query_lse, query_delta = (
        lax.all_gather(log_total, "ctx", axis=2, tiled=True),
        lax.all_gather(row_delta, "ctx", axis=2, tiled=True),
    )
    local_keys = heads_view(key_vectors)
    local_values = heads_view(value_vectors)
    query_piece = lax.all_gather(queries, "ctx", axis=0, tiled=True)
    grad_piece = lax.all_gather(attention_grad, "ctx", axis=0, tiled=True)

    def advance(state_now, offset, extent):
        remote_queries = heads_view(lax.dynamic_slice_in_dim(query_piece, offset, extent, 0))
        remote_grads = heads_view(lax.dynamic_slice_in_dim(grad_piece, offset, extent, 0))
        lse_rows = lax.dynamic_slice_in_dim(query_lse, offset, extent, 2)
        delta_rows = lax.dynamic_slice_in_dim(query_delta, offset, extent, 2)
        shifted, counts, itself = block_weights(
            remote_queries, label_rows(all_labels, offset, extent), local_keys, local_labels
        )
        weights = weights_of(shifted, counts, lse_rows)
        upstream = jnp.einsum(
            "pshd,kshd->shpk", remote_grads, local_values, preferred_element_type=f32
        )
        score_grad = jnp.where(itself, 0.0, weights * (upstream - delta_rows[..., None])).astype(
            bf16
        )
        key_now = state_now[0] + jnp.einsum(
            "shpk,pshd->kshd", score_grad, remote_queries, preferred_element_type=f32
        )
        value_now = state_now[1] + jnp.einsum(
            "shpk,pshd->kshd", weights.astype(bf16), remote_grads, preferred_element_type=f32
        )
        return (key_now, value_now)

    key_part, value_part = blockwise(advance, (head_zero, head_zero), query_piece.shape[0])
    keys_grad = key_part.reshape(rows_here, seqs_here, width_heads).astype(bf16)
    values_grad = value_part.reshape(rows_here, seqs_here, width_heads).astype(bf16)
    unit_back = jax.vjp(unit_keys, queries.astype(f32))[1]
    queries_total = (
        query_part.reshape(rows_here, seqs_here, width_heads) + unit_back(keys_grad.astype(f32))[0]
    ).astype(bf16)
    query_grad = jnp.einsum("psd,pse->de", normed, queries_total, preferred_element_type=f32)
    value_grad = jnp.einsum("psd,pse->de", normed, values_grad, preferred_element_type=f32)
    normed_grad = branch_sum(
        jnp.einsum("pse,de->psd", queries_total, full_query, preferred_element_type=f32)
        + jnp.einsum("pse,de->psd", values_grad, full_value, preferred_element_type=f32)
    )
    attn_back, attention_gain_grad, attention_shift_grad = norm_back(
        normed_grad, columns(attn_scaled), attn_inverse, columns(attention_gain)
    )
    second_grad = (second_cotangent.astype(f32) + attn_back).astype(bf16)
    expand_bias_sum, shrink_bias_sum, attn_gain_sum, attn_shift_sum, ffn_gain_sum, ffn_shift_sum = (
        lax.psum(
            (
                expand_bias_grad,
                shrink_bias_grad,
                attention_gain_grad,
                attention_shift_grad,
                forward_gain_grad,
                forward_shift_grad,
            ),
            ("shard", "ctx"),
        )
    )
    query_sum, value_sum, expand_sum, output_sum, shrink_sum = over_context(
        query_grad, value_grad, expand_grad, output_grad, shrink_grad
    )
    query_own, value_own, expand_own = to_row_owners(query_sum, value_sum, expand_sum)
    output_own, shrink_own = to_col_owners(output_sum, shrink_sum)
    return (
        first_out,
        second_out,
        first_grad,
        second_grad,
        query_own,
        value_own,
        output_own,
        expand_own,
        expand_bias_sum,
        shrink_own,
        shrink_bias_sum,
        attn_gain_sum,
        attn_shift_sum,
        ffn_gain_sum,
        ffn_shift_sum,
    )


def swap(vectors, axis, bits):
    size = lax.axis_size(axis)
    return lax.ppermute(vectors, axis, [(at, at ^ bits) for at in range(size)])


def where_am_i():
    return lax.axis_index("shard"), lax.axis_index("ctx"), lax.axis_index("tp")


def plane_pairs(step, inverse):
    shards, planes = lax.axis_size("shard"), lax.axis_size("tp")
    local_seqs = planes // shards
    pairs = []
    for shard in range(shards):
        for plane in range(planes):
            chunk = step ^ plane
            there = (chunk % shards) * planes + shard * local_seqs + chunk // shards
            here = shard * planes + plane
            pairs.append((there, here) if inverse else (here, there))
    return pairs


def rows_in(sliced, beside=(), extra=None):
    shard, _, plane = where_am_i()
    shards, planes = lax.axis_size("shard"), lax.axis_size("tp")
    count, slots, seqs, width = sliced.shape
    extent = slots // shards
    by_seq = sliced.transpose(2, 0, 1, 3).reshape(seqs, count, shards, extent, width)
    by_seq = by_seq.transpose(0, 2, 1, 3, 4).reshape(seqs * shards, count * extent, width)
    if extra is not None:
        by_seq = jnp.concatenate([by_seq, jnp.concatenate([extra] * seqs, 0)], 1)
    mine = (plane % seqs) * shards + shard
    landed = []
    for step in range(planes):
        chunk = lax.dynamic_index_in_dim(by_seq, step ^ plane, 0, False)
        landed.append(lax.ppermute(chunk, ("shard", "tp"), plane_pairs(step, False)))
    landed, beside = lax.optimization_barrier((landed, beside))
    whole = jnp.zeros((count * extent, planes * width), sliced.dtype)
    for step in range(planes):
        piece = landed[step][: count * extent]
        whole = lax.dynamic_update_slice_in_dim(whole, piece, (step ^ mine) * width, 1)
    whole = whole.reshape(count, extent, planes * width)
    if extra is None:
        return whole, beside
    extras = jnp.zeros((planes,) + extra.shape[1:], extra.dtype)
    for step in range(planes):
        piece = landed[step][None, count * extent :]
        extras = lax.dynamic_update_slice_in_dim(extras, piece, step ^ mine, 0)
    return whole, beside, extras


def rows_out(whole, seqs, beside=()):
    shard, _, plane = where_am_i()
    shards, planes = lax.axis_size("shard"), lax.axis_size("tp")
    count, extent, features = whole.shape
    width = features // planes
    mine = (plane % seqs) * shards + shard
    flat = whole.reshape(count * extent, features)
    landed = []
    for step in range(planes):
        piece = lax.dynamic_slice_in_dim(flat, (step ^ mine) * width, width, 1)
        landed.append(lax.ppermute(piece, ("shard", "tp"), plane_pairs(step, True)))
    landed, beside = lax.optimization_barrier((landed, beside))
    by_seq = jnp.zeros((seqs * shards, count * extent, width), whole.dtype)
    for step in range(planes):
        by_seq = lax.dynamic_update_slice_in_dim(by_seq, landed[step][None], step ^ plane, 0)
    parts = by_seq.reshape(seqs, shards, count, extent, width).transpose(2, 1, 3, 0, 4)
    return parts.reshape(count, shards * extent, seqs, width), beside


def quarter_of(local, at):
    extent = local.shape[0] // lax.axis_size("ctx")
    return lax.dynamic_slice_in_dim(local, at * extent, extent, 0)


def by_half(own, other):
    first = lax.axis_index("shard") == 0
    return jnp.stack([jnp.where(first, own, other), jnp.where(first, other, own)])


def core_parts(local):
    mine = quarter_of(local, lax.axis_index("ctx"))
    halves = by_half(mine, swap(mine, "shard", 1))
    extent, width = mine.shape
    shards = lax.axis_size("shard")
    parts = halves.reshape(2, shards, extent // shards, width).transpose(1, 0, 2, 3)
    return parts.reshape(shards, extent, width)


def gather_rows(wide):
    ctx = lax.axis_index("ctx")
    quarters, (extent, width) = lax.axis_size("ctx"), wide.shape
    half = jnp.zeros((quarters, extent, width), wide.dtype)
    for j in range(quarters):
        piece = wide if j == 0 else swap(wide, "ctx", j)
        half = lax.dynamic_update_slice_in_dim(half, piece[None], ctx ^ j, 0)
    both = by_half(half, swap(half, "shard", 1)).reshape(2, quarters, 2, extent // 2, width)
    return both.transpose(2, 1, 0, 3, 4).reshape(2 * quarters * extent, width)


def split_bias(values):
    high = values.astype(jnp.bfloat16)
    rest = values - high.astype(jnp.float32)
    middle = rest.astype(jnp.bfloat16)
    return jnp.stack([high, middle, (rest - middle.astype(jnp.float32)).astype(jnp.bfloat16)])


def shard_half(wide, at):
    extent = wide.shape[1] // 2
    return lax.dynamic_slice_in_dim(wide, at * extent, extent, 1)


def chip_sums(rows_wide, columns_wide):
    shard = lax.axis_index("shard")

    def product(at):
        return lax.dot_general(
            shard_half(rows_wide, at),
            columns_wide,
            (((0,), (0,)), ((), ())),
            preferred_element_type=jnp.float32,
        )

    theirs = swap(product(1 - shard).astype(jnp.bfloat16), "shard", 1)
    return product(shard) + theirs.astype(jnp.float32)


def sum_parts(parts):
    return jnp.sum(parts.astype(jnp.float32), 0)


def send_ctx(sums):
    quarters = lax.axis_size("ctx")
    parts = sums.reshape(quarters, sums.shape[0] // quarters, sums.shape[1])
    return lax.all_to_all(parts, "ctx", 0, 0, tiled=True)


def scatter_ctx(sums):
    return sum_parts(send_ctx(sums))


def scatter_tp(sums):
    planes = lax.axis_size("tp")
    parts = sums.reshape(sums.shape[0], planes, -1).transpose(1, 0, 2)
    return sum_parts(lax.all_to_all(parts, "tp", 0, 0, tiled=True))


def collect_ctx(quarter):
    ctx = lax.axis_index("ctx")
    quarters, extent = lax.axis_size("ctx"), quarter.shape[0]
    whole = jnp.zeros((quarters * extent, quarter.shape[1]), quarter.dtype)
    for j in range(quarters):
        piece = quarter if j == 0 else swap(quarter, "ctx", j)
        whole = lax.dynamic_update_slice_in_dim(whole, piece, (ctx ^ j) * extent, 0)
    return whole


def reduce_context_first(sums):
    bf16 = jnp.bfloat16
    quarter = scatter_ctx(sums.astype(bf16)).astype(bf16)
    return collect_ctx(scatter_tp(quarter).astype(bf16)).astype(jnp.float32)


def after(values, ready):
    return lax.optimization_barrier((values, ready))[0]


def row_norm_back(grad, scaled, inverse, gain):
    weighted = grad * gain
    first = jnp.mean(weighted, -1, keepdims=True)
    second = jnp.mean(weighted * scaled, -1, keepdims=True)
    inner = inverse * (weighted - first - scaled * second)
    return inner, jnp.sum(grad * scaled, 0), jnp.sum(grad, 0)


def heads_out(vectors):
    heads = HEADS
    sent = vectors.reshape(vectors.shape[0], heads, -1).transpose(1, 0, 2)
    landed = lax.all_to_all(sent, ("ctx", "shard"), split_axis=0, concat_axis=0, tiled=True)
    return landed.reshape(-1, landed.shape[2])


def heads_back(vectors):
    sent = vectors.reshape(HEADS, -1, vectors.shape[1])
    landed = lax.all_to_all(sent, ("ctx", "shard"), split_axis=0, concat_axis=0, tiled=True)
    return landed.transpose(1, 0, 2).reshape(landed.shape[1], -1)


def plane_labels(segment_ids, bucket_ids, positions):
    shard, _, plane = where_am_i()
    seqs = positions.shape[0]
    packed = jnp.concatenate([positions[:, None], segment_ids[:, None], bucket_ids], 1)
    mine = lax.dynamic_index_in_dim(packed, plane % seqs, 0, False)
    mine = jnp.where(shard == plane // seqs, mine, swap(mine, "shard", 1))
    mine = lax.all_gather(mine, "ctx", axis=1, tiled=True)
    places = mine[0]
    return places, doc_bounds(mine[1]), into_places(places, bucket_hot(mine[2:]))


def row_device(
    first_half,
    second_half,
    first_cotangent,
    second_cotangent,
    segment_ids,
    bucket_ids,
    positions,
    query_weight,
    value_weight,
    output_weight,
    expand_weight,
    expand_bias,
    shrink_weight,
    shrink_bias,
    attention_gain,
    attention_shift,
    forward_gain,
    forward_shift,
):
    bf16, f32 = jnp.bfloat16, jnp.float32
    planes = lax.axis_size("tp")
    _, ctx, plane = where_am_i()
    seqs_here, width = first_half.shape[1:]
    units = expand_bias.shape[0]
    split = query_weight.shape[0]

    local_pair = jnp.stack(
        [query_weight.reshape(split, -1, DH), value_weight.reshape(split, -1, DH)], 2
    ).reshape(split, -1)
    pair_parts = core_parts(local_pair)
    pair_rows = pair_parts.shape[1] * pair_parts.shape[2] // width
    biases = split_bias(jnp.concatenate([expand_bias, shrink_bias])).reshape(-1, width)
    bias_rows = biases.shape[0]
    biases = jnp.pad(biases, ((0, -bias_rows % 16), (0, 0)))
    extra = jnp.concatenate(
        [pair_parts.reshape(-1, pair_rows, width), jnp.stack([biases] * pair_parts.shape[0])], 1
    )
    (second_rows,), (places, bounds, hot), extras = rows_in(
        second_half[None], plane_labels(segment_ids, bucket_ids, positions), extra
    )
    pair_wide = extras[:, :pair_rows].reshape((planes,) + pair_parts.shape[1:]).transpose(1, 0, 2)
    pair_full = gather_rows(pair_wide.reshape(pair_parts.shape[1], -1))
    biases = extras[:, pair_rows : pair_rows + bias_rows].astype(f32).reshape(planes, 3, -1)
    biases = (biases[:, 0] + biases[:, 1]) + biases[:, 2]
    unit_bias = jnp.concatenate(
        [
            lax.dynamic_index_in_dim(biases, plane, 0, False)[:units],
            lax.dynamic_index_in_dim(biases, plane ^ 2, 0, False)[:units],
        ]
    )
    row_bias = biases[:, units:].reshape(-1)

    normed, attn_scaled, attn_inverse = norm_rows(
        second_rows.astype(f32), attention_gain, attention_shift
    )
    normed = normed.astype(bf16)
    pair = dot(normed, pair_full, NN).astype(bf16)
    local_up, local_down, local_out = after(
        (expand_weight, shrink_weight.T, output_weight.T), pair_full
    )
    up, down, out = (quarter_of(item, ctx) for item in (local_up, local_down, local_out))
    landed, far, outs_near = lax.optimization_barrier(
        (
            heads_out(pair),
            swap(jnp.concatenate([up, down], 1), "tp", 2),
            [out] + [swap(out, "tp", k) for k in range(1, planes)],
        )
    )
    outs_wide = jnp.zeros((planes,) + out.shape, bf16)
    for k in range(planes):
        outs_wide = lax.dynamic_update_slice_in_dim(outs_wide, outs_near[k][None], plane ^ k, 0)
    outs_wide = outs_wide.transpose(1, 0, 2).reshape(out.shape[0], -1)
    wide = jnp.concatenate([up, far[:, :units], down, far[:, units:], outs_wide], 1)
    whole = lax.all_gather(wide, ("shard", "ctx"), axis=0, tiled=True)
    up_full, down_full, output_full = (
        whole[:, : 2 * units],
        whole[:, 2 * units : 4 * units],
        whole[:, 4 * units :],
    )

    sorted_pair = into_places(places, landed)
    query_sorted, value_sorted = sorted_pair[:, :DH], sorted_pair[:, DH:]
    (first_rows, second_grad_rows), (mix, logs) = rows_in(
        after(jnp.stack([first_half, second_cotangent]), landed),
        attend(bounds, query_sorted, value_sorted, hot),
    )
    far_grad_rows, attention = lax.optimization_barrier(
        (
            swap(after(second_grad_rows, mix), "tp", 1),
            heads_back(out_of_places(places, mix.T.astype(bf16))),
        )
    )

    first_out = (first_rows.astype(f32) + dot(attention, output_full, NT)).astype(bf16)
    ffn_in, ffn_scaled, ffn_inverse = norm_rows(first_out.astype(f32), forward_gain, forward_shift)
    ffn_in = ffn_in.astype(bf16)

    def units_of(rows, grad_rows):
        exact, pull = jax.vjp(smooth_unit, dot(rows, up_full, NN) + unit_bias)
        pre_grad = pull(dot(grad_rows, down_full, NN))[0].astype(bf16)
        return exact.astype(bf16), pre_grad

    (first_grad_rows,), (far_in, (hidden, pre_grad)) = rows_in(
        after(first_cotangent, first_out)[None],
        (swap(ffn_in, "tp", 1), units_of(ffn_in, second_grad_rows)),
    )
    far_hidden, far_pre_grad = units_of(far_in, far_grad_rows)
    far_ffn_grad = dot(far_pre_grad, up_full, NT).astype(bf16)
    all_pre_grad = jnp.concatenate([pre_grad, far_pre_grad], 0)
    all_hidden = jnp.concatenate([hidden, far_hidden], 0)
    theirs, ffn_grad, expand_sums, shrink_sums = lax.optimization_barrier(
        (
            swap(far_ffn_grad, "tp", 1),
            dot(pre_grad, up_full, NT),
            chip_sums(jnp.concatenate([ffn_in, far_in], 0), all_pre_grad).astype(bf16),
            chip_sums(jnp.concatenate([second_grad_rows, far_grad_rows], 0), all_hidden).astype(bf16),
        )
    )
    ffn_back, ffn_gain_grad, ffn_shift_grad = row_norm_back(
        ffn_grad + theirs.astype(f32), ffn_scaled, ffn_inverse, forward_gain
    )
    first_grad = (first_grad_rows.astype(f32) + ffn_back).astype(bf16)
    attention_grad = dot(first_grad, output_full, NN).astype(bf16)
    shrink_bias_grad = jnp.sum(second_grad_rows.astype(f32), 0)
    expand_bias_grad = jnp.sum(all_pre_grad.astype(f32), 0)
    far_branch = swap(dot(far_hidden, down_full, NT).astype(bf16), "tp", 1)
    second_out = (
        second_rows.astype(f32) + dot(hidden, down_full, NT) + far_branch.astype(f32) + row_bias
    ).astype(bf16)

    outs = jnp.stack([first_out, second_out])
    early = jnp.concatenate(
        [expand_sums, shrink_sums, chip_sums(first_grad, attention).astype(bf16)], 1
    )
    grad_heads, outs, early = lax.optimization_barrier((heads_out(attention_grad), outs, early))
    early_mine = lax.psum_scatter(early, "ctx", scatter_dimension=0, tiled=True)
    outs_sliced, parts = rows_out(
        outs,
        seqs_here,
        attend_back(
            bounds, query_sorted, value_sorted, hot, into_places(places, grad_heads), mix, logs
        ),
    )
    pair_grad_heads = out_of_places(places, jnp.concatenate(parts, 1))
    far_sums = jnp.concatenate(
        [early_mine[:, units : 2 * units], early_mine[:, 3 * units : 4 * units]], 1
    )
    near_sums = jnp.concatenate([early_mine[:, :units], early_mine[:, 2 * units : 3 * units]], 1)
    first_grad_sliced, (pair_grad, far_sums) = rows_out(
        after(first_grad, pair_grad_heads)[None],
        seqs_here,
        (heads_back(pair_grad_heads), swap(far_sums, "tp", 2)),
    )
    early_own = (near_sums.astype(f32) + far_sums.astype(f32)).astype(bf16)
    early_own = lax.all_gather(early_own, "ctx", axis=0, tiled=True).astype(f32)
    expand_own, shrink_own = early_own[:, :units], early_own[:, units:].T

    pair_sums = chip_sums(normed, pair_grad).astype(bf16)
    normed_grad = dot(pair_grad, pair_full, NT)
    attn_back, attn_gain_grad, attn_shift_grad = row_norm_back(
        normed_grad, attn_scaled, attn_inverse, attention_gain
    )
    second_grad = (second_grad_rows.astype(f32) + attn_back).astype(bf16)

    row_grads = jnp.stack(
        [shrink_bias_grad, attn_gain_grad, attn_shift_grad, ffn_gain_grad, ffn_shift_grad]
    )
    spread = jnp.arange(planes, dtype=jnp.int32)[:, None]
    unit_grads = jnp.where(spread == plane, expand_bias_grad[None, :units], 0.0)
    unit_grads = jnp.where(spread == plane ^ 2, expand_bias_grad[None, units:], unit_grads)
    packed = jnp.concatenate(
        [unit_grads, row_grads.reshape(5, planes, width).transpose(1, 0, 2).reshape(planes, -1)], 1
    )
    quarters = lax.axis_size("ctx")
    packed = (packed + swap(packed, "shard", 1)).astype(bf16)
    packed = packed.reshape(planes, quarters, -1)
    vector_width = packed.shape[2]
    packed = jnp.pad(packed, ((0, 0), (0, 0), (0, 32 * width - vector_width)))
    packed = packed.reshape(planes, quarters, 16, 2 * width).transpose(1, 2, 0, 3)
    late = jnp.concatenate(
        [pair_sums.reshape(quarters, split // quarters, -1), packed.reshape(quarters, 16, -1)], 1
    )
    second_grad_sliced, late = rows_out(
        second_grad[None], seqs_here, sum_parts(lax.all_to_all(late, "ctx", 0, 0, tiled=True))
    )
    late = late.astype(bf16).reshape(-1, planes, 2 * width)
    late = jnp.concatenate(
        [late, jnp.pad(early_mine[:, 4 * units :].reshape(-1, planes, width), ((0, 16), (0, 0), (0, 0)))], 2
    )
    late_own = collect_ctx(scatter_tp(late.reshape(late.shape[0], -1)).astype(bf16)).astype(f32)
    late_own = late_own.reshape(quarters, -1, 3 * width)
    owned = late_own[:, split // quarters :, : 2 * width].reshape(quarters, -1)
    owned = owned[:, :vector_width].reshape(-1)
    late_own = late_own[:, : split // quarters].reshape(split, -1)
    pair_own = late_own[:, : 2 * width].reshape(split, -1, 2, DH)
    query_own = pair_own[:, :, 0].reshape(query_weight.shape)
    value_own = pair_own[:, :, 1].reshape(value_weight.shape)
    output_own = late_own[:, 2 * width :].T
    row_own = owned[units:].reshape(5, width)
    return (
        outs_sliced[0],
        outs_sliced[1],
        first_grad_sliced[0],
        second_grad_sliced[0],
        query_own,
        value_own,
        output_own,
        expand_own,
        owned[:units],
        shrink_own,
        row_own[0],
        row_own[1],
        row_own[2],
        row_own[3],
        row_own[4],
    )


def row_planes(mesh):
    sizes = mesh.shape
    return sizes["tp"] == SEQS and sizes["shard"] == 2 and sizes["ctx"] == 4 and HEADS == 8


def solution(mesh):
    return jax.shard_map(
        row_device if row_planes(mesh) else general_device,
        mesh=mesh,
        in_specs=(
            P("ctx", "shard", "tp"),
            P("ctx", "shard", "tp"),
            P("ctx", "shard", "tp"),
            P("ctx", "shard", "tp"),
            P("shard", "ctx"),
            P("shard", None, "ctx"),
            P("shard", "ctx"),
            P("shard", "tp"),
            P("shard", "tp"),
            P("tp", "shard"),
            P("shard", "tp"),
            P("tp"),
            P("tp", "shard"),
            P("tp"),
            P(),
            P(),
            P(),
            P(),
        ),
        out_specs=(
            P("ctx", "shard", "tp"),
            P("ctx", "shard", "tp"),
            P("ctx", "shard", "tp"),
            P("ctx", "shard", "tp"),
            P("shard", "tp"),
            P("shard", "tp"),
            P("tp", "shard"),
            P("shard", "tp"),
            P("tp"),
            P("tp", "shard"),
            P("tp"),
            P("tp"),
            P("tp"),
            P("tp"),
            P("tp"),
        ),
        check_vma=False,
    )
```

```python
import jax
import jax.numpy as jnp
from jax import lax
from jax.experimental import pallas as pl
from jax.experimental.layout import Layout, with_layout_constraint
from jax.experimental.pallas import tpu as pltpu
from jax.sharding import PartitionSpec as P

D = 1024
DH = 128
ROUNDS = 4


SELF_SCORE = -10.0
NEG_FILL = -1e30
BLOCK_ROWS = 512


BUCKETS = 64
HEADS = 8
SEQS = 4
TILE = 512
GROUP = 1
BOUND = 38.0
NT = (((1,), (1,)), ((), ()))
NN = (((1,), (0,)), ((), ()))


def dot(left, right, dims):
    return lax.dot_general(left, right, dims, preferred_element_type=jnp.float32)


def start_of(place, bounds_ref):
    start = jnp.where(place >= bounds_ref[0], bounds_ref[0], 0)
    start = jnp.where(place >= bounds_ref[1], bounds_ref[1], start)
    return jnp.where(place >= bounds_ref[2], bounds_ref[2], start)


def tile_masks(begin_row, bounds_ref):
    query_lane = lax.broadcasted_iota(jnp.int32, (1, TILE), 1)
    doc_start = start_of(query_lane + begin_row, bounds_ref)
    first = start_of(begin_row, bounds_ref) // TILE
    last_start = start_of(begin_row + TILE - 1, bounds_ref)
    full = jnp.minimum((last_start + TILE - 1) // TILE, begin_row // TILE)
    return doc_start, first, full


def rows_at(ref, block, tiles=1):
    return ref[pl.ds(pl.multiple_of(block * TILE, TILE), tiles * TILE), :]


def norm_factor(q):
    return lax.rsqrt(jnp.mean(q * q, -1, keepdims=True) + 1e-06)


def attend_kernel(bounds_ref, q_ref, v_ref, hot_ref, out_ref, log_ref, key_sc, vt_sc):
    block = pl.program_id(0)
    blocks = pl.num_programs(0)

    @pl.when(block == 0)
    def _():
        def prep(at, carry):
            q = rows_at(q_ref, at).astype(jnp.float32)
            begin = pl.multiple_of(at * TILE, TILE)
            key_sc[pl.ds(begin, TILE), :] = (q * (norm_factor(q) * DH ** (-0.5))).astype(jnp.bfloat16)
            v = rows_at(v_ref, at).astype(jnp.float32)
            vt_sc[:, pl.ds(begin, TILE)] = v.T.astype(jnp.bfloat16)
            return carry

        lax.fori_loop(0, blocks, prep, 0)

    begin_row = block * TILE
    doc_start, first, full = tile_masks(begin_row, bounds_ref)
    q = rows_at(q_ref, block)
    hot = rows_at(hot_ref, block)
    key_row = lax.broadcasted_iota(jnp.int32, (TILE, 1), 0)
    lane = lax.broadcasted_iota(jnp.int32, (1, TILE), 1)

    def scores(at, tiles):
        return dot(rows_at(key_sc, at, tiles), q, NT), dot(rows_at(hot_ref, at, tiles), hot, NT)

    def vt(at, tiles):
        return vt_sc[:, pl.ds(pl.multiple_of(at * TILE, TILE), tiles * TILE)]

    itself = key_row == lane

    def diagonal():
        s, c = scores(block, 1)
        c = jnp.where((key_row < lane) & (key_row + begin_row >= doc_start), c, 0.0)
        return jnp.where(itself, SELF_SCORE, s), jnp.where(itself, float(ROUNDS), c)

    def in_document(c, at):
        return jnp.where(key_row + at * TILE >= doc_start, c, 0.0)

    def mixed(at, tiles, p):
        return dot(vt(at, tiles), p.astype(jnp.bfloat16), NN)

    @pl.when(bounds_ref[3] == 1)
    def _():
        def fold(at, tiles, carry, masked):
            total, acc = carry
            s, c = scores(at, tiles)
            if masked:
                c = in_document(c, at)
            p = c * jnp.exp(s)
            return total + jnp.sum(p, 0, keepdims=True), acc + mixed(at, tiles, p)

        s, c = diagonal()
        p = c * jnp.exp(s)
        carry = jnp.sum(p, 0, keepdims=True), mixed(block, 1, p)
        carry = lax.fori_loop(first, full, lambda at, x: fold(at, 1, x, True), carry)
        rest = (block - full) % GROUP
        carry = lax.fori_loop(full, full + rest, lambda at, x: fold(at, 1, x, False), carry)
        total, acc = lax.fori_loop(
            0,
            (block - full) // GROUP,
            lambda at, x: fold(full + rest + GROUP * at, GROUP, x, False),
            carry,
        )
        out_ref[...] = acc / total
        log_ref[pl.ds(block, 1), :] = jnp.log(total)

    @pl.when(bounds_ref[3] == 0)
    def _():
        def fold(at, carry):
            high, total, acc = carry
            s, c = scores(at, 1)
            c = in_document(c, at)
            s = jnp.where(c > 0, s, NEG_FILL)
            new_high = jnp.maximum(high, jnp.max(s, 0, keepdims=True))
            fade = jnp.exp(high - new_high)
            p = c * jnp.exp(s - new_high)
            total = total * fade + jnp.sum(p, 0, keepdims=True)
            return new_high, total, acc * fade + mixed(at, 1, p)

        s, c = diagonal()
        s = jnp.where(c > 0, s, NEG_FILL)
        high = jnp.max(s, 0, keepdims=True)
        p = c * jnp.exp(s - high)
        carry = high, jnp.sum(p, 0, keepdims=True), mixed(block, 1, p)
        high, total, acc = lax.fori_loop(first, block, fold, carry)
        out_ref[...] = acc / total
        log_ref[pl.ds(block, 1), :] = high + jnp.log(total)


def attend(bounds, q, v, hot):
    rows = q.shape[0]
    blocks = rows // TILE
    whole = lambda shape: pl.BlockSpec(shape, lambda i, *_: (0,) * len(shape))
    return pl.pallas_call(
        attend_kernel,
        name="attend",
        out_shape=(
            jax.ShapeDtypeStruct((DH, rows), jnp.float32),
            jax.ShapeDtypeStruct((blocks, TILE), jnp.float32),
        ),
        grid_spec=pltpu.PrefetchScalarGridSpec(
            num_scalar_prefetch=1,
            grid=(blocks,),
            in_specs=[whole((rows, DH)), whole((rows, DH)), whole((rows, ROUNDS * BUCKETS))],
            out_specs=[pl.BlockSpec((DH, TILE), lambda i, *_: (0, i)), whole((blocks, TILE))],
            scratch_shapes=[pltpu.VMEM((rows, DH), jnp.bfloat16), pltpu.VMEM((DH, rows), jnp.bfloat16)],
        ),
        compiler_params=pltpu.CompilerParams(
            dimension_semantics=("arbitrary",), vmem_limit_bytes=40 * 2**20
        ),
        cost_estimate=pl.CostEstimate(
            flops=rows * DH, bytes_accessed=rows * DH, transcendentals=0
        ),
    )(bounds, q, v, hot)


def attend_back_kernel(
    bounds_ref, q_ref, v_ref, hot_ref, grad_ref, out_ref, log_ref,
    q_grad_ref, v_grad_ref, key_sc, kt_sc, dk_sc, dv_sc, dq_sc,
):
    block = pl.program_id(0)
    blocks = pl.num_programs(0)

    @pl.when(block == 0)
    def _():
        def prep(at, carry):
            begin = pl.multiple_of(at * TILE, TILE)
            q = rows_at(q_ref, at).astype(jnp.float32)
            k = q * (norm_factor(q) * DH ** (-0.5))
            key_sc[pl.ds(begin, TILE), :] = k.astype(jnp.bfloat16)
            kt_sc[:, pl.ds(begin, TILE)] = k.T.astype(jnp.bfloat16)
            dk_sc[pl.ds(begin, TILE), :] = jnp.zeros((TILE, DH), jnp.float32)
            dv_sc[pl.ds(begin, TILE), :] = jnp.zeros((TILE, DH), jnp.float32)
            return carry

        lax.fori_loop(0, blocks, prep, 0)

    begin_row = block * TILE
    doc_start, first, full = tile_masks(begin_row, bounds_ref)
    q = rows_at(q_ref, block)
    hot = rows_at(hot_ref, block)
    grad = rows_at(grad_ref, block)
    log_row = log_ref[pl.ds(block, 1), :]
    delta = jnp.sum(grad.astype(jnp.float32).T * out_ref[...], 0, keepdims=True)
    key_row = lax.broadcasted_iota(jnp.int32, (TILE, 1), 0)
    lane = lax.broadcasted_iota(jnp.int32, (1, TILE), 1)

    itself = key_row == lane

    def fold(at, tiles, acc, masked, bounded, diagonal=False):
        rows = pl.ds(pl.multiple_of(at * TILE, TILE), tiles * TILE)
        s = dot(key_sc[rows, :], q, NT)
        c = dot(hot_ref[rows, :], hot, NT)
        up = dot(v_ref[rows, :], grad, NT)
        if diagonal:
            c = jnp.where((key_row < lane) & (key_row + begin_row >= doc_start), c, 0.0)
            c = jnp.where(itself, float(ROUNDS), c)
            s = jnp.where(itself, SELF_SCORE, s)
        elif masked:
            c = jnp.where(key_row + at * TILE >= doc_start, c, 0.0)
        if not bounded:
            s = jnp.where(c > 0, s, NEG_FILL)
        w = c * jnp.exp(s - log_row)
        ds = w * (up - delta)
        if diagonal:
            ds = jnp.where(itself, 0.0, ds)
        w = w.astype(jnp.bfloat16)
        ds = ds.astype(jnp.bfloat16)
        dv_sc[rows, :] += dot(w, grad, NN)
        dk_sc[rows, :] += dot(ds, q, NN)
        return acc + dot(kt_sc[:, rows], ds, NN)

    def store(acc):
        dq_sc[pl.ds(pl.multiple_of(begin_row, TILE), TILE), :] = acc.T

    nothing = jnp.zeros((DH, TILE), jnp.float32)

    @pl.when(bounds_ref[3] == 1)
    def _():
        acc = fold(block, 1, nothing, True, True, True)
        acc = lax.fori_loop(first, full, lambda at, x: fold(at, 1, x, True, True), acc)
        rest = (block - full) % GROUP
        acc = lax.fori_loop(full, full + rest, lambda at, x: fold(at, 1, x, False, True), acc)
        store(
            lax.fori_loop(
                0,
                (block - full) // GROUP,
                lambda at, x: fold(full + rest + GROUP * at, GROUP, x, False, True),
                acc,
            )
        )

    @pl.when(bounds_ref[3] == 0)
    def _():
        acc = fold(block, 1, nothing, True, False, True)
        store(lax.fori_loop(first, block, lambda at, x: fold(at, 1, x, True, False), acc))

    @pl.when(block == blocks - 1)
    def _():
        def finish(at, carry):
            begin = pl.multiple_of(at * TILE, TILE)
            q = rows_at(q_ref, at).astype(jnp.float32)
            r = norm_factor(q)
            g = rows_at(dk_sc, at).astype(jnp.bfloat16).astype(jnp.float32)
            back = (r * DH ** (-0.5)) * (g - q * (r * r * jnp.mean(q * g, -1, keepdims=True)))
            q_grad_ref[pl.ds(begin, TILE), :] = (rows_at(dq_sc, at) + back).astype(jnp.bfloat16)
            v_grad_ref[pl.ds(begin, TILE), :] = rows_at(dv_sc, at).astype(jnp.bfloat16)
            return carry

        lax.fori_loop(0, blocks, finish, 0)


def attend_back(bounds, q, v, hot, grad, out, logs):
    rows = q.shape[0]
    blocks = rows // TILE
    whole = lambda shape: pl.BlockSpec(shape, lambda i, *_: (0,) * len(shape))
    return pl.pallas_call(
        attend_back_kernel,
        name="attend_back",
        out_shape=(jax.ShapeDtypeStruct((rows, DH), jnp.bfloat16),) * 2,
        grid_spec=pltpu.PrefetchScalarGridSpec(
            num_scalar_prefetch=1,
            grid=(blocks,),
            in_specs=[
                whole((rows, DH)), whole((rows, DH)), whole((rows, ROUNDS * BUCKETS)), whole((rows, DH)),
                pl.BlockSpec((DH, TILE), lambda i, *_: (0, i)), whole((blocks, TILE)),
            ],
            out_specs=[whole((rows, DH))] * 2,
            scratch_shapes=[
                pltpu.VMEM((rows, DH), jnp.bfloat16),
                pltpu.VMEM((DH, rows), jnp.bfloat16),
                pltpu.VMEM((rows, DH), jnp.float32),
                pltpu.VMEM((rows, DH), jnp.float32),
                pltpu.VMEM((rows, DH), jnp.float32),
            ],
        ),
        compiler_params=pltpu.CompilerParams(
            dimension_semantics=("arbitrary",), vmem_limit_bytes=48 * 2**20
        ),
        cost_estimate=pl.CostEstimate(
            flops=rows * DH, bytes_accessed=rows * DH, transcendentals=0
        ),
    )(bounds, q, v, hot, grad, out, logs)


def place_matrix(places):
    rows = places.shape[0]
    return (jnp.arange(rows, dtype=jnp.int32)[:, None] == places[None, :]).astype(jnp.bfloat16)


def into_places(places, vectors):
    return jnp.einsum("pa,ad->pd", place_matrix(places), vectors, preferred_element_type=jnp.float32).astype(jnp.bfloat16)


def out_of_places(places, vectors):
    return jnp.einsum("pa,pd->ad", place_matrix(places), vectors, preferred_element_type=jnp.float32).astype(jnp.bfloat16)


def bucket_hot(buckets):
    hot = buckets.T[:, :, None] == jnp.arange(BUCKETS, dtype=jnp.int32)
    return hot.astype(jnp.bfloat16).reshape(buckets.shape[1], ROUNDS * BUCKETS)


def doc_bounds(segments):
    return jnp.sum((segments[None, :] < jnp.arange(1, 4, dtype=jnp.int32)[:, None]).astype(jnp.int32), 1)


def with_bound(bounds, queries):
    squares = jnp.sum(queries.astype(jnp.float32) ** 2, -1)
    return jnp.concatenate([bounds, (jnp.max(squares) <= BOUND**2).astype(jnp.int32)[None]])


def smooth_unit(values_in):
    return jax.nn.gelu(values_in, approximate=False)


def norm_rows(rows_wide, gain_row, shift_row):
    centre = jnp.mean(rows_wide, -1, keepdims=True)
    offset = rows_wide - centre
    inverse = lax.rsqrt(jnp.mean(offset * offset, -1, keepdims=True) + 1e-05)
    scaled = offset * inverse
    return (scaled * gain_row + shift_row, scaled, inverse)


def unit_keys(queries):
    shaped = queries.reshape(queries.shape[:-1] + (queries.shape[-1] // DH, DH))
    factor = lax.rsqrt(jnp.mean(shaped * shaped, -1, keepdims=True) + 1e-06) * DH ** (-0.5)
    return (shaped * factor).reshape(queries.shape)


def heads_view(vectors):
    return vectors.reshape(vectors.shape[0], vectors.shape[1], vectors.shape[2] // DH, DH)


def full_rows(sliced):
    return lax.all_gather(sliced, "tp", axis=2, tiled=True)


def branch_sum(partial_value):
    return lax.psum_scatter(partial_value, "tp", scatter_dimension=2, tiled=True)


def norm_back(grad_slice, scaled_slice, inverse, gain_slice):
    weighted = grad_slice * gain_slice
    first_sum, second_sum = lax.psum(
        (jnp.sum(weighted, -1, keepdims=True), jnp.sum(weighted * scaled_slice, -1, keepdims=True)),
        "tp",
    )
    inner = inverse * (weighted - first_sum / D - scaled_slice * (second_sum / D))
    return (inner, jnp.sum(grad_slice * scaled_slice, (0, 1)), jnp.sum(grad_slice, (0, 1)))


def label_rows(all_labels, begin_row, extent):
    all_segments, all_buckets, all_positions = all_labels
    return (
        lax.dynamic_slice_in_dim(all_segments, begin_row, extent, 1),
        lax.dynamic_slice_in_dim(all_buckets, begin_row, extent, 2),
        lax.dynamic_slice_in_dim(all_positions, begin_row, extent, 1),
    )


def block_weights(query_heads, query_labels, key_heads, key_labels):
    query_seg, query_buck, query_pos = query_labels
    key_seg, key_buck, key_pos = key_labels
    scores = jnp.einsum(
        "pshd,kshd->shpk", query_heads, key_heads, preferred_element_type=jnp.float32
    )
    matches = jnp.sum((query_buck[:, :, :, None] == key_buck[:, :, None, :]).astype(jnp.int32), 1)
    same_doc = query_seg[:, :, None] == key_seg[:, None, :]
    earlier = key_pos[:, None, :] < query_pos[:, :, None]
    itself = key_pos[:, None, :] == query_pos[:, :, None]
    counts = jnp.where(itself, ROUNDS, jnp.where(earlier & same_doc, matches, 0)).astype(
        jnp.float32
    )[:, None]
    shifted = jnp.where(itself[:, None], SELF_SCORE, scores)
    return (shifted, counts, itself[:, None])


def weights_of(shifted, counts, log_total):
    return jnp.where(counts > 0, counts * jnp.exp(shifted - log_total[..., None]), 0.0)


def blockwise(advance, running, row_count):
    extent = BLOCK_ROWS

    def turn(state_now, block_index):
        return (advance(state_now, block_index * extent, extent), None)

    return lax.scan(turn, running, jnp.arange(row_count // extent, dtype=jnp.int32))[0]


def over_keys(key_vectors, value_vectors, folder, initial):
    return folder(
        initial,
        (
            lax.all_gather(key_vectors, "ctx", axis=0, tiled=True),
            lax.all_gather(value_vectors, "ctx", axis=0, tiled=True),
        ),
        jnp.int32(0),
    )


def over_context(first_part, second_part, third_part, fourth_part, fifth_part):
    return (
        lax.psum(first_part.astype(jnp.bfloat16), "ctx").astype(jnp.float32),
        lax.psum(second_part.astype(jnp.bfloat16), "ctx").astype(jnp.float32),
        lax.psum(third_part.astype(jnp.bfloat16), "ctx").astype(jnp.float32),
        lax.psum(fourth_part.astype(jnp.bfloat16), "ctx").astype(jnp.float32),
        lax.psum(fifth_part.astype(jnp.bfloat16), "ctx").astype(jnp.float32),
    )


def to_row_owners(first_part, second_part, third_part):
    return (
        lax.psum_scatter(
            first_part.astype(jnp.bfloat16), "shard", scatter_dimension=0, tiled=True
        ).astype(jnp.float32),
        lax.psum_scatter(
            second_part.astype(jnp.bfloat16), "shard", scatter_dimension=0, tiled=True
        ).astype(jnp.float32),
        lax.psum_scatter(
            third_part.astype(jnp.bfloat16), "shard", scatter_dimension=0, tiled=True
        ).astype(jnp.float32),
    )


def to_col_owners(first_part, second_part):
    return (
        lax.psum_scatter(
            first_part.astype(jnp.bfloat16), "shard", scatter_dimension=1, tiled=True
        ).astype(jnp.float32),
        lax.psum_scatter(
            second_part.astype(jnp.bfloat16), "shard", scatter_dimension=1, tiled=True
        ).astype(jnp.float32),
    )


def general_device(
    first_half,
    second_half,
    first_cotangent,
    second_cotangent,
    segment_ids,
    bucket_ids,
    positions,
    query_weight,
    value_weight,
    output_weight,
    expand_weight,
    expand_bias,
    shrink_weight,
    shrink_bias,
    attention_gain,
    attention_shift,
    forward_gain,
    forward_shift,
):
    rows_here, seqs_here, slice_width = first_half.shape
    width_heads = query_weight.shape[1]
    heads_here = width_heads // DH
    tp_start = lax.axis_index("tp") * slice_width
    ctx_start = lax.axis_index("ctx") * rows_here
    bf16 = jnp.bfloat16
    f32 = jnp.float32

    def columns(wide):
        return lax.dynamic_slice_in_dim(wide, tp_start, slice_width, wide.ndim - 1)

    full_query, full_value, full_expand = (
        lax.all_gather(query_weight, "shard", axis=0, tiled=True),
        lax.all_gather(value_weight, "shard", axis=0, tiled=True),
        lax.all_gather(expand_weight, "shard", axis=0, tiled=True),
    )
    full_output, full_shrink = (
        lax.all_gather(output_weight, "shard", axis=1, tiled=True),
        lax.all_gather(shrink_weight, "shard", axis=1, tiled=True),
    )
    all_labels = (
        lax.all_gather(segment_ids, "ctx", axis=1, tiled=True),
        lax.all_gather(bucket_ids, "ctx", axis=2, tiled=True),
        lax.all_gather(positions, "ctx", axis=1, tiled=True),
    )
    local_labels = label_rows(all_labels, ctx_start, rows_here)
    second_wide = full_rows(second_half)
    normed, attn_scaled, attn_inverse = norm_rows(
        second_wide.astype(f32), attention_gain, attention_shift
    )
    normed = normed.astype(bf16)
    queries = jnp.einsum("psd,de->pse", normed, full_query, preferred_element_type=f32).astype(bf16)
    key_vectors = unit_keys(queries.astype(f32)).astype(bf16)
    value_vectors = jnp.einsum(
        "psd,de->pse", normed, full_value, preferred_element_type=f32
    ).astype(bf16)
    query_heads = heads_view(queries)
    stat_shape = (seqs_here, heads_here, rows_here)
    head_zero = jnp.zeros((rows_here, seqs_here, heads_here, DH), f32)

    def norm_fold(running, pieces, begin_row):
        key_piece = pieces[0]

        def advance(state_now, offset, extent):
            highest, summed = state_now
            key_heads = heads_view(lax.dynamic_slice_in_dim(key_piece, offset, extent, 0))
            shifted, counts, _ = block_weights(
                query_heads, local_labels, key_heads, label_rows(all_labels, offset, extent)
            )
            usable = counts > 0
            new_high = jnp.maximum(highest, jnp.max(jnp.where(usable, shifted, NEG_FILL), -1))
            summed = summed * jnp.exp(highest - new_high) + jnp.sum(
                jnp.where(usable, counts * jnp.exp(shifted - new_high[..., None]), 0.0), -1
            )
            return (new_high, summed)

        return blockwise(advance, running, key_piece.shape[0])

    highest, summed = over_keys(
        key_vectors,
        value_vectors,
        norm_fold,
        (jnp.full(stat_shape, NEG_FILL, f32), jnp.zeros(stat_shape, f32)),
    )
    log_total = highest + jnp.log(summed)

    def key_block(pieces, offset, extent):
        key_heads = heads_view(lax.dynamic_slice_in_dim(pieces[0], offset, extent, 0))
        value_heads = heads_view(lax.dynamic_slice_in_dim(pieces[1], offset, extent, 0))
        shifted, counts, itself = block_weights(
            query_heads, local_labels, key_heads, label_rows(all_labels, offset, extent)
        )
        return (key_heads, value_heads, weights_of(shifted, counts, log_total), itself)

    def mix_fold(running, pieces, begin_row):

        def advance(state_now, offset, extent):
            key_heads, value_heads, weights, itself = key_block(pieces, offset, extent)
            return state_now + jnp.einsum(
                "shpk,kshd->pshd", weights.astype(bf16), value_heads, preferred_element_type=f32
            )

        return blockwise(advance, running, pieces[0].shape[0])

    head_mix = over_keys(key_vectors, value_vectors, mix_fold, head_zero)
    attention = head_mix.reshape(rows_here, seqs_here, width_heads).astype(bf16)
    branch = branch_sum(
        jnp.einsum("pse,ed->psd", attention, full_output, preferred_element_type=f32)
    )
    first_out = (first_half.astype(f32) + branch).astype(bf16)
    first_wide = full_rows(first_out)
    ffn_in, ffn_scaled, ffn_inverse = norm_rows(first_wide.astype(f32), forward_gain, forward_shift)
    ffn_in = ffn_in.astype(bf16)
    pre_act = (
        jnp.einsum("psd,df->psf", ffn_in, full_expand, preferred_element_type=f32) + expand_bias
    )
    hidden_exact, unit_pull = jax.vjp(smooth_unit, pre_act)
    hidden = hidden_exact.astype(bf16)
    second_branch = (
        branch_sum(jnp.einsum("psf,fd->psd", hidden, full_shrink, preferred_element_type=f32))
        + shrink_bias
    )
    second_out = (second_half.astype(f32) + second_branch).astype(bf16)
    cotangent_wide = full_rows(second_cotangent)
    hidden_grad = jnp.einsum("psd,fd->psf", cotangent_wide, full_shrink, preferred_element_type=f32)
    pre_grad = unit_pull(hidden_grad)[0].astype(bf16)
    shrink_grad = jnp.einsum("psf,psd->fd", hidden, cotangent_wide, preferred_element_type=f32)
    shrink_bias_grad = jnp.sum(second_cotangent.astype(f32), (0, 1))
    expand_grad = jnp.einsum("psd,psf->df", ffn_in, pre_grad, preferred_element_type=f32)
    expand_bias_grad = jnp.sum(pre_grad.astype(f32), (0, 1))
    ffn_grad = branch_sum(
        jnp.einsum("psf,df->psd", pre_grad, full_expand, preferred_element_type=f32)
    )
    ffn_back, forward_gain_grad, forward_shift_grad = norm_back(
        ffn_grad, columns(ffn_scaled), ffn_inverse, columns(forward_gain)
    )
    first_grad = (first_cotangent.astype(f32) + ffn_back).astype(bf16)
    grad_wide = full_rows(first_grad)
    output_grad = jnp.einsum("pse,psd->ed", attention, grad_wide, preferred_element_type=f32)
    attention_grad = jnp.einsum(
        "psd,ed->pse", grad_wide, full_output, preferred_element_type=f32
    ).astype(bf16)
    grad_heads = heads_view(attention_grad)

    def delta_fold(running, pieces, begin_row):

        def advance(state_now, offset, extent):
            key_heads, value_heads, weights, itself = key_block(pieces, offset, extent)
            upstream = jnp.einsum(
                "pshd,kshd->shpk", grad_heads, value_heads, preferred_element_type=f32
            )
            return state_now + jnp.sum(weights * upstream, -1)

        return blockwise(advance, running, pieces[0].shape[0])

    row_delta = over_keys(key_vectors, value_vectors, delta_fold, jnp.zeros(stat_shape, f32))

    def query_fold(running, pieces, begin_row):

        def advance(state_now, offset, extent):
            key_heads, value_heads, weights, itself = key_block(pieces, offset, extent)
            upstream = jnp.einsum(
                "pshd,kshd->shpk", grad_heads, value_heads, preferred_element_type=f32
            )
            score_grad = jnp.where(itself, 0.0, weights * (upstream - row_delta[..., None])).astype(
                bf16
            )
            return state_now + jnp.einsum(
                "shpk,kshd->pshd", score_grad, key_heads, preferred_element_type=f32
            )

        return blockwise(advance, running, pieces[0].shape[0])

    query_part = over_keys(key_vectors, value_vectors, query_fold, head_zero)
    query_lse, query_delta = (
        lax.all_gather(log_total, "ctx", axis=2, tiled=True),
        lax.all_gather(row_delta, "ctx", axis=2, tiled=True),
    )
    local_keys = heads_view(key_vectors)
    local_values = heads_view(value_vectors)
    query_piece = lax.all_gather(queries, "ctx", axis=0, tiled=True)
    grad_piece = lax.all_gather(attention_grad, "ctx", axis=0, tiled=True)

    def advance(state_now, offset, extent):
        remote_queries = heads_view(lax.dynamic_slice_in_dim(query_piece, offset, extent, 0))
        remote_grads = heads_view(lax.dynamic_slice_in_dim(grad_piece, offset, extent, 0))
        lse_rows = lax.dynamic_slice_in_dim(query_lse, offset, extent, 2)
        delta_rows = lax.dynamic_slice_in_dim(query_delta, offset, extent, 2)
        shifted, counts, itself = block_weights(
            remote_queries, label_rows(all_labels, offset, extent), local_keys, local_labels
        )
        weights = weights_of(shifted, counts, lse_rows)
        upstream = jnp.einsum(
            "pshd,kshd->shpk", remote_grads, local_values, preferred_element_type=f32
        )
        score_grad = jnp.where(itself, 0.0, weights * (upstream - delta_rows[..., None])).astype(
            bf16
        )
        key_now = state_now[0] + jnp.einsum(
            "shpk,pshd->kshd", score_grad, remote_queries, preferred_element_type=f32
        )
        value_now = state_now[1] + jnp.einsum(
            "shpk,pshd->kshd", weights.astype(bf16), remote_grads, preferred_element_type=f32
        )
        return (key_now, value_now)

    key_part, value_part = blockwise(advance, (head_zero, head_zero), query_piece.shape[0])
    keys_grad = key_part.reshape(rows_here, seqs_here, width_heads).astype(bf16)
    values_grad = value_part.reshape(rows_here, seqs_here, width_heads).astype(bf16)
    unit_back = jax.vjp(unit_keys, queries.astype(f32))[1]
    queries_total = (
        query_part.reshape(rows_here, seqs_here, width_heads) + unit_back(keys_grad.astype(f32))[0]
    ).astype(bf16)
    query_grad = jnp.einsum("psd,pse->de", normed, queries_total, preferred_element_type=f32)
    value_grad = jnp.einsum("psd,pse->de", normed, values_grad, preferred_element_type=f32)
    normed_grad = branch_sum(
        jnp.einsum("pse,de->psd", queries_total, full_query, preferred_element_type=f32)
        + jnp.einsum("pse,de->psd", values_grad, full_value, preferred_element_type=f32)
    )
    attn_back, attention_gain_grad, attention_shift_grad = norm_back(
        normed_grad, columns(attn_scaled), attn_inverse, columns(attention_gain)
    )
    second_grad = (second_cotangent.astype(f32) + attn_back).astype(bf16)
    expand_bias_sum, shrink_bias_sum, attn_gain_sum, attn_shift_sum, ffn_gain_sum, ffn_shift_sum = (
        lax.psum(
            (
                expand_bias_grad,
                shrink_bias_grad,
                attention_gain_grad,
                attention_shift_grad,
                forward_gain_grad,
                forward_shift_grad,
            ),
            ("shard", "ctx"),
        )
    )
    query_sum, value_sum, expand_sum, output_sum, shrink_sum = over_context(
        query_grad, value_grad, expand_grad, output_grad, shrink_grad
    )
    query_own, value_own, expand_own = to_row_owners(query_sum, value_sum, expand_sum)
    output_own, shrink_own = to_col_owners(output_sum, shrink_sum)
    return (
        first_out,
        second_out,
        first_grad,
        second_grad,
        query_own,
        value_own,
        output_own,
        expand_own,
        expand_bias_sum,
        shrink_own,
        shrink_bias_sum,
        attn_gain_sum,
        attn_shift_sum,
        ffn_gain_sum,
        ffn_shift_sum,
    )


def swap(vectors, axis, bits):
    size = lax.axis_size(axis)
    return lax.ppermute(vectors, axis, [(at, at ^ bits) for at in range(size)])


def where_am_i():
    return lax.axis_index("shard"), lax.axis_index("ctx"), lax.axis_index("tp")


def plane_pairs(step, inverse):
    shards, planes = lax.axis_size("shard"), lax.axis_size("tp")
    local_seqs = planes // shards
    pairs = []
    for shard in range(shards):
        for plane in range(planes):
            chunk = step ^ plane
            there = (chunk % shards) * planes + shard * local_seqs + chunk // shards
            here = shard * planes + plane
            pairs.append((there, here) if inverse else (here, there))
    return pairs


def rows_in(sliced, beside=(), extra=None):
    shard, _, plane = where_am_i()
    shards, planes = lax.axis_size("shard"), lax.axis_size("tp")
    count, slots, seqs, width = sliced.shape
    extent = slots // shards
    by_seq = sliced.transpose(2, 0, 1, 3).reshape(seqs, count, shards, extent, width)
    by_seq = by_seq.transpose(0, 2, 1, 3, 4).reshape(seqs * shards, count * extent, width)
    if extra is not None:
        by_seq = jnp.concatenate([by_seq, jnp.concatenate([extra] * seqs, 0)], 1)
    mine = (plane % seqs) * shards + shard
    landed = []
    for step in range(planes):
        chunk = lax.dynamic_index_in_dim(by_seq, step ^ plane, 0, False)
        landed.append(lax.ppermute(chunk, ("shard", "tp"), plane_pairs(step, False)))
    landed, beside = lax.optimization_barrier((landed, beside))
    whole = jnp.zeros((count * extent, planes * width), sliced.dtype)
    for step in range(planes):
        piece = landed[step][: count * extent]
        whole = lax.dynamic_update_slice_in_dim(whole, piece, (step ^ mine) * width, 1)
    whole = whole.reshape(count, extent, planes * width)
    if extra is None:
        return whole, beside
    extras = jnp.zeros((planes,) + extra.shape[1:], extra.dtype)
    for step in range(planes):
        piece = landed[step][None, count * extent :]
        extras = lax.dynamic_update_slice_in_dim(extras, piece, step ^ mine, 0)
    return whole, beside, extras


def rows_out(whole, seqs, beside=()):
    shard, _, plane = where_am_i()
    shards, planes = lax.axis_size("shard"), lax.axis_size("tp")
    count, extent, features = whole.shape
    width = features // planes
    mine = (plane % seqs) * shards + shard
    flat = whole.reshape(count * extent, features)
    landed = []
    for step in range(planes):
        piece = lax.dynamic_slice_in_dim(flat, (step ^ mine) * width, width, 1)
        landed.append(lax.ppermute(piece, ("shard", "tp"), plane_pairs(step, True)))
    landed, beside = lax.optimization_barrier((landed, beside))
    by_seq = jnp.zeros((seqs * shards, count * extent, width), whole.dtype)
    for step in range(planes):
        by_seq = lax.dynamic_update_slice_in_dim(by_seq, landed[step][None], step ^ plane, 0)
    parts = by_seq.reshape(seqs, shards, count, extent, width).transpose(2, 1, 3, 0, 4)
    return parts.reshape(count, shards * extent, seqs, width), beside


def quarter_of(local, at):
    extent = local.shape[0] // lax.axis_size("ctx")
    return lax.dynamic_slice_in_dim(local, at * extent, extent, 0)


def by_half(own, other):
    first = lax.axis_index("shard") == 0
    return jnp.stack([jnp.where(first, own, other), jnp.where(first, other, own)])


def plain(vectors):
    return with_layout_constraint(vectors, Layout(major_to_minor=tuple(range(vectors.ndim))))


def core_parts(local):
    mine = quarter_of(local, lax.axis_index("ctx"))
    return by_half(mine, swap(mine, "shard", 1))


def split_bias(values):
    high = values.astype(jnp.bfloat16)
    rest = values - high.astype(jnp.float32)
    middle = rest.astype(jnp.bfloat16)
    return jnp.stack([high, middle, (rest - middle.astype(jnp.float32)).astype(jnp.bfloat16)])


def shard_half(wide, at):
    extent = wide.shape[1] // 2
    return lax.dynamic_slice_in_dim(wide, at * extent, extent, 1)


def chip_sums(rows_wide, columns_wide):
    shard = lax.axis_index("shard")

    def product(at):
        return lax.dot_general(
            shard_half(rows_wide, at),
            columns_wide,
            (((0,), (0,)), ((), ())),
            preferred_element_type=jnp.float32,
        )

    theirs = swap(product(1 - shard).astype(jnp.bfloat16), "shard", 1)
    return product(shard) + theirs.astype(jnp.float32)


def sum_parts(parts):
    return jnp.sum(parts.astype(jnp.float32), 0)


def send_ctx(sums):
    quarters = lax.axis_size("ctx")
    parts = sums.reshape(quarters, sums.shape[0] // quarters, sums.shape[1])
    return lax.all_to_all(parts, "ctx", 0, 0, tiled=True)


def scatter_ctx(sums):
    return sum_parts(send_ctx(sums))


def scatter_tp(sums):
    planes = lax.axis_size("tp")
    parts = sums.reshape(sums.shape[0], planes, -1).transpose(1, 0, 2)
    return sum_parts(lax.all_to_all(parts, "tp", 0, 0, tiled=True))


def collect_ctx(quarter):
    quarters = lax.axis_size("ctx")
    return in_order([quarter] + [swap(quarter, "ctx", j) for j in range(1, quarters)])


def in_order(pieces):
    ctx, extent = lax.axis_index("ctx"), pieces[0].shape[0]
    whole = jnp.zeros((len(pieces) * extent,) + pieces[0].shape[1:], pieces[0].dtype)
    for j, piece in enumerate(pieces):
        whole = lax.dynamic_update_slice_in_dim(whole, piece, (ctx ^ j) * extent, 0)
    return whole


def reduce_context_first(sums):
    bf16 = jnp.bfloat16
    quarter = scatter_ctx(sums.astype(bf16)).astype(bf16)
    return collect_ctx(scatter_tp(quarter).astype(bf16)).astype(jnp.float32)


def plane_part(parts, k):
    return lax.dynamic_index_in_dim(parts, lax.axis_index("tp") ^ k, 0, False)


def sum_everywhere(parts):
    total = plane_part(parts, 0)
    total = sum((swap(plane_part(parts, k), "tp", k) for k in range(1, lax.axis_size("tp"))), total)
    total = total + swap(total, "shard", 1)
    return sum(swap(total, "ctx", j) for j in range(1, lax.axis_size("ctx"))) + total


def after(values, ready):
    return lax.optimization_barrier((values, ready))[0]


def row_norm_back(grad, scaled, inverse, gain):
    weighted = grad * gain
    first = jnp.mean(weighted, -1, keepdims=True)
    second = jnp.mean(weighted * scaled, -1, keepdims=True)
    inner = inverse * (weighted - first - scaled * second)
    return inner, jnp.sum(grad * scaled, 0), jnp.sum(grad, 0)


def heads_out(vectors):
    heads = HEADS
    sent = vectors.reshape(vectors.shape[0], heads, -1).transpose(1, 0, 2)
    landed = lax.all_to_all(sent, ("ctx", "shard"), split_axis=0, concat_axis=0, tiled=True)
    return landed.reshape(-1, landed.shape[2])


def heads_back(vectors):
    sent = vectors.reshape(HEADS, -1, vectors.shape[1])
    landed = lax.all_to_all(sent, ("ctx", "shard"), split_axis=0, concat_axis=0, tiled=True)
    return landed.transpose(1, 0, 2).reshape(landed.shape[1], -1)


def plane_labels(segment_ids, bucket_ids, positions):
    shard, _, plane = where_am_i()
    seqs, slots = positions.shape
    packed = jnp.concatenate([positions[:, None], segment_ids[:, None], bucket_ids], 1)
    kinds = packed.shape[1]
    mine = lax.dynamic_index_in_dim(packed, plane % seqs, 0, False).reshape(-1, 128)
    mine = jnp.where(shard == plane // seqs, mine, swap(mine, "shard", 1))
    whole = collect_ctx(mine).reshape(-1, kinds, slots).transpose(1, 0, 2).reshape(kinds, -1)
    return whole[0], whole[1], whole[2:]


def pack_rows_kernel(code_ref, *refs):
    out_ref = refs[-1]
    extent = refs[0].shape[0]
    for j, ref in enumerate(refs[:-1]):
        out_ref[pl.ds(pl.multiple_of((code_ref[0] ^ j) * extent, extent), extent), :] = ref[...]


def pack_rows(pieces, code):
    extent, width = pieces[0].shape
    whole = lambda shape: pl.BlockSpec(shape, lambda i, *_: (0, 0))
    return pl.pallas_call(
        pack_rows_kernel,
        name="pack_rows",
        out_shape=jax.ShapeDtypeStruct((len(pieces) * extent, width), pieces[0].dtype),
        grid_spec=pltpu.PrefetchScalarGridSpec(
            num_scalar_prefetch=1,
            grid=(1,),
            in_specs=[whole((extent, width)) for _ in pieces],
            out_specs=whole((len(pieces) * extent, width)),
        ),
        compiler_params=pltpu.CompilerParams(vmem_limit_bytes=24 * 2**20),
        cost_estimate=pl.CostEstimate(flops=0, bytes_accessed=4 * len(pieces) * extent * width, transcendentals=0),
    )(jnp.reshape(code, (1,)).astype(jnp.int32), *pieces)


def pack_weights_kernel(code_ref, near_ref, far_ref, *refs):
    out_ref = refs[-1]
    units = near_ref.shape[1] // 2
    out_ref[:, :units] = near_ref[:, :units]
    out_ref[:, units : 2 * units] = far_ref[:, :units]
    out_ref[:, 2 * units : 3 * units] = near_ref[:, units:]
    out_ref[:, 3 * units : 4 * units] = far_ref[:, units:]
    width = refs[0].shape[1]
    for k, ref in enumerate(refs[:-1]):
        place = pl.multiple_of(4 * units + (code_ref[0] ^ k) * width, width)
        out_ref[:, pl.ds(place, width)] = ref[...]


def pack_weights(near, far, outs, code):
    extent, units = near.shape
    width = outs[0].shape[1]
    columns = 2 * units + len(outs) * width
    whole = lambda shape: pl.BlockSpec(shape, lambda i, *_: (0, 0))
    return pl.pallas_call(
        pack_weights_kernel,
        name="pack_weights",
        out_shape=jax.ShapeDtypeStruct((extent, columns), near.dtype),
        grid_spec=pltpu.PrefetchScalarGridSpec(
            num_scalar_prefetch=1,
            grid=(1,),
            in_specs=[whole((extent, units))] * 2 + [whole((extent, width)) for _ in outs],
            out_specs=whole((extent, columns)),
        ),
        compiler_params=pltpu.CompilerParams(vmem_limit_bytes=24 * 2**20),
        cost_estimate=pl.CostEstimate(flops=0, bytes_accessed=4 * extent * columns, transcendentals=0),
    )(jnp.reshape(code, (1,)).astype(jnp.int32), near, far, *outs)


def row_device(
    first_half,
    second_half,
    first_cotangent,
    second_cotangent,
    segment_ids,
    bucket_ids,
    positions,
    query_weight,
    value_weight,
    output_weight,
    expand_weight,
    expand_bias,
    shrink_weight,
    shrink_bias,
    attention_gain,
    attention_shift,
    forward_gain,
    forward_shift,
):
    bf16, f32 = jnp.bfloat16, jnp.float32
    planes = lax.axis_size("tp")
    shard, ctx, plane = where_am_i()
    seqs_here, width = first_half.shape[1:]
    units = expand_bias.shape[0]
    split = query_weight.shape[0]

    local_pair = jnp.stack(
        [query_weight.reshape(split, -1, DH), value_weight.reshape(split, -1, DH)], 2
    ).reshape(split, -1)
    pair_parts = core_parts(local_pair)
    pair_rows = pair_parts.shape[1] * pair_parts.shape[2] // width
    biases = split_bias(jnp.concatenate([expand_bias, shrink_bias])).reshape(-1, width)
    bias_rows = biases.shape[0]
    biases = jnp.pad(biases, ((0, -bias_rows % 16), (0, 0)))
    extra = jnp.concatenate(
        [pair_parts.reshape(-1, pair_rows, width), jnp.stack([biases] * pair_parts.shape[0])], 1
    )
    (second_rows,), _, extras = rows_in(second_half[None], (), extra)
    biases = extras[:, pair_rows : pair_rows + bias_rows].astype(f32).reshape(planes, 3, -1)
    biases = (biases[:, 0] + biases[:, 1]) + biases[:, 2]
    unit_bias = jnp.concatenate(
        [
            lax.dynamic_index_in_dim(biases, plane, 0, False)[:units],
            lax.dynamic_index_in_dim(biases, plane ^ 2, 0, False)[:units],
        ]
    )
    row_bias = biases[:, units:].reshape(-1)

    pair_wide = extras[:, :pair_rows].reshape((planes,) + pair_parts.shape[1:]).transpose(1, 0, 2)
    pair_wide = plain(pair_wide.reshape(pair_parts.shape[1], -1))
    up, down, out = (
        quarter_of(item, ctx) for item in (expand_weight, shrink_weight.T, output_weight.T)
    )
    quarters = lax.axis_size("ctx")
    pair_pieces, (normed, attn_scaled, attn_inverse), labels = lax.optimization_barrier(
        (
            [swap(pair_wide, "ctx", j) for j in range(1, quarters)],
            norm_rows(second_rows.astype(f32), attention_gain, attention_shift),
            plane_labels(*after((segment_ids, bucket_ids, positions), second_rows)),
        )
    )
    places, segments, buckets = labels
    normed = normed.astype(bf16)
    pair_mine = pack_rows([pair_wide] + pair_pieces, ctx)
    pair_other = swap(pair_mine, "shard", 1)
    pair = (
        dot(shard_half(normed, shard), pair_mine, NN)
        + dot(shard_half(normed, 1 - shard), pair_other, NN)
    ).astype(bf16)
    sent, out = after((plain(jnp.concatenate([up, down], 1)), plain(out)), pair_mine)
    landed, far, outs_near, hot, bounds = lax.optimization_barrier(
        (
            heads_out(pair),
            swap(sent, "tp", 2),
            [swap(out, "tp", k) for k in range(1, planes)],
            into_places(places, bucket_hot(buckets)),
            doc_bounds(segments),
        )
    )
    wide = pack_weights(sent, far, [out] + outs_near, plane)
    whole = lax.all_gather(after(wide, landed), ("shard", "ctx"), axis=0, tiled=True)
    up_full, down_full, output_full = (
        whole[:, : 2 * units],
        whole[:, 2 * units : 4 * units],
        whole[:, 4 * units :],
    )

    sorted_pair = into_places(places, landed)
    query_sorted, value_sorted = sorted_pair[:, :DH], sorted_pair[:, DH:]
    bounds = with_bound(bounds, query_sorted)
    (first_rows, second_grad_rows), (mix, logs) = rows_in(
        after(jnp.stack([first_half, second_cotangent]), landed),
        attend(bounds, query_sorted, value_sorted, hot),
    )
    far_grad_rows = swap(after(second_grad_rows, mix), "tp", 1)
    attention = heads_back(out_of_places(places, mix.T.astype(bf16)))

    first_out = (first_rows.astype(f32) + dot(attention, output_full, NT)).astype(bf16)
    ffn_in, ffn_scaled, ffn_inverse = norm_rows(first_out.astype(f32), forward_gain, forward_shift)
    ffn_in, far_grad_rows = lax.optimization_barrier((ffn_in.astype(bf16), far_grad_rows))

    def units_of(rows, grad_rows):
        pre_act = dot(rows, up_full, NN) + unit_bias
        below = 0.5 * (1.0 + lax.erf(pre_act * 2**-0.5))
        slope = below + pre_act * (jnp.exp(-0.5 * pre_act * pre_act) * (2 * jnp.pi) ** -0.5)
        pre_grad = (dot(grad_rows, down_full, NN) * slope).astype(bf16)
        return (pre_act * below).astype(bf16), pre_grad

    normed_all = lax.all_gather(after(normed, first_out), ("ctx", "shard"), axis=0, tiled=True)
    far_in, (hidden, pre_grad) = lax.optimization_barrier(
        (swap(ffn_in, "tp", 1), units_of(ffn_in, second_grad_rows))
    )
    (first_grad_rows,), (far_hidden, far_pre_grad) = rows_in(
        after(first_cotangent, far_in)[None], units_of(far_in, far_grad_rows)
    )
    far_ffn_grad = dot(far_pre_grad, up_full, NT).astype(bf16)
    all_rows = jnp.concatenate([ffn_in, far_in], 0)
    all_grad_rows = jnp.concatenate([second_grad_rows, far_grad_rows], 0)
    all_pre_grad = jnp.concatenate([pre_grad, far_pre_grad], 0)
    all_hidden = jnp.concatenate([hidden, far_hidden], 0)
    all_rows, all_grad_rows, pre_grad = after((all_rows, all_grad_rows, pre_grad), far_ffn_grad)
    theirs, far_branch, own_branch, ffn_grad, expand_sums, shrink_sums = lax.optimization_barrier(
        (
            swap(far_ffn_grad, "tp", 1),
            dot(far_hidden, down_full, NT).astype(bf16),
            second_rows.astype(f32) + dot(hidden, down_full, NT) + row_bias,
            dot(pre_grad, up_full, NT),
            chip_sums(all_rows, all_pre_grad).astype(bf16),
            chip_sums(all_grad_rows, all_hidden).astype(bf16),
        )
    )
    ffn_back, ffn_gain_grad, ffn_shift_grad = row_norm_back(
        ffn_grad + theirs.astype(f32), ffn_scaled, ffn_inverse, forward_gain
    )
    first_grad = (first_grad_rows.astype(f32) + ffn_back).astype(bf16)
    attention_grad = dot(first_grad, output_full, NN).astype(bf16)
    shrink_bias_grad = jnp.sum(second_grad_rows.astype(f32), 0)
    expand_bias_grad = jnp.sum(all_pre_grad.astype(f32), 0)
    far_branch = swap(far_branch, "tp", 1)

    spread = jnp.arange(planes, dtype=jnp.int32)[:, None]
    unit_grads = jnp.where(spread == plane, expand_bias_grad[None, :units], 0.0)
    unit_grads = jnp.where(spread == plane ^ 2, expand_bias_grad[None, units:], unit_grads)
    packed = jnp.concatenate(
        [unit_grads]
        + [item.reshape(planes, width) for item in (shrink_bias_grad, ffn_gain_grad, ffn_shift_grad)],
        1,
    )
    packed = (packed + swap(packed, "shard", 1)).astype(bf16).reshape(planes, quarters, -1)
    vector_width = packed.shape[2]
    packed = jnp.pad(packed, ((0, 0), (0, 0), (0, 16 * width - vector_width)))
    packed = packed.reshape(planes, quarters, 16, width).transpose(1, 2, 0, 3)
    packed = jnp.pad(packed.reshape(quarters, 16, -1), ((0, 0), (0, 0), (4 * units, 0)))
    early = jnp.concatenate(
        [expand_sums, shrink_sums, chip_sums(first_grad, attention).astype(bf16)], 1
    )
    early = jnp.concatenate([early.reshape(quarters, split // quarters, -1), packed], 1)
    early = early.reshape(-1, early.shape[2])
    grad_heads, early, normed_all = lax.optimization_barrier(
        (heads_out(attention_grad), early, normed_all)
    )
    early_mine = lax.psum_scatter(early, "ctx", scatter_dimension=0, tiled=True)
    outs_sliced, parts = rows_out(
        after(jnp.stack([first_out, first_grad]), grad_heads),
        seqs_here,
        attend_back(
            bounds, query_sorted, value_sorted, hot, into_places(places, grad_heads), mix, logs
        ),
    )
    far_branch, own_branch = after((far_branch, own_branch), parts)
    second_out = (own_branch + far_branch.astype(f32)).astype(bf16)
    pair_grad_heads = out_of_places(places, jnp.concatenate(parts, 1))
    early_mine = after(early_mine, pair_grad_heads)
    far_sums = jnp.concatenate(
        [early_mine[:, units : 2 * units], early_mine[:, 3 * units : 4 * units]], 1
    )
    near_sums = jnp.concatenate([early_mine[:, :units], early_mine[:, 2 * units : 3 * units]], 1)

    pair_sums = lax.dot_general(
        normed_all, pair_grad_heads, (((0,), (0,)), ((), ())), preferred_element_type=f32
    ).astype(bf16)
    late = early_mine[:, 4 * units :].reshape(-1, planes, width).transpose(1, 0, 2)
    late = jnp.concatenate([pair_sums.reshape(planes, -1, 2 * DH), late], 1)
    second_out_sliced, (pair_grad, far_sums) = rows_out(
        second_out[None], seqs_here, (heads_back(pair_grad_heads), swap(far_sums, "tp", 2))
    )
    grad_mine, grad_other = dot(pair_grad, pair_mine, NT), dot(pair_grad, pair_other, NT)
    normed_grad = jnp.concatenate(
        [
            jnp.where(shard == 0, grad_mine, grad_other),
            jnp.where(shard == 0, grad_other, grad_mine),
        ],
        1,
    )
    attn_back, attn_gain_grad, attn_shift_grad = row_norm_back(
        normed_grad, attn_scaled, attn_inverse, attention_gain
    )
    second_grad = (second_grad_rows.astype(f32) + attn_back).astype(bf16)

    early_own = (near_sums.astype(f32) + far_sums.astype(f32)).astype(bf16)
    early_own = early_own[: split // quarters]
    second_grad_sliced, (early_pieces, late_pieces) = rows_out(
        second_grad[None],
        seqs_here,
        (
            [swap(early_own, "ctx", j) for j in range(1, quarters)],
            [swap(plane_part(late, k), "tp", k) for k in range(1, planes)],
        ),
    )
    early_own = pack_rows([early_own] + early_pieces, ctx).astype(f32)
    expand_own, shrink_own = early_own[:, :units], early_own[:, units:].T
    late = plane_part(late, 0).astype(f32)
    late = sum((piece.astype(f32) for piece in late_pieces), late).astype(bf16)

    split_at = width
    turned = lax.ppermute(
        late[:split_at],
        ("ctx", "tp"),
        [(at * planes + to, to * planes + at) for at in range(quarters) for to in range(planes)],
    )
    late_own = collect_ctx(jnp.concatenate([turned, late[split_at:]], 0)[None])
    pair_head = late_own[:, :split_at].reshape(-1, width)
    late_own = late_own[:, split_at:].astype(f32)
    output_own = late_own[:, : split // quarters].reshape(split, width).T
    owned = late_own[:, split // quarters :].reshape(quarters, -1)[:, :vector_width].reshape(-1)
    row_own = owned[units:].reshape(3, width)
    near = lax.dynamic_slice_in_dim(pair_head, shard * split, split, 0)
    other = swap(lax.dynamic_slice_in_dim(pair_head, (1 - shard) * split, split, 0), "shard", 1)
    pair_own = by_half(near, other).astype(f32)
    query_own = jnp.concatenate([pair_own[0, :, :DH], pair_own[1, :, :DH]], 1)
    value_own = jnp.concatenate([pair_own[0, :, DH:], pair_own[1, :, DH:]], 1)

    norm_grads = jnp.concatenate(
        [attn_gain_grad.reshape(planes, width), attn_shift_grad.reshape(planes, width)], 1
    )
    norm_own = sum_everywhere(after(norm_grads, second_grad_sliced))
    norm_own = norm_own.reshape(2, width)
    return (
        outs_sliced[0],
        second_out_sliced[0],
        outs_sliced[1],
        second_grad_sliced[0],
        query_own,
        value_own,
        output_own,
        expand_own,
        owned[:units],
        shrink_own,
        row_own[0],
        norm_own[0],
        norm_own[1],
        row_own[1],
        row_own[2],
    )


def row_planes(mesh):
    sizes = mesh.shape
    return sizes["tp"] == SEQS and sizes["shard"] == 2 and sizes["ctx"] == 4 and HEADS == 8


def solution(mesh):
    return jax.shard_map(
        row_device if row_planes(mesh) else general_device,
        mesh=mesh,
        in_specs=(
            P("ctx", "shard", "tp"),
            P("ctx", "shard", "tp"),
            P("ctx", "shard", "tp"),
            P("ctx", "shard", "tp"),
            P("shard", "ctx"),
            P("shard", None, "ctx"),
            P("shard", "ctx"),
            P("shard", "tp"),
            P("shard", "tp"),
            P("tp", "shard"),
            P("shard", "tp"),
            P("tp"),
            P("tp", "shard"),
            P("tp"),
            P(),
            P(),
            P(),
            P(),
        ),
        out_specs=(
            P("ctx", "shard", "tp"),
            P("ctx", "shard", "tp"),
            P("ctx", "shard", "tp"),
            P("ctx", "shard", "tp"),
            P("shard", "tp"),
            P("shard", "tp"),
            P("tp", "shard"),
            P("shard", "tp"),
            P("tp"),
            P("tp", "shard"),
            P("tp"),
            P("tp"),
            P("tp"),
            P("tp"),
            P("tp"),
        ),
        check_vma=False,
    )
```

```python
import jax
import jax.numpy as jnp
from jax import lax
from jax.experimental import pallas as pl
from jax.experimental.layout import Layout, with_layout_constraint
from jax.experimental.pallas import tpu as pltpu
from jax.sharding import PartitionSpec as P

D = 1024
DH = 128
ROUNDS = 4


SELF_SCORE = -10.0
NEG_FILL = -1e30
BLOCK_ROWS = 512


BUCKETS = 64
HEADS = 8
SEQS = 4
TILE = 512
GROUP = 1
BOUND = 38.0
NT = (((1,), (1,)), ((), ()))
NN = (((1,), (0,)), ((), ()))


def dot(left, right, dims):
    return lax.dot_general(left, right, dims, preferred_element_type=jnp.float32)


def start_of(place, bounds_ref):
    start = jnp.where(place >= bounds_ref[0], bounds_ref[0], 0)
    start = jnp.where(place >= bounds_ref[1], bounds_ref[1], start)
    return jnp.where(place >= bounds_ref[2], bounds_ref[2], start)


def tile_masks(begin_row, bounds_ref):
    query_lane = lax.broadcasted_iota(jnp.int32, (1, TILE), 1)
    doc_start = start_of(query_lane + begin_row, bounds_ref)
    first = start_of(begin_row, bounds_ref) // TILE
    last_start = start_of(begin_row + TILE - 1, bounds_ref)
    full = jnp.minimum((last_start + TILE - 1) // TILE, begin_row // TILE)
    return doc_start, first, full


def rows_at(ref, block, tiles=1):
    return ref[pl.ds(pl.multiple_of(block * TILE, TILE), tiles * TILE), :]


def norm_factor(q):
    return lax.rsqrt(jnp.mean(q * q, -1, keepdims=True) + 1e-06)


def attend_kernel(bounds_ref, q_ref, v_ref, hot_ref, out_ref, log_ref, key_sc, vt_sc):
    block = pl.program_id(0)
    blocks = pl.num_programs(0)

    @pl.when(block == 0)
    def _():
        def prep(at, carry):
            q = rows_at(q_ref, at).astype(jnp.float32)
            begin = pl.multiple_of(at * TILE, TILE)
            key_sc[pl.ds(begin, TILE), :] = (q * (norm_factor(q) * DH ** (-0.5))).astype(jnp.bfloat16)
            v = rows_at(v_ref, at).astype(jnp.float32)
            vt_sc[:, pl.ds(begin, TILE)] = v.T.astype(jnp.bfloat16)
            return carry

        lax.fori_loop(0, blocks, prep, 0)

    begin_row = block * TILE
    doc_start, first, full = tile_masks(begin_row, bounds_ref)
    q = rows_at(q_ref, block)
    hot = rows_at(hot_ref, block)
    key_row = lax.broadcasted_iota(jnp.int32, (TILE, 1), 0)
    lane = lax.broadcasted_iota(jnp.int32, (1, TILE), 1)

    def scores(at, tiles):
        return dot(rows_at(key_sc, at, tiles), q, NT), dot(rows_at(hot_ref, at, tiles), hot, NT)

    def vt(at, tiles):
        return vt_sc[:, pl.ds(pl.multiple_of(at * TILE, TILE), tiles * TILE)]

    itself = key_row == lane

    def diagonal():
        s, c = scores(block, 1)
        c = jnp.where((key_row < lane) & (key_row + begin_row >= doc_start), c, 0.0)
        return jnp.where(itself, SELF_SCORE, s), jnp.where(itself, float(ROUNDS), c)

    def in_document(c, at):
        return jnp.where(key_row + at * TILE >= doc_start, c, 0.0)

    def mixed(at, tiles, p):
        return dot(vt(at, tiles), p.astype(jnp.bfloat16), NN)

    @pl.when(bounds_ref[3] == 1)
    def _():
        def fold(at, tiles, carry, masked):
            total, acc = carry
            s, c = scores(at, tiles)
            if masked:
                c = in_document(c, at)
            p = c * jnp.exp(s)
            return total + jnp.sum(p, 0, keepdims=True), acc + mixed(at, tiles, p)

        s, c = diagonal()
        p = c * jnp.exp(s)
        carry = jnp.sum(p, 0, keepdims=True), mixed(block, 1, p)
        carry = lax.fori_loop(first, full, lambda at, x: fold(at, 1, x, True), carry)
        rest = (block - full) % GROUP
        carry = lax.fori_loop(full, full + rest, lambda at, x: fold(at, 1, x, False), carry)
        total, acc = lax.fori_loop(
            0,
            (block - full) // GROUP,
            lambda at, x: fold(full + rest + GROUP * at, GROUP, x, False),
            carry,
        )
        out_ref[...] = acc / total
        log_ref[pl.ds(block, 1), :] = jnp.log(total)

    @pl.when(bounds_ref[3] == 0)
    def _():
        def fold(at, carry):
            high, total, acc = carry
            s, c = scores(at, 1)
            c = in_document(c, at)
            s = jnp.where(c > 0, s, NEG_FILL)
            new_high = jnp.maximum(high, jnp.max(s, 0, keepdims=True))
            fade = jnp.exp(high - new_high)
            p = c * jnp.exp(s - new_high)
            total = total * fade + jnp.sum(p, 0, keepdims=True)
            return new_high, total, acc * fade + mixed(at, 1, p)

        s, c = diagonal()
        s = jnp.where(c > 0, s, NEG_FILL)
        high = jnp.max(s, 0, keepdims=True)
        p = c * jnp.exp(s - high)
        carry = high, jnp.sum(p, 0, keepdims=True), mixed(block, 1, p)
        high, total, acc = lax.fori_loop(first, block, fold, carry)
        out_ref[...] = acc / total
        log_ref[pl.ds(block, 1), :] = high + jnp.log(total)


def attend(bounds, q, v, hot):
    rows = q.shape[0]
    blocks = rows // TILE
    whole = lambda shape: pl.BlockSpec(shape, lambda i, *_: (0,) * len(shape))
    return pl.pallas_call(
        attend_kernel,
        name="attend",
        out_shape=(
            jax.ShapeDtypeStruct((DH, rows), jnp.float32),
            jax.ShapeDtypeStruct((blocks, TILE), jnp.float32),
        ),
        grid_spec=pltpu.PrefetchScalarGridSpec(
            num_scalar_prefetch=1,
            grid=(blocks,),
            in_specs=[whole((rows, DH)), whole((rows, DH)), whole((rows, ROUNDS * BUCKETS))],
            out_specs=[pl.BlockSpec((DH, TILE), lambda i, *_: (0, i)), whole((blocks, TILE))],
            scratch_shapes=[pltpu.VMEM((rows, DH), jnp.bfloat16), pltpu.VMEM((DH, rows), jnp.bfloat16)],
        ),
        compiler_params=pltpu.CompilerParams(
            dimension_semantics=("arbitrary",), vmem_limit_bytes=40 * 2**20
        ),
        cost_estimate=pl.CostEstimate(
            flops=rows * DH, bytes_accessed=rows * DH, transcendentals=0
        ),
    )(bounds, q, v, hot)


def attend_back_kernel(
    bounds_ref, q_ref, v_ref, hot_ref, grad_ref, out_ref, log_ref,
    q_grad_ref, v_grad_ref, key_sc, kt_sc, dk_sc, dv_sc, dq_sc,
):
    block = pl.program_id(0)
    blocks = pl.num_programs(0)

    @pl.when(block == 0)
    def _():
        def prep(at, carry):
            begin = pl.multiple_of(at * TILE, TILE)
            q = rows_at(q_ref, at).astype(jnp.float32)
            k = q * (norm_factor(q) * DH ** (-0.5))
            key_sc[pl.ds(begin, TILE), :] = k.astype(jnp.bfloat16)
            kt_sc[:, pl.ds(begin, TILE)] = k.T.astype(jnp.bfloat16)
            dk_sc[pl.ds(begin, TILE), :] = jnp.zeros((TILE, DH), jnp.float32)
            dv_sc[pl.ds(begin, TILE), :] = jnp.zeros((TILE, DH), jnp.float32)
            return carry

        lax.fori_loop(0, blocks, prep, 0)

    begin_row = block * TILE
    doc_start, first, full = tile_masks(begin_row, bounds_ref)
    q = rows_at(q_ref, block)
    hot = rows_at(hot_ref, block)
    grad = rows_at(grad_ref, block)
    log_row = log_ref[pl.ds(block, 1), :]
    delta = jnp.sum(grad.astype(jnp.float32).T * out_ref[...], 0, keepdims=True)
    key_row = lax.broadcasted_iota(jnp.int32, (TILE, 1), 0)
    lane = lax.broadcasted_iota(jnp.int32, (1, TILE), 1)

    itself = key_row == lane

    def fold(at, tiles, acc, masked, bounded, diagonal=False):
        rows = pl.ds(pl.multiple_of(at * TILE, TILE), tiles * TILE)
        s = dot(key_sc[rows, :], q, NT)
        c = dot(hot_ref[rows, :], hot, NT)
        up = dot(v_ref[rows, :], grad, NT)
        if diagonal:
            c = jnp.where((key_row < lane) & (key_row + begin_row >= doc_start), c, 0.0)
            c = jnp.where(itself, float(ROUNDS), c)
            s = jnp.where(itself, SELF_SCORE, s)
        elif masked:
            c = jnp.where(key_row + at * TILE >= doc_start, c, 0.0)
        if not bounded:
            s = jnp.where(c > 0, s, NEG_FILL)
        w = c * jnp.exp(s - log_row)
        ds = w * (up - delta)
        if diagonal:
            ds = jnp.where(itself, 0.0, ds)
        w = w.astype(jnp.bfloat16)
        ds = ds.astype(jnp.bfloat16)
        dv_sc[rows, :] += dot(w, grad, NN)
        dk_sc[rows, :] += dot(ds, q, NN)
        return acc + dot(kt_sc[:, rows], ds, NN)

    def store(acc):
        dq_sc[pl.ds(pl.multiple_of(begin_row, TILE), TILE), :] = acc.T

    nothing = jnp.zeros((DH, TILE), jnp.float32)

    @pl.when(bounds_ref[3] == 1)
    def _():
        acc = fold(block, 1, nothing, True, True, True)
        acc = lax.fori_loop(first, full, lambda at, x: fold(at, 1, x, True, True), acc)
        rest = (block - full) % GROUP
        acc = lax.fori_loop(full, full + rest, lambda at, x: fold(at, 1, x, False, True), acc)
        store(
            lax.fori_loop(
                0,
                (block - full) // GROUP,
                lambda at, x: fold(full + rest + GROUP * at, GROUP, x, False, True),
                acc,
            )
        )

    @pl.when(bounds_ref[3] == 0)
    def _():
        acc = fold(block, 1, nothing, True, False, True)
        store(lax.fori_loop(first, block, lambda at, x: fold(at, 1, x, True, False), acc))

    @pl.when(block == blocks - 1)
    def _():
        def finish(at, carry):
            begin = pl.multiple_of(at * TILE, TILE)
            q = rows_at(q_ref, at).astype(jnp.float32)
            r = norm_factor(q)
            g = rows_at(dk_sc, at).astype(jnp.bfloat16).astype(jnp.float32)
            back = (r * DH ** (-0.5)) * (g - q * (r * r * jnp.mean(q * g, -1, keepdims=True)))
            q_grad_ref[pl.ds(begin, TILE), :] = (rows_at(dq_sc, at) + back).astype(jnp.bfloat16)
            v_grad_ref[pl.ds(begin, TILE), :] = rows_at(dv_sc, at).astype(jnp.bfloat16)
            return carry

        lax.fori_loop(0, blocks, finish, 0)


def attend_back(bounds, q, v, hot, grad, out, logs):
    rows = q.shape[0]
    blocks = rows // TILE
    whole = lambda shape: pl.BlockSpec(shape, lambda i, *_: (0,) * len(shape))
    return pl.pallas_call(
        attend_back_kernel,
        name="attend_back",
        out_shape=(jax.ShapeDtypeStruct((rows, DH), jnp.bfloat16),) * 2,
        grid_spec=pltpu.PrefetchScalarGridSpec(
            num_scalar_prefetch=1,
            grid=(blocks,),
            in_specs=[
                whole((rows, DH)), whole((rows, DH)), whole((rows, ROUNDS * BUCKETS)), whole((rows, DH)),
                pl.BlockSpec((DH, TILE), lambda i, *_: (0, i)), whole((blocks, TILE)),
            ],
            out_specs=[whole((rows, DH))] * 2,
            scratch_shapes=[
                pltpu.VMEM((rows, DH), jnp.bfloat16),
                pltpu.VMEM((DH, rows), jnp.bfloat16),
                pltpu.VMEM((rows, DH), jnp.float32),
                pltpu.VMEM((rows, DH), jnp.float32),
                pltpu.VMEM((rows, DH), jnp.float32),
            ],
        ),
        compiler_params=pltpu.CompilerParams(
            dimension_semantics=("arbitrary",), vmem_limit_bytes=48 * 2**20
        ),
        cost_estimate=pl.CostEstimate(
            flops=rows * DH, bytes_accessed=rows * DH, transcendentals=0
        ),
    )(bounds, q, v, hot, grad, out, logs)


def place_matrix(places):
    rows = places.shape[0]
    return (jnp.arange(rows, dtype=jnp.int32)[:, None] == places[None, :]).astype(jnp.bfloat16)


def into_places(places, vectors):
    return jnp.einsum("pa,ad->pd", place_matrix(places), vectors, preferred_element_type=jnp.float32).astype(jnp.bfloat16)


def out_of_places(places, vectors):
    rows = places.shape[0]
    picks = (places[:, None] == jnp.arange(rows, dtype=jnp.int32)[None, :]).astype(jnp.bfloat16)
    return dot(picks, vectors, NN).astype(jnp.bfloat16)


def bucket_hot(buckets):
    hot = buckets.T[:, :, None] == jnp.arange(BUCKETS, dtype=jnp.int32)
    return hot.astype(jnp.bfloat16).reshape(buckets.shape[1], ROUNDS * BUCKETS)


def doc_bounds(segments):
    return jnp.sum((segments[None, :] < jnp.arange(1, 4, dtype=jnp.int32)[:, None]).astype(jnp.int32), 1)


def with_bound(bounds, queries):
    squares = jnp.sum(queries.astype(jnp.float32) ** 2, -1)
    return jnp.concatenate([bounds, (jnp.max(squares) <= BOUND**2).astype(jnp.int32)[None]])


def smooth_unit(values_in):
    return jax.nn.gelu(values_in, approximate=False)


def norm_rows(rows_wide, gain_row, shift_row):
    centre = jnp.mean(rows_wide, -1, keepdims=True)
    offset = rows_wide - centre
    inverse = lax.rsqrt(jnp.mean(offset * offset, -1, keepdims=True) + 1e-05)
    scaled = offset * inverse
    return (scaled * gain_row + shift_row, scaled, inverse)


def unit_keys(queries):
    shaped = queries.reshape(queries.shape[:-1] + (queries.shape[-1] // DH, DH))
    factor = lax.rsqrt(jnp.mean(shaped * shaped, -1, keepdims=True) + 1e-06) * DH ** (-0.5)
    return (shaped * factor).reshape(queries.shape)


def heads_view(vectors):
    return vectors.reshape(vectors.shape[0], vectors.shape[1], vectors.shape[2] // DH, DH)


def full_rows(sliced):
    return lax.all_gather(sliced, "tp", axis=2, tiled=True)


def branch_sum(partial_value):
    return lax.psum_scatter(partial_value, "tp", scatter_dimension=2, tiled=True)


def norm_back(grad_slice, scaled_slice, inverse, gain_slice):
    weighted = grad_slice * gain_slice
    first_sum, second_sum = lax.psum(
        (jnp.sum(weighted, -1, keepdims=True), jnp.sum(weighted * scaled_slice, -1, keepdims=True)),
        "tp",
    )
    inner = inverse * (weighted - first_sum / D - scaled_slice * (second_sum / D))
    return (inner, jnp.sum(grad_slice * scaled_slice, (0, 1)), jnp.sum(grad_slice, (0, 1)))


def label_rows(all_labels, begin_row, extent):
    all_segments, all_buckets, all_positions = all_labels
    return (
        lax.dynamic_slice_in_dim(all_segments, begin_row, extent, 1),
        lax.dynamic_slice_in_dim(all_buckets, begin_row, extent, 2),
        lax.dynamic_slice_in_dim(all_positions, begin_row, extent, 1),
    )


def block_weights(query_heads, query_labels, key_heads, key_labels):
    query_seg, query_buck, query_pos = query_labels
    key_seg, key_buck, key_pos = key_labels
    scores = jnp.einsum(
        "pshd,kshd->shpk", query_heads, key_heads, preferred_element_type=jnp.float32
    )
    matches = jnp.sum((query_buck[:, :, :, None] == key_buck[:, :, None, :]).astype(jnp.int32), 1)
    same_doc = query_seg[:, :, None] == key_seg[:, None, :]
    earlier = key_pos[:, None, :] < query_pos[:, :, None]
    itself = key_pos[:, None, :] == query_pos[:, :, None]
    counts = jnp.where(itself, ROUNDS, jnp.where(earlier & same_doc, matches, 0)).astype(
        jnp.float32
    )[:, None]
    shifted = jnp.where(itself[:, None], SELF_SCORE, scores)
    return (shifted, counts, itself[:, None])


def weights_of(shifted, counts, log_total):
    return jnp.where(counts > 0, counts * jnp.exp(shifted - log_total[..., None]), 0.0)


def blockwise(advance, running, row_count):
    extent = BLOCK_ROWS

    def turn(state_now, block_index):
        return (advance(state_now, block_index * extent, extent), None)

    return lax.scan(turn, running, jnp.arange(row_count // extent, dtype=jnp.int32))[0]


def over_keys(key_vectors, value_vectors, folder, initial):
    return folder(
        initial,
        (
            lax.all_gather(key_vectors, "ctx", axis=0, tiled=True),
            lax.all_gather(value_vectors, "ctx", axis=0, tiled=True),
        ),
        jnp.int32(0),
    )


def over_context(first_part, second_part, third_part, fourth_part, fifth_part):
    return (
        lax.psum(first_part.astype(jnp.bfloat16), "ctx").astype(jnp.float32),
        lax.psum(second_part.astype(jnp.bfloat16), "ctx").astype(jnp.float32),
        lax.psum(third_part.astype(jnp.bfloat16), "ctx").astype(jnp.float32),
        lax.psum(fourth_part.astype(jnp.bfloat16), "ctx").astype(jnp.float32),
        lax.psum(fifth_part.astype(jnp.bfloat16), "ctx").astype(jnp.float32),
    )


def to_row_owners(first_part, second_part, third_part):
    return (
        lax.psum_scatter(
            first_part.astype(jnp.bfloat16), "shard", scatter_dimension=0, tiled=True
        ).astype(jnp.float32),
        lax.psum_scatter(
            second_part.astype(jnp.bfloat16), "shard", scatter_dimension=0, tiled=True
        ).astype(jnp.float32),
        lax.psum_scatter(
            third_part.astype(jnp.bfloat16), "shard", scatter_dimension=0, tiled=True
        ).astype(jnp.float32),
    )


def to_col_owners(first_part, second_part):
    return (
        lax.psum_scatter(
            first_part.astype(jnp.bfloat16), "shard", scatter_dimension=1, tiled=True
        ).astype(jnp.float32),
        lax.psum_scatter(
            second_part.astype(jnp.bfloat16), "shard", scatter_dimension=1, tiled=True
        ).astype(jnp.float32),
    )


def general_device(
    first_half,
    second_half,
    first_cotangent,
    second_cotangent,
    segment_ids,
    bucket_ids,
    positions,
    query_weight,
    value_weight,
    output_weight,
    expand_weight,
    expand_bias,
    shrink_weight,
    shrink_bias,
    attention_gain,
    attention_shift,
    forward_gain,
    forward_shift,
):
    rows_here, seqs_here, slice_width = first_half.shape
    width_heads = query_weight.shape[1]
    heads_here = width_heads // DH
    tp_start = lax.axis_index("tp") * slice_width
    ctx_start = lax.axis_index("ctx") * rows_here
    bf16 = jnp.bfloat16
    f32 = jnp.float32

    def columns(wide):
        return lax.dynamic_slice_in_dim(wide, tp_start, slice_width, wide.ndim - 1)

    full_query, full_value, full_expand = (
        lax.all_gather(query_weight, "shard", axis=0, tiled=True),
        lax.all_gather(value_weight, "shard", axis=0, tiled=True),
        lax.all_gather(expand_weight, "shard", axis=0, tiled=True),
    )
    full_output, full_shrink = (
        lax.all_gather(output_weight, "shard", axis=1, tiled=True),
        lax.all_gather(shrink_weight, "shard", axis=1, tiled=True),
    )
    all_labels = (
        lax.all_gather(segment_ids, "ctx", axis=1, tiled=True),
        lax.all_gather(bucket_ids, "ctx", axis=2, tiled=True),
        lax.all_gather(positions, "ctx", axis=1, tiled=True),
    )
    local_labels = label_rows(all_labels, ctx_start, rows_here)
    second_wide = full_rows(second_half)
    normed, attn_scaled, attn_inverse = norm_rows(
        second_wide.astype(f32), attention_gain, attention_shift
    )
    normed = normed.astype(bf16)
    queries = jnp.einsum("psd,de->pse", normed, full_query, preferred_element_type=f32).astype(bf16)
    key_vectors = unit_keys(queries.astype(f32)).astype(bf16)
    value_vectors = jnp.einsum(
        "psd,de->pse", normed, full_value, preferred_element_type=f32
    ).astype(bf16)
    query_heads = heads_view(queries)
    stat_shape = (seqs_here, heads_here, rows_here)
    head_zero = jnp.zeros((rows_here, seqs_here, heads_here, DH), f32)

    def norm_fold(running, pieces, begin_row):
        key_piece = pieces[0]

        def advance(state_now, offset, extent):
            highest, summed = state_now
            key_heads = heads_view(lax.dynamic_slice_in_dim(key_piece, offset, extent, 0))
            shifted, counts, _ = block_weights(
                query_heads, local_labels, key_heads, label_rows(all_labels, offset, extent)
            )
            usable = counts > 0
            new_high = jnp.maximum(highest, jnp.max(jnp.where(usable, shifted, NEG_FILL), -1))
            summed = summed * jnp.exp(highest - new_high) + jnp.sum(
                jnp.where(usable, counts * jnp.exp(shifted - new_high[..., None]), 0.0), -1
            )
            return (new_high, summed)

        return blockwise(advance, running, key_piece.shape[0])

    highest, summed = over_keys(
        key_vectors,
        value_vectors,
        norm_fold,
        (jnp.full(stat_shape, NEG_FILL, f32), jnp.zeros(stat_shape, f32)),
    )
    log_total = highest + jnp.log(summed)

    def key_block(pieces, offset, extent):
        key_heads = heads_view(lax.dynamic_slice_in_dim(pieces[0], offset, extent, 0))
        value_heads = heads_view(lax.dynamic_slice_in_dim(pieces[1], offset, extent, 0))
        shifted, counts, itself = block_weights(
            query_heads, local_labels, key_heads, label_rows(all_labels, offset, extent)
        )
        return (key_heads, value_heads, weights_of(shifted, counts, log_total), itself)

    def mix_fold(running, pieces, begin_row):

        def advance(state_now, offset, extent):
            key_heads, value_heads, weights, itself = key_block(pieces, offset, extent)
            return state_now + jnp.einsum(
                "shpk,kshd->pshd", weights.astype(bf16), value_heads, preferred_element_type=f32
            )

        return blockwise(advance, running, pieces[0].shape[0])

    head_mix = over_keys(key_vectors, value_vectors, mix_fold, head_zero)
    attention = head_mix.reshape(rows_here, seqs_here, width_heads).astype(bf16)
    branch = branch_sum(
        jnp.einsum("pse,ed->psd", attention, full_output, preferred_element_type=f32)
    )
    first_out = (first_half.astype(f32) + branch).astype(bf16)
    first_wide = full_rows(first_out)
    ffn_in, ffn_scaled, ffn_inverse = norm_rows(first_wide.astype(f32), forward_gain, forward_shift)
    ffn_in = ffn_in.astype(bf16)
    pre_act = (
        jnp.einsum("psd,df->psf", ffn_in, full_expand, preferred_element_type=f32) + expand_bias
    )
    hidden_exact, unit_pull = jax.vjp(smooth_unit, pre_act)
    hidden = hidden_exact.astype(bf16)
    second_branch = (
        branch_sum(jnp.einsum("psf,fd->psd", hidden, full_shrink, preferred_element_type=f32))
        + shrink_bias
    )
    second_out = (second_half.astype(f32) + second_branch).astype(bf16)
    cotangent_wide = full_rows(second_cotangent)
    hidden_grad = jnp.einsum("psd,fd->psf", cotangent_wide, full_shrink, preferred_element_type=f32)
    pre_grad = unit_pull(hidden_grad)[0].astype(bf16)
    shrink_grad = jnp.einsum("psf,psd->fd", hidden, cotangent_wide, preferred_element_type=f32)
    shrink_bias_grad = jnp.sum(second_cotangent.astype(f32), (0, 1))
    expand_grad = jnp.einsum("psd,psf->df", ffn_in, pre_grad, preferred_element_type=f32)
    expand_bias_grad = jnp.sum(pre_grad.astype(f32), (0, 1))
    ffn_grad = branch_sum(
        jnp.einsum("psf,df->psd", pre_grad, full_expand, preferred_element_type=f32)
    )
    ffn_back, forward_gain_grad, forward_shift_grad = norm_back(
        ffn_grad, columns(ffn_scaled), ffn_inverse, columns(forward_gain)
    )
    first_grad = (first_cotangent.astype(f32) + ffn_back).astype(bf16)
    grad_wide = full_rows(first_grad)
    output_grad = jnp.einsum("pse,psd->ed", attention, grad_wide, preferred_element_type=f32)
    attention_grad = jnp.einsum(
        "psd,ed->pse", grad_wide, full_output, preferred_element_type=f32
    ).astype(bf16)
    grad_heads = heads_view(attention_grad)

    def delta_fold(running, pieces, begin_row):

        def advance(state_now, offset, extent):
            key_heads, value_heads, weights, itself = key_block(pieces, offset, extent)
            upstream = jnp.einsum(
                "pshd,kshd->shpk", grad_heads, value_heads, preferred_element_type=f32
            )
            return state_now + jnp.sum(weights * upstream, -1)

        return blockwise(advance, running, pieces[0].shape[0])

    row_delta = over_keys(key_vectors, value_vectors, delta_fold, jnp.zeros(stat_shape, f32))

    def query_fold(running, pieces, begin_row):

        def advance(state_now, offset, extent):
            key_heads, value_heads, weights, itself = key_block(pieces, offset, extent)
            upstream = jnp.einsum(
                "pshd,kshd->shpk", grad_heads, value_heads, preferred_element_type=f32
            )
            score_grad = jnp.where(itself, 0.0, weights * (upstream - row_delta[..., None])).astype(
                bf16
            )
            return state_now + jnp.einsum(
                "shpk,kshd->pshd", score_grad, key_heads, preferred_element_type=f32
            )

        return blockwise(advance, running, pieces[0].shape[0])

    query_part = over_keys(key_vectors, value_vectors, query_fold, head_zero)
    query_lse, query_delta = (
        lax.all_gather(log_total, "ctx", axis=2, tiled=True),
        lax.all_gather(row_delta, "ctx", axis=2, tiled=True),
    )
    local_keys = heads_view(key_vectors)
    local_values = heads_view(value_vectors)
    query_piece = lax.all_gather(queries, "ctx", axis=0, tiled=True)
    grad_piece = lax.all_gather(attention_grad, "ctx", axis=0, tiled=True)

    def advance(state_now, offset, extent):
        remote_queries = heads_view(lax.dynamic_slice_in_dim(query_piece, offset, extent, 0))
        remote_grads = heads_view(lax.dynamic_slice_in_dim(grad_piece, offset, extent, 0))
        lse_rows = lax.dynamic_slice_in_dim(query_lse, offset, extent, 2)
        delta_rows = lax.dynamic_slice_in_dim(query_delta, offset, extent, 2)
        shifted, counts, itself = block_weights(
            remote_queries, label_rows(all_labels, offset, extent), local_keys, local_labels
        )
        weights = weights_of(shifted, counts, lse_rows)
        upstream = jnp.einsum(
            "pshd,kshd->shpk", remote_grads, local_values, preferred_element_type=f32
        )
        score_grad = jnp.where(itself, 0.0, weights * (upstream - delta_rows[..., None])).astype(
            bf16
        )
        key_now = state_now[0] + jnp.einsum(
            "shpk,pshd->kshd", score_grad, remote_queries, preferred_element_type=f32
        )
        value_now = state_now[1] + jnp.einsum(
            "shpk,pshd->kshd", weights.astype(bf16), remote_grads, preferred_element_type=f32
        )
        return (key_now, value_now)

    key_part, value_part = blockwise(advance, (head_zero, head_zero), query_piece.shape[0])
    keys_grad = key_part.reshape(rows_here, seqs_here, width_heads).astype(bf16)
    values_grad = value_part.reshape(rows_here, seqs_here, width_heads).astype(bf16)
    unit_back = jax.vjp(unit_keys, queries.astype(f32))[1]
    queries_total = (
        query_part.reshape(rows_here, seqs_here, width_heads) + unit_back(keys_grad.astype(f32))[0]
    ).astype(bf16)
    query_grad = jnp.einsum("psd,pse->de", normed, queries_total, preferred_element_type=f32)
    value_grad = jnp.einsum("psd,pse->de", normed, values_grad, preferred_element_type=f32)
    normed_grad = branch_sum(
        jnp.einsum("pse,de->psd", queries_total, full_query, preferred_element_type=f32)
        + jnp.einsum("pse,de->psd", values_grad, full_value, preferred_element_type=f32)
    )
    attn_back, attention_gain_grad, attention_shift_grad = norm_back(
        normed_grad, columns(attn_scaled), attn_inverse, columns(attention_gain)
    )
    second_grad = (second_cotangent.astype(f32) + attn_back).astype(bf16)
    expand_bias_sum, shrink_bias_sum, attn_gain_sum, attn_shift_sum, ffn_gain_sum, ffn_shift_sum = (
        lax.psum(
            (
                expand_bias_grad,
                shrink_bias_grad,
                attention_gain_grad,
                attention_shift_grad,
                forward_gain_grad,
                forward_shift_grad,
            ),
            ("shard", "ctx"),
        )
    )
    query_sum, value_sum, expand_sum, output_sum, shrink_sum = over_context(
        query_grad, value_grad, expand_grad, output_grad, shrink_grad
    )
    query_own, value_own, expand_own = to_row_owners(query_sum, value_sum, expand_sum)
    output_own, shrink_own = to_col_owners(output_sum, shrink_sum)
    return (
        first_out,
        second_out,
        first_grad,
        second_grad,
        query_own,
        value_own,
        output_own,
        expand_own,
        expand_bias_sum,
        shrink_own,
        shrink_bias_sum,
        attn_gain_sum,
        attn_shift_sum,
        ffn_gain_sum,
        ffn_shift_sum,
    )


def swap(vectors, axis, bits):
    size = lax.axis_size(axis)
    return lax.ppermute(vectors, axis, [(at, at ^ bits) for at in range(size)])


def where_am_i():
    return lax.axis_index("shard"), lax.axis_index("ctx"), lax.axis_index("tp")


def plane_pairs(step, inverse):
    shards, planes = lax.axis_size("shard"), lax.axis_size("tp")
    local_seqs = planes // shards
    pairs = []
    for shard in range(shards):
        for plane in range(planes):
            chunk = step ^ plane
            there = (chunk % shards) * planes + shard * local_seqs + chunk // shards
            here = shard * planes + plane
            pairs.append((there, here) if inverse else (here, there))
    return pairs


def rows_in(sliced, beside=(), extra=None):
    shard, _, plane = where_am_i()
    shards, planes = lax.axis_size("shard"), lax.axis_size("tp")
    count, slots, seqs, width = sliced.shape
    extent = slots // shards
    by_seq = sliced.transpose(2, 0, 1, 3).reshape(seqs, count, shards, extent, width)
    by_seq = by_seq.transpose(0, 2, 1, 3, 4).reshape(seqs * shards, count * extent, width)
    if extra is not None:
        by_seq = jnp.concatenate([by_seq, jnp.concatenate([extra] * seqs, 0)], 1)
    mine = (plane % seqs) * shards + shard
    landed = []
    for step in range(planes):
        chunk = lax.dynamic_index_in_dim(by_seq, step ^ plane, 0, False)
        landed.append(lax.ppermute(chunk, ("shard", "tp"), plane_pairs(step, False)))
    landed, beside = lax.optimization_barrier((landed, beside))
    whole = jnp.zeros((count * extent, planes * width), sliced.dtype)
    for step in range(planes):
        piece = landed[step][: count * extent]
        whole = lax.dynamic_update_slice_in_dim(whole, piece, (step ^ mine) * width, 1)
    whole = whole.reshape(count, extent, planes * width)
    if extra is None:
        return whole, beside
    extras = jnp.zeros((planes,) + extra.shape[1:], extra.dtype)
    for step in range(planes):
        piece = landed[step][None, count * extent :]
        extras = lax.dynamic_update_slice_in_dim(extras, piece, step ^ mine, 0)
    return whole, beside, extras


def rows_out(whole, seqs, beside=(), first=None):
    shard, _, plane = where_am_i()
    shards, planes = lax.axis_size("shard"), lax.axis_size("tp")
    count, extent, features = whole.shape
    width = features // planes
    mine = (plane % seqs) * shards + shard
    flat = whole.reshape(count * extent, features)

    def send(step):
        piece = lax.dynamic_slice_in_dim(flat, (step ^ mine) * width, width, 1)
        return lax.ppermute(piece, ("shard", "tp"), plane_pairs(step, True))

    half = planes // 2 if first is not None else 0
    landed = [send(step) for step in range(half)]
    if first is not None:
        landed, beside, flat = lax.optimization_barrier((landed, beside, flat))
        beside = first(beside)
    rest = [send(step) for step in range(half, planes)]
    rest, beside = lax.optimization_barrier((rest, beside))
    landed = landed + rest
    by_seq = jnp.zeros((seqs * shards, count * extent, width), whole.dtype)
    for step in range(planes):
        by_seq = lax.dynamic_update_slice_in_dim(by_seq, landed[step][None], step ^ plane, 0)
    parts = by_seq.reshape(seqs, shards, count, extent, width).transpose(2, 1, 3, 0, 4)
    return parts.reshape(count, shards * extent, seqs, width), beside


def quarter_of(local, at):
    extent = local.shape[0] // lax.axis_size("ctx")
    return lax.dynamic_slice_in_dim(local, at * extent, extent, 0)


def by_half(own, other):
    first = lax.axis_index("shard") == 0
    return jnp.stack([jnp.where(first, own, other), jnp.where(first, other, own)])


def plain(vectors):
    return with_layout_constraint(vectors, Layout(major_to_minor=tuple(range(vectors.ndim))))


def core_parts(local):
    mine = quarter_of(local, lax.axis_index("ctx"))
    return by_half(mine, swap(mine, "shard", 1))


def split_bias(values):
    high = values.astype(jnp.bfloat16)
    rest = values - high.astype(jnp.float32)
    middle = rest.astype(jnp.bfloat16)
    return jnp.stack([high, middle, (rest - middle.astype(jnp.float32)).astype(jnp.bfloat16)])


def shard_half(wide, at):
    extent = wide.shape[1] // 2
    return lax.dynamic_slice_in_dim(wide, at * extent, extent, 1)


def chip_sums(rows_wide, columns_wide):
    shard = lax.axis_index("shard")

    def product(at):
        return lax.dot_general(
            shard_half(rows_wide, at),
            columns_wide,
            (((0,), (0,)), ((), ())),
            preferred_element_type=jnp.float32,
        )

    theirs = swap(product(1 - shard).astype(jnp.bfloat16), "shard", 1)
    return product(shard) + theirs.astype(jnp.float32)


def sum_parts(parts):
    return jnp.sum(parts.astype(jnp.float32), 0)


def send_ctx(sums):
    quarters = lax.axis_size("ctx")
    parts = sums.reshape(quarters, sums.shape[0] // quarters, sums.shape[1])
    return lax.all_to_all(parts, "ctx", 0, 0, tiled=True)


def scatter_ctx(sums):
    return sum_parts(send_ctx(sums))


def scatter_tp(sums):
    planes = lax.axis_size("tp")
    parts = sums.reshape(sums.shape[0], planes, -1).transpose(1, 0, 2)
    return sum_parts(lax.all_to_all(parts, "tp", 0, 0, tiled=True))


def collect_ctx(quarter):
    quarters = lax.axis_size("ctx")
    return in_order([quarter] + [swap(quarter, "ctx", j) for j in range(1, quarters)])


def in_order(pieces):
    ctx, extent = lax.axis_index("ctx"), pieces[0].shape[0]
    whole = jnp.zeros((len(pieces) * extent,) + pieces[0].shape[1:], pieces[0].dtype)
    for j, piece in enumerate(pieces):
        whole = lax.dynamic_update_slice_in_dim(whole, piece, (ctx ^ j) * extent, 0)
    return whole


def reduce_context_first(sums):
    bf16 = jnp.bfloat16
    quarter = scatter_ctx(sums.astype(bf16)).astype(bf16)
    return collect_ctx(scatter_tp(quarter).astype(bf16)).astype(jnp.float32)


def plane_part(parts, k):
    return lax.dynamic_index_in_dim(parts, lax.axis_index("tp") ^ k, 0, False)


def sum_in_plane(total):
    total = total + swap(total, "shard", 1)
    return sum(swap(total, "ctx", j) for j in range(1, lax.axis_size("ctx"))) + total


def after(values, ready):
    return lax.optimization_barrier((values, ready))[0]


def row_norm_back(grad, scaled, inverse, gain):
    weighted = grad * gain
    first = jnp.mean(weighted, -1, keepdims=True)
    second = jnp.mean(weighted * scaled, -1, keepdims=True)
    inner = inverse * (weighted - first - scaled * second)
    return inner, jnp.sum(grad * scaled, 0), jnp.sum(grad, 0)


def heads_out(vectors):
    heads = HEADS
    sent = vectors.reshape(vectors.shape[0], heads, -1).transpose(1, 0, 2)
    landed = lax.all_to_all(sent, ("ctx", "shard"), split_axis=0, concat_axis=0, tiled=True)
    return landed.reshape(-1, landed.shape[2])


def heads_back(vectors):
    sent = vectors.reshape(HEADS, -1, vectors.shape[1])
    landed = lax.all_to_all(sent, ("ctx", "shard"), split_axis=0, concat_axis=0, tiled=True)
    return landed.transpose(1, 0, 2).reshape(landed.shape[1], -1)


def plane_labels(segment_ids, bucket_ids, positions):
    shard, _, plane = where_am_i()
    seqs, slots = positions.shape
    packed = jnp.concatenate([positions[:, None], segment_ids[:, None], bucket_ids], 1)
    kinds = packed.shape[1]
    mine = lax.dynamic_index_in_dim(packed, plane % seqs, 0, False).reshape(-1, 128)
    mine = jnp.where(shard == plane // seqs, mine, swap(mine, "shard", 1))
    whole = collect_ctx(mine).reshape(-1, kinds, slots).transpose(1, 0, 2).reshape(kinds, -1)
    return whole[0], whole[1], whole[2:]


def pack_rows_kernel(code_ref, *refs):
    pieces, out_ref, sems = refs[:-2], refs[-2], refs[-1]
    extent = pieces[0].shape[0]
    copies = []
    for j, ref in enumerate(pieces):
        place = pl.multiple_of((code_ref[0] ^ j) * extent, extent)
        copies.append(pltpu.make_async_copy(ref, out_ref.at[pl.ds(place, extent), :], sems.at[j]))
        copies[-1].start()
    for copy in copies:
        copy.wait()


def pack_rows(pieces, code):
    extent, width = pieces[0].shape
    shape = (len(pieces) * extent, width)
    return pl.pallas_call(
        pack_rows_kernel,
        name="pack_rows",
        out_shape=jax.ShapeDtypeStruct(shape, pieces[0].dtype),
        grid_spec=pltpu.PrefetchScalarGridSpec(
            num_scalar_prefetch=1,
            grid=(1,),
            in_specs=[pl.BlockSpec(memory_space=pl.ANY)] * len(pieces),
            out_specs=pl.BlockSpec(shape, lambda i, *_: (0, 0)),
            scratch_shapes=[pltpu.SemaphoreType.DMA((len(pieces),))],
        ),
        compiler_params=pltpu.CompilerParams(vmem_limit_bytes=24 * 2**20),
        cost_estimate=pl.CostEstimate(flops=0, bytes_accessed=4 * len(pieces) * extent * width, transcendentals=0),
    )(jnp.reshape(code, (1,)).astype(jnp.int32), *pieces)


def pack_weights_kernel(code_ref, near_ref, far_ref, *refs):
    out_ref = refs[-1]
    units = near_ref.shape[1] // 2
    out_ref[:, :units] = near_ref[:, :units]
    out_ref[:, units : 2 * units] = far_ref[:, :units]
    out_ref[:, 2 * units : 3 * units] = near_ref[:, units:]
    out_ref[:, 3 * units : 4 * units] = far_ref[:, units:]
    width = refs[0].shape[1]
    for k, ref in enumerate(refs[:-1]):
        place = pl.multiple_of(4 * units + (code_ref[0] ^ k) * width, width)
        out_ref[:, pl.ds(place, width)] = ref[...]


def pack_weights(near, far, outs, code):
    extent, units = near.shape
    width = outs[0].shape[1]
    columns = 2 * units + len(outs) * width
    whole = lambda shape: pl.BlockSpec(shape, lambda i, *_: (0, 0))
    return pl.pallas_call(
        pack_weights_kernel,
        name="pack_weights",
        out_shape=jax.ShapeDtypeStruct((extent, columns), near.dtype),
        grid_spec=pltpu.PrefetchScalarGridSpec(
            num_scalar_prefetch=1,
            grid=(1,),
            in_specs=[whole((extent, units))] * 2 + [whole((extent, width)) for _ in outs],
            out_specs=whole((extent, columns)),
        ),
        compiler_params=pltpu.CompilerParams(vmem_limit_bytes=24 * 2**20),
        cost_estimate=pl.CostEstimate(flops=0, bytes_accessed=4 * extent * columns, transcendentals=0),
    )(jnp.reshape(code, (1,)).astype(jnp.int32), near, far, *outs)


def row_device(
    first_half,
    second_half,
    first_cotangent,
    second_cotangent,
    segment_ids,
    bucket_ids,
    positions,
    query_weight,
    value_weight,
    output_weight,
    expand_weight,
    expand_bias,
    shrink_weight,
    shrink_bias,
    attention_gain,
    attention_shift,
    forward_gain,
    forward_shift,
):
    bf16, f32 = jnp.bfloat16, jnp.float32
    planes = lax.axis_size("tp")
    shard, ctx, plane = where_am_i()
    seqs_here, width = first_half.shape[1:]
    units = expand_bias.shape[0]
    split = query_weight.shape[0]

    local_pair = jnp.stack(
        [query_weight.reshape(split, -1, DH), value_weight.reshape(split, -1, DH)], 2
    ).reshape(split, -1)
    pair_parts = core_parts(local_pair)
    pair_rows = pair_parts.shape[1] * pair_parts.shape[2] // width
    biases = split_bias(jnp.concatenate([expand_bias, shrink_bias])).reshape(-1, width)
    bias_rows = biases.shape[0]
    biases = jnp.pad(biases, ((0, -bias_rows % 16), (0, 0)))
    extra = jnp.concatenate(
        [pair_parts.reshape(-1, pair_rows, width), jnp.stack([biases] * pair_parts.shape[0])], 1
    )
    (second_rows,), _, extras = rows_in(second_half[None], (), extra)
    biases = extras[:, pair_rows : pair_rows + bias_rows].astype(f32).reshape(planes, 3, -1)
    biases = (biases[:, 0] + biases[:, 1]) + biases[:, 2]
    unit_bias = jnp.concatenate(
        [
            lax.dynamic_index_in_dim(biases, plane, 0, False)[:units],
            lax.dynamic_index_in_dim(biases, plane ^ 2, 0, False)[:units],
        ]
    )
    row_bias = biases[:, units:].reshape(-1)

    pair_wide = extras[:, :pair_rows].reshape((planes,) + pair_parts.shape[1:]).transpose(1, 0, 2)
    pair_wide = plain(pair_wide.reshape(pair_parts.shape[1], -1))
    up, down, out = (
        quarter_of(item, ctx) for item in (expand_weight, shrink_weight.T, output_weight.T)
    )
    quarters = lax.axis_size("ctx")
    pair_pieces, (normed, attn_scaled, attn_inverse), labels = lax.optimization_barrier(
        (
            [swap(pair_wide, "ctx", j) for j in range(1, quarters)],
            norm_rows(second_rows.astype(f32), attention_gain, attention_shift),
            plane_labels(*after((segment_ids, bucket_ids, positions), second_rows)),
        )
    )
    places, segments, buckets = labels
    normed = normed.astype(bf16)
    pair_mine = pack_rows([pair_wide] + pair_pieces, ctx)
    pair_other = swap(pair_mine, "shard", 1)
    pair = (
        dot(shard_half(normed, shard), pair_mine, NN)
        + dot(shard_half(normed, 1 - shard), pair_other, NN)
    ).astype(bf16)
    sent, out = after((plain(jnp.concatenate([up, down], 1)), plain(out)), pair_mine)
    landed, far, outs_near, hot, bounds = lax.optimization_barrier(
        (
            heads_out(pair),
            swap(sent, "tp", 2),
            [swap(out, "tp", k) for k in range(1, planes)],
            into_places(places, bucket_hot(buckets)),
            doc_bounds(segments),
        )
    )
    wide = pack_weights(sent, far, [out] + outs_near, plane)
    whole = lax.all_gather(after(wide, landed), ("shard", "ctx"), axis=0, tiled=True)
    up_full, down_full, output_full = (
        whole[:, : 2 * units],
        whole[:, 2 * units : 4 * units],
        whole[:, 4 * units :],
    )

    sorted_pair = into_places(places, landed)
    query_sorted, value_sorted = sorted_pair[:, :DH], sorted_pair[:, DH:]
    bounds = with_bound(bounds, query_sorted)
    (first_rows, second_grad_rows), (mix, logs) = rows_in(
        after(jnp.stack([first_half, second_cotangent]), landed),
        attend(bounds, query_sorted, value_sorted, hot),
    )
    far_grad_rows = swap(after(second_grad_rows, mix), "tp", 1)
    attention = heads_back(out_of_places(places, mix.T.astype(bf16)))

    first_out = (first_rows.astype(f32) + dot(attention, output_full, NT)).astype(bf16)
    ffn_in, ffn_scaled, ffn_inverse = norm_rows(first_out.astype(f32), forward_gain, forward_shift)
    ffn_in, far_grad_rows = lax.optimization_barrier((ffn_in.astype(bf16), far_grad_rows))

    def units_of(rows, grad_rows):
        pre_act = dot(rows, up_full, NN) + unit_bias
        below = 0.5 * (1.0 + lax.erf(pre_act * 2**-0.5))
        slope = below + pre_act * (jnp.exp(-0.5 * pre_act * pre_act) * (2 * jnp.pi) ** -0.5)
        pre_grad = (dot(grad_rows, down_full, NN) * slope).astype(bf16)
        return (pre_act * below).astype(bf16), pre_grad

    normed_all = lax.all_gather(after(normed, first_out), ("ctx", "shard"), axis=0, tiled=True)
    far_in, (hidden, pre_grad) = lax.optimization_barrier(
        (swap(ffn_in, "tp", 1), units_of(ffn_in, second_grad_rows))
    )
    (first_grad_rows,), (far_hidden, far_pre_grad) = rows_in(
        after(first_cotangent, far_in)[None], units_of(far_in, far_grad_rows)
    )
    far_ffn_grad = dot(far_pre_grad, up_full, NT).astype(bf16)
    all_rows = jnp.concatenate([ffn_in, far_in], 0)
    all_grad_rows = jnp.concatenate([second_grad_rows, far_grad_rows], 0)
    all_pre_grad = jnp.concatenate([pre_grad, far_pre_grad], 0)
    all_hidden = jnp.concatenate([hidden, far_hidden], 0)
    all_rows, all_grad_rows, pre_grad = after((all_rows, all_grad_rows, pre_grad), far_ffn_grad)
    theirs, far_branch, own_branch, ffn_grad, expand_sums, shrink_sums = lax.optimization_barrier(
        (
            swap(far_ffn_grad, "tp", 1),
            dot(far_hidden, down_full, NT).astype(bf16),
            second_rows.astype(f32) + dot(hidden, down_full, NT) + row_bias,
            dot(pre_grad, up_full, NT),
            chip_sums(all_rows, all_pre_grad).astype(bf16),
            chip_sums(all_grad_rows, all_hidden).astype(bf16),
        )
    )
    ffn_back, ffn_gain_grad, ffn_shift_grad = row_norm_back(
        ffn_grad + theirs.astype(f32), ffn_scaled, ffn_inverse, forward_gain
    )
    first_grad = (first_grad_rows.astype(f32) + ffn_back).astype(bf16)
    attention_grad = dot(first_grad, output_full, NN).astype(bf16)
    shrink_bias_grad = jnp.sum(second_grad_rows.astype(f32), 0)
    expand_bias_grad = jnp.sum(all_pre_grad.astype(f32), 0)
    far_branch = swap(far_branch, "tp", 1)

    spread = jnp.arange(planes, dtype=jnp.int32)[:, None]
    unit_grads = jnp.where(spread == plane, expand_bias_grad[None, :units], 0.0)
    unit_grads = jnp.where(spread == plane ^ 2, expand_bias_grad[None, units:], unit_grads)
    packed = jnp.concatenate(
        [unit_grads]
        + [item.reshape(planes, width) for item in (shrink_bias_grad, ffn_gain_grad, ffn_shift_grad)],
        1,
    )
    packed = (packed + swap(packed, "shard", 1)).astype(bf16).reshape(planes, quarters, -1)
    vector_width = packed.shape[2]
    packed = jnp.pad(packed, ((0, 0), (0, 0), (0, 16 * width - vector_width)))
    packed = packed.reshape(planes, quarters, 16, width).transpose(1, 2, 0, 3)
    packed = jnp.pad(packed.reshape(quarters, 16, -1), ((0, 0), (0, 0), (4 * units, 0)))
    early = jnp.concatenate(
        [expand_sums, shrink_sums, chip_sums(first_grad, attention).astype(bf16)], 1
    )
    early = jnp.concatenate([early.reshape(quarters, split // quarters, -1), packed], 1)
    early = early.reshape(-1, early.shape[2])
    grad_heads, early, normed_all = lax.optimization_barrier(
        (heads_out(attention_grad), early, normed_all)
    )
    early_mine = lax.psum_scatter(early, "ctx", scatter_dimension=0, tiled=True)
    outs_sliced, parts = rows_out(
        after(jnp.stack([first_out, first_grad]), grad_heads),
        seqs_here,
        attend_back(
            bounds, query_sorted, value_sorted, hot, into_places(places, grad_heads), mix, logs
        ),
    )
    far_branch, own_branch = after((far_branch, own_branch), parts)
    second_out = (own_branch + far_branch.astype(f32)).astype(bf16)
    def with_far(pair_grad_heads):
        sums = after(early_mine, pair_grad_heads)
        far = jnp.concatenate([sums[:, units : 2 * units], sums[:, 3 * units : 4 * units]], 1)
        pair_sums = lax.dot_general(
            normed_all, pair_grad_heads, (((0,), (0,)), ((), ())), preferred_element_type=f32
        ).astype(bf16)
        late = sums[:, 4 * units :].reshape(-1, planes, width).transpose(1, 0, 2)
        late = jnp.concatenate([pair_sums.reshape(planes, -1, 2 * DH), late], 1)
        return late, sums, heads_back(pair_grad_heads), swap(far, "tp", 2)

    second_out_sliced, (late, early_mine, pair_grad, far_sums) = rows_out(
        second_out[None],
        seqs_here,
        out_of_places(places, jnp.concatenate(parts, 1)),
        with_far,
    )
    near_sums = jnp.concatenate([early_mine[:, :units], early_mine[:, 2 * units : 3 * units]], 1)

    grad_mine, grad_other = dot(pair_grad, pair_mine, NT), dot(pair_grad, pair_other, NT)
    normed_grad = jnp.concatenate(
        [
            jnp.where(shard == 0, grad_mine, grad_other),
            jnp.where(shard == 0, grad_other, grad_mine),
        ],
        1,
    )
    attn_back, attn_gain_grad, attn_shift_grad = row_norm_back(
        normed_grad, attn_scaled, attn_inverse, attention_gain
    )
    second_grad = (second_grad_rows.astype(f32) + attn_back).astype(bf16)

    early_own = (near_sums.astype(f32) + far_sums.astype(f32)).astype(bf16)
    early_own = early_own[: split // quarters]
    pieces = [swap(plane_part(late, k), "tp", k) for k in range(1, planes)]
    late = sum((piece.astype(f32) for piece in pieces), plane_part(late, 0).astype(f32)).astype(bf16)
    split_at = width
    turned = lax.ppermute(
        late[:split_at],
        ("ctx", "tp"),
        [(at * planes + to, to * planes + at) for at in range(quarters) for to in range(planes)],
    )
    norm_grads = jnp.concatenate(
        [attn_gain_grad.reshape(planes, width), attn_shift_grad.reshape(planes, width)], 1
    )
    second_grad_sliced, (early_pieces, turned, norm_pieces) = rows_out(
        second_grad[None],
        seqs_here,
        (
            [swap(early_own, "ctx", j) for j in range(1, quarters)],
            turned,
            [swap(plane_part(norm_grads, k), "tp", k) for k in range(1, planes)],
        ),
    )
    early_own = pack_rows([early_own] + early_pieces, ctx).astype(f32)
    expand_own, shrink_own = early_own[:, :units], early_own[:, units:].T
    norm_own = sum_in_plane(sum(norm_pieces, plane_part(norm_grads, 0))).reshape(2, width)
    late_own = collect_ctx(jnp.concatenate([turned, late[split_at:]], 0)[None])
    pair_head = late_own[:, :split_at].reshape(-1, width)
    late_own = late_own[:, split_at:].astype(f32)
    output_own = late_own[:, : split // quarters].reshape(split, width).T
    owned = late_own[:, split // quarters :].reshape(quarters, -1)[:, :vector_width].reshape(-1)
    row_own = owned[units:].reshape(3, width)
    near = lax.dynamic_slice_in_dim(pair_head, shard * split, split, 0)
    other = swap(lax.dynamic_slice_in_dim(pair_head, (1 - shard) * split, split, 0), "shard", 1)
    pair_own = by_half(near, other).astype(f32)
    query_own = jnp.concatenate([pair_own[0, :, :DH], pair_own[1, :, :DH]], 1)
    value_own = jnp.concatenate([pair_own[0, :, DH:], pair_own[1, :, DH:]], 1)

    return (
        outs_sliced[0],
        second_out_sliced[0],
        outs_sliced[1],
        second_grad_sliced[0],
        query_own,
        value_own,
        output_own,
        expand_own,
        owned[:units],
        shrink_own,
        row_own[0],
        norm_own[0],
        norm_own[1],
        row_own[1],
        row_own[2],
    )


def row_planes(mesh):
    sizes = mesh.shape
    return sizes["tp"] == SEQS and sizes["shard"] == 2 and sizes["ctx"] == 4 and HEADS == 8


def solution(mesh):
    return jax.shard_map(
        row_device if row_planes(mesh) else general_device,
        mesh=mesh,
        in_specs=(
            P("ctx", "shard", "tp"),
            P("ctx", "shard", "tp"),
            P("ctx", "shard", "tp"),
            P("ctx", "shard", "tp"),
            P("shard", "ctx"),
            P("shard", None, "ctx"),
            P("shard", "ctx"),
            P("shard", "tp"),
            P("shard", "tp"),
            P("tp", "shard"),
            P("shard", "tp"),
            P("tp"),
            P("tp", "shard"),
            P("tp"),
            P(),
            P(),
            P(),
            P(),
        ),
        out_specs=(
            P("ctx", "shard", "tp"),
            P("ctx", "shard", "tp"),
            P("ctx", "shard", "tp"),
            P("ctx", "shard", "tp"),
            P("shard", "tp"),
            P("shard", "tp"),
            P("tp", "shard"),
            P("shard", "tp"),
            P("tp"),
            P("tp", "shard"),
            P("tp"),
            P("tp"),
            P("tp"),
            P("tp"),
            P("tp"),
        ),
        check_vma=False,
    )
```

```python
import jax
import jax.numpy as jnp
from jax import lax
from jax.experimental import pallas as pl
from jax.experimental.layout import Layout, with_layout_constraint
from jax.experimental.pallas import tpu as pltpu
from jax.sharding import PartitionSpec as P

D = 1024
DH = 128
ROUNDS = 4


SELF_SCORE = -10.0
NEG_FILL = -1e30
BLOCK_ROWS = 512


BUCKETS = 64
HEADS = 8
SEQS = 4
TILE = 512
GROUP = 1
BOUND = 38.0
NT = (((1,), (1,)), ((), ()))
NN = (((1,), (0,)), ((), ()))


def dot(left, right, dims):
    return lax.dot_general(left, right, dims, preferred_element_type=jnp.float32)


def start_of(place, bounds_ref):
    start = jnp.where(place >= bounds_ref[0], bounds_ref[0], 0)
    start = jnp.where(place >= bounds_ref[1], bounds_ref[1], start)
    return jnp.where(place >= bounds_ref[2], bounds_ref[2], start)


def tile_masks(begin_row, bounds_ref):
    query_lane = lax.broadcasted_iota(jnp.int32, (1, TILE), 1)
    doc_start = start_of(query_lane + begin_row, bounds_ref)
    first = start_of(begin_row, bounds_ref) // TILE
    last_start = start_of(begin_row + TILE - 1, bounds_ref)
    full = jnp.minimum((last_start + TILE - 1) // TILE, begin_row // TILE)
    return doc_start, first, full


def rows_at(ref, block, tiles=1):
    return ref[pl.ds(pl.multiple_of(block * TILE, TILE), tiles * TILE), :]


def norm_factor(q):
    return lax.rsqrt(jnp.mean(q * q, -1, keepdims=True) + 1e-06)


def attend_kernel(bounds_ref, q_ref, v_ref, hot_ref, out_ref, log_ref, key_sc, vt_sc):
    block = pl.program_id(0)
    blocks = pl.num_programs(0)

    @pl.when(block == 0)
    def _():
        def prep(at, carry):
            q = rows_at(q_ref, at).astype(jnp.float32)
            begin = pl.multiple_of(at * TILE, TILE)
            key_sc[pl.ds(begin, TILE), :] = (q * (norm_factor(q) * DH ** (-0.5))).astype(jnp.bfloat16)
            v = rows_at(v_ref, at).astype(jnp.float32)
            vt_sc[:, pl.ds(begin, TILE)] = v.T.astype(jnp.bfloat16)
            return carry

        lax.fori_loop(0, blocks, prep, 0)

    begin_row = block * TILE
    doc_start, first, full = tile_masks(begin_row, bounds_ref)
    q = rows_at(q_ref, block)
    hot = rows_at(hot_ref, block)
    key_row = lax.broadcasted_iota(jnp.int32, (TILE, 1), 0)
    lane = lax.broadcasted_iota(jnp.int32, (1, TILE), 1)

    def scores(at, tiles):
        return dot(rows_at(key_sc, at, tiles), q, NT), dot(rows_at(hot_ref, at, tiles), hot, NT)

    def vt(at, tiles):
        return vt_sc[:, pl.ds(pl.multiple_of(at * TILE, TILE), tiles * TILE)]

    itself = key_row == lane

    def diagonal():
        s, c = scores(block, 1)
        c = jnp.where((key_row < lane) & (key_row + begin_row >= doc_start), c, 0.0)
        return jnp.where(itself, SELF_SCORE, s), jnp.where(itself, float(ROUNDS), c)

    def in_document(c, at):
        return jnp.where(key_row + at * TILE >= doc_start, c, 0.0)

    def mixed(at, tiles, p):
        return dot(vt(at, tiles), p.astype(jnp.bfloat16), NN)

    @pl.when(bounds_ref[3] == 1)
    def _():
        def fold(at, tiles, carry, masked):
            total, acc = carry
            s, c = scores(at, tiles)
            if masked:
                c = in_document(c, at)
            p = c * jnp.exp(s)
            return total + jnp.sum(p, 0, keepdims=True), acc + mixed(at, tiles, p)

        s, c = diagonal()
        p = c * jnp.exp(s)
        carry = jnp.sum(p, 0, keepdims=True), mixed(block, 1, p)
        carry = lax.fori_loop(first, full, lambda at, x: fold(at, 1, x, True), carry)
        rest = (block - full) % GROUP
        carry = lax.fori_loop(full, full + rest, lambda at, x: fold(at, 1, x, False), carry)
        total, acc = lax.fori_loop(
            0,
            (block - full) // GROUP,
            lambda at, x: fold(full + rest + GROUP * at, GROUP, x, False),
            carry,
        )
        out_ref[...] = acc / total
        log_ref[pl.ds(block, 1), :] = jnp.log(total)

    @pl.when(bounds_ref[3] == 0)
    def _():
        def fold(at, carry):
            high, total, acc = carry
            s, c = scores(at, 1)
            c = in_document(c, at)
            s = jnp.where(c > 0, s, NEG_FILL)
            new_high = jnp.maximum(high, jnp.max(s, 0, keepdims=True))
            fade = jnp.exp(high - new_high)
            p = c * jnp.exp(s - new_high)
            total = total * fade + jnp.sum(p, 0, keepdims=True)
            return new_high, total, acc * fade + mixed(at, 1, p)

        s, c = diagonal()
        s = jnp.where(c > 0, s, NEG_FILL)
        high = jnp.max(s, 0, keepdims=True)
        p = c * jnp.exp(s - high)
        carry = high, jnp.sum(p, 0, keepdims=True), mixed(block, 1, p)
        high, total, acc = lax.fori_loop(first, block, fold, carry)
        out_ref[...] = acc / total
        log_ref[pl.ds(block, 1), :] = high + jnp.log(total)


def attend(bounds, q, v, hot):
    rows = q.shape[0]
    blocks = rows // TILE
    whole = lambda shape: pl.BlockSpec(shape, lambda i, *_: (0,) * len(shape))
    return pl.pallas_call(
        attend_kernel,
        name="attend",
        out_shape=(
            jax.ShapeDtypeStruct((DH, rows), jnp.float32),
            jax.ShapeDtypeStruct((blocks, TILE), jnp.float32),
        ),
        grid_spec=pltpu.PrefetchScalarGridSpec(
            num_scalar_prefetch=1,
            grid=(blocks,),
            in_specs=[whole((rows, DH)), whole((rows, DH)), whole((rows, ROUNDS * BUCKETS))],
            out_specs=[pl.BlockSpec((DH, TILE), lambda i, *_: (0, i)), whole((blocks, TILE))],
            scratch_shapes=[pltpu.VMEM((rows, DH), jnp.bfloat16), pltpu.VMEM((DH, rows), jnp.bfloat16)],
        ),
        compiler_params=pltpu.CompilerParams(
            dimension_semantics=("arbitrary",), vmem_limit_bytes=40 * 2**20
        ),
        cost_estimate=pl.CostEstimate(
            flops=rows * DH, bytes_accessed=rows * DH, transcendentals=0
        ),
    )(bounds, q, v, hot)


def attend_back_kernel(
    bounds_ref, q_ref, v_ref, hot_ref, grad_ref, out_ref, log_ref,
    q_grad_ref, v_grad_ref, key_sc, kt_sc, dk_sc, dv_sc, dq_sc,
):
    block = pl.program_id(0)
    blocks = pl.num_programs(0)

    @pl.when(block == 0)
    def _():
        def prep(at, carry):
            begin = pl.multiple_of(at * TILE, TILE)
            q = rows_at(q_ref, at).astype(jnp.float32)
            k = q * (norm_factor(q) * DH ** (-0.5))
            key_sc[pl.ds(begin, TILE), :] = k.astype(jnp.bfloat16)
            kt_sc[:, pl.ds(begin, TILE)] = k.T.astype(jnp.bfloat16)
            dk_sc[pl.ds(begin, TILE), :] = jnp.zeros((TILE, DH), jnp.float32)
            dv_sc[pl.ds(begin, TILE), :] = jnp.zeros((TILE, DH), jnp.float32)
            return carry

        lax.fori_loop(0, blocks, prep, 0)

    begin_row = block * TILE
    doc_start, first, full = tile_masks(begin_row, bounds_ref)
    q = rows_at(q_ref, block)
    hot = rows_at(hot_ref, block)
    grad = rows_at(grad_ref, block)
    log_row = log_ref[pl.ds(block, 1), :]
    delta = jnp.sum(grad.astype(jnp.float32).T * out_ref[...], 0, keepdims=True)
    key_row = lax.broadcasted_iota(jnp.int32, (TILE, 1), 0)
    lane = lax.broadcasted_iota(jnp.int32, (1, TILE), 1)

    itself = key_row == lane

    def fold(at, tiles, acc, masked, bounded, diagonal=False):
        rows = pl.ds(pl.multiple_of(at * TILE, TILE), tiles * TILE)
        s = dot(key_sc[rows, :], q, NT)
        c = dot(hot_ref[rows, :], hot, NT)
        up = dot(v_ref[rows, :], grad, NT)
        if diagonal:
            c = jnp.where((key_row < lane) & (key_row + begin_row >= doc_start), c, 0.0)
            c = jnp.where(itself, float(ROUNDS), c)
            s = jnp.where(itself, SELF_SCORE, s)
        elif masked:
            c = jnp.where(key_row + at * TILE >= doc_start, c, 0.0)
        if not bounded:
            s = jnp.where(c > 0, s, NEG_FILL)
        w = c * jnp.exp(s - log_row)
        ds = w * (up - delta)
        if diagonal:
            ds = jnp.where(itself, 0.0, ds)
        w = w.astype(jnp.bfloat16)
        ds = ds.astype(jnp.bfloat16)
        dv_sc[rows, :] += dot(w, grad, NN)
        dk_sc[rows, :] += dot(ds, q, NN)
        return acc + dot(kt_sc[:, rows], ds, NN)

    def store(acc):
        dq_sc[pl.ds(pl.multiple_of(begin_row, TILE), TILE), :] = acc.T

    nothing = jnp.zeros((DH, TILE), jnp.float32)

    @pl.when(bounds_ref[3] == 1)
    def _():
        acc = fold(block, 1, nothing, True, True, True)
        acc = lax.fori_loop(first, full, lambda at, x: fold(at, 1, x, True, True), acc)
        rest = (block - full) % GROUP
        acc = lax.fori_loop(full, full + rest, lambda at, x: fold(at, 1, x, False, True), acc)
        store(
            lax.fori_loop(
                0,
                (block - full) // GROUP,
                lambda at, x: fold(full + rest + GROUP * at, GROUP, x, False, True),
                acc,
            )
        )

    @pl.when(bounds_ref[3] == 0)
    def _():
        acc = fold(block, 1, nothing, True, False, True)
        store(lax.fori_loop(first, block, lambda at, x: fold(at, 1, x, True, False), acc))

    @pl.when(block == blocks - 1)
    def _():
        def finish(at, carry):
            begin = pl.multiple_of(at * TILE, TILE)
            q = rows_at(q_ref, at).astype(jnp.float32)
            r = norm_factor(q)
            g = rows_at(dk_sc, at).astype(jnp.bfloat16).astype(jnp.float32)
            back = (r * DH ** (-0.5)) * (g - q * (r * r * jnp.mean(q * g, -1, keepdims=True)))
            q_grad_ref[pl.ds(begin, TILE), :] = (rows_at(dq_sc, at) + back).astype(jnp.bfloat16)
            v_grad_ref[pl.ds(begin, TILE), :] = rows_at(dv_sc, at).astype(jnp.bfloat16)
            return carry

        lax.fori_loop(0, blocks, finish, 0)


def attend_back(bounds, q, v, hot, grad, out, logs):
    rows = q.shape[0]
    blocks = rows // TILE
    whole = lambda shape: pl.BlockSpec(shape, lambda i, *_: (0,) * len(shape))
    return pl.pallas_call(
        attend_back_kernel,
        name="attend_back",
        out_shape=(jax.ShapeDtypeStruct((rows, DH), jnp.bfloat16),) * 2,
        grid_spec=pltpu.PrefetchScalarGridSpec(
            num_scalar_prefetch=1,
            grid=(blocks,),
            in_specs=[
                whole((rows, DH)), whole((rows, DH)), whole((rows, ROUNDS * BUCKETS)), whole((rows, DH)),
                pl.BlockSpec((DH, TILE), lambda i, *_: (0, i)), whole((blocks, TILE)),
            ],
            out_specs=[whole((rows, DH))] * 2,
            scratch_shapes=[
                pltpu.VMEM((rows, DH), jnp.bfloat16),
                pltpu.VMEM((DH, rows), jnp.bfloat16),
                pltpu.VMEM((rows, DH), jnp.float32),
                pltpu.VMEM((rows, DH), jnp.float32),
                pltpu.VMEM((rows, DH), jnp.float32),
            ],
        ),
        compiler_params=pltpu.CompilerParams(
            dimension_semantics=("arbitrary",), vmem_limit_bytes=48 * 2**20
        ),
        cost_estimate=pl.CostEstimate(
            flops=rows * DH, bytes_accessed=rows * DH, transcendentals=0
        ),
    )(bounds, q, v, hot, grad, out, logs)


def place_matrix(places):
    rows = places.shape[0]
    return (jnp.arange(rows, dtype=jnp.int32)[:, None] == places[None, :]).astype(jnp.bfloat16)


def into_places(places, vectors):
    return jnp.einsum("pa,ad->pd", place_matrix(places), vectors, preferred_element_type=jnp.float32).astype(jnp.bfloat16)


def out_of_places(places, vectors):
    rows = places.shape[0]
    picks = (places[:, None] == jnp.arange(rows, dtype=jnp.int32)[None, :]).astype(jnp.bfloat16)
    return dot(picks, vectors, NN).astype(jnp.bfloat16)


def bucket_hot(buckets):
    hot = buckets.T[:, :, None] == jnp.arange(BUCKETS, dtype=jnp.int32)
    return hot.astype(jnp.bfloat16).reshape(buckets.shape[1], ROUNDS * BUCKETS)


def doc_bounds(segments):
    return jnp.sum((segments[None, :] < jnp.arange(1, 4, dtype=jnp.int32)[:, None]).astype(jnp.int32), 1)


def with_bound(bounds, queries):
    squares = jnp.sum(queries.astype(jnp.float32) ** 2, -1)
    return jnp.concatenate([bounds, (jnp.max(squares) <= BOUND**2).astype(jnp.int32)[None]])


def smooth_unit(values_in):
    return jax.nn.gelu(values_in, approximate=False)


def norm_rows(rows_wide, gain_row, shift_row):
    centre = jnp.mean(rows_wide, -1, keepdims=True)
    offset = rows_wide - centre
    inverse = lax.rsqrt(jnp.mean(offset * offset, -1, keepdims=True) + 1e-05)
    scaled = offset * inverse
    return (scaled * gain_row + shift_row, scaled, inverse)


def unit_keys(queries):
    shaped = queries.reshape(queries.shape[:-1] + (queries.shape[-1] // DH, DH))
    factor = lax.rsqrt(jnp.mean(shaped * shaped, -1, keepdims=True) + 1e-06) * DH ** (-0.5)
    return (shaped * factor).reshape(queries.shape)


def heads_view(vectors):
    return vectors.reshape(vectors.shape[0], vectors.shape[1], vectors.shape[2] // DH, DH)


def full_rows(sliced):
    return lax.all_gather(sliced, "tp", axis=2, tiled=True)


def branch_sum(partial_value):
    return lax.psum_scatter(partial_value, "tp", scatter_dimension=2, tiled=True)


def norm_back(grad_slice, scaled_slice, inverse, gain_slice):
    weighted = grad_slice * gain_slice
    first_sum, second_sum = lax.psum(
        (jnp.sum(weighted, -1, keepdims=True), jnp.sum(weighted * scaled_slice, -1, keepdims=True)),
        "tp",
    )
    inner = inverse * (weighted - first_sum / D - scaled_slice * (second_sum / D))
    return (inner, jnp.sum(grad_slice * scaled_slice, (0, 1)), jnp.sum(grad_slice, (0, 1)))


def label_rows(all_labels, begin_row, extent):
    all_segments, all_buckets, all_positions = all_labels
    return (
        lax.dynamic_slice_in_dim(all_segments, begin_row, extent, 1),
        lax.dynamic_slice_in_dim(all_buckets, begin_row, extent, 2),
        lax.dynamic_slice_in_dim(all_positions, begin_row, extent, 1),
    )


def block_weights(query_heads, query_labels, key_heads, key_labels):
    query_seg, query_buck, query_pos = query_labels
    key_seg, key_buck, key_pos = key_labels
    scores = jnp.einsum(
        "pshd,kshd->shpk", query_heads, key_heads, preferred_element_type=jnp.float32
    )
    matches = jnp.sum((query_buck[:, :, :, None] == key_buck[:, :, None, :]).astype(jnp.int32), 1)
    same_doc = query_seg[:, :, None] == key_seg[:, None, :]
    earlier = key_pos[:, None, :] < query_pos[:, :, None]
    itself = key_pos[:, None, :] == query_pos[:, :, None]
    counts = jnp.where(itself, ROUNDS, jnp.where(earlier & same_doc, matches, 0)).astype(
        jnp.float32
    )[:, None]
    shifted = jnp.where(itself[:, None], SELF_SCORE, scores)
    return (shifted, counts, itself[:, None])


def weights_of(shifted, counts, log_total):
    return jnp.where(counts > 0, counts * jnp.exp(shifted - log_total[..., None]), 0.0)


def blockwise(advance, running, row_count):
    extent = BLOCK_ROWS

    def turn(state_now, block_index):
        return (advance(state_now, block_index * extent, extent), None)

    return lax.scan(turn, running, jnp.arange(row_count // extent, dtype=jnp.int32))[0]


def over_keys(key_vectors, value_vectors, folder, initial):
    return folder(
        initial,
        (
            lax.all_gather(key_vectors, "ctx", axis=0, tiled=True),
            lax.all_gather(value_vectors, "ctx", axis=0, tiled=True),
        ),
        jnp.int32(0),
    )


def over_context(first_part, second_part, third_part, fourth_part, fifth_part):
    return (
        lax.psum(first_part.astype(jnp.bfloat16), "ctx").astype(jnp.float32),
        lax.psum(second_part.astype(jnp.bfloat16), "ctx").astype(jnp.float32),
        lax.psum(third_part.astype(jnp.bfloat16), "ctx").astype(jnp.float32),
        lax.psum(fourth_part.astype(jnp.bfloat16), "ctx").astype(jnp.float32),
        lax.psum(fifth_part.astype(jnp.bfloat16), "ctx").astype(jnp.float32),
    )


def to_row_owners(first_part, second_part, third_part):
    return (
        lax.psum_scatter(
            first_part.astype(jnp.bfloat16), "shard", scatter_dimension=0, tiled=True
        ).astype(jnp.float32),
        lax.psum_scatter(
            second_part.astype(jnp.bfloat16), "shard", scatter_dimension=0, tiled=True
        ).astype(jnp.float32),
        lax.psum_scatter(
            third_part.astype(jnp.bfloat16), "shard", scatter_dimension=0, tiled=True
        ).astype(jnp.float32),
    )


def to_col_owners(first_part, second_part):
    return (
        lax.psum_scatter(
            first_part.astype(jnp.bfloat16), "shard", scatter_dimension=1, tiled=True
        ).astype(jnp.float32),
        lax.psum_scatter(
            second_part.astype(jnp.bfloat16), "shard", scatter_dimension=1, tiled=True
        ).astype(jnp.float32),
    )


def general_device(
    first_half,
    second_half,
    first_cotangent,
    second_cotangent,
    segment_ids,
    bucket_ids,
    positions,
    query_weight,
    value_weight,
    output_weight,
    expand_weight,
    expand_bias,
    shrink_weight,
    shrink_bias,
    attention_gain,
    attention_shift,
    forward_gain,
    forward_shift,
):
    rows_here, seqs_here, slice_width = first_half.shape
    width_heads = query_weight.shape[1]
    heads_here = width_heads // DH
    tp_start = lax.axis_index("tp") * slice_width
    ctx_start = lax.axis_index("ctx") * rows_here
    bf16 = jnp.bfloat16
    f32 = jnp.float32

    def columns(wide):
        return lax.dynamic_slice_in_dim(wide, tp_start, slice_width, wide.ndim - 1)

    full_query, full_value, full_expand = (
        lax.all_gather(query_weight, "shard", axis=0, tiled=True),
        lax.all_gather(value_weight, "shard", axis=0, tiled=True),
        lax.all_gather(expand_weight, "shard", axis=0, tiled=True),
    )
    full_output, full_shrink = (
        lax.all_gather(output_weight, "shard", axis=1, tiled=True),
        lax.all_gather(shrink_weight, "shard", axis=1, tiled=True),
    )
    all_labels = (
        lax.all_gather(segment_ids, "ctx", axis=1, tiled=True),
        lax.all_gather(bucket_ids, "ctx", axis=2, tiled=True),
        lax.all_gather(positions, "ctx", axis=1, tiled=True),
    )
    local_labels = label_rows(all_labels, ctx_start, rows_here)
    second_wide = full_rows(second_half)
    normed, attn_scaled, attn_inverse = norm_rows(
        second_wide.astype(f32), attention_gain, attention_shift
    )
    normed = normed.astype(bf16)
    queries = jnp.einsum("psd,de->pse", normed, full_query, preferred_element_type=f32).astype(bf16)
    key_vectors = unit_keys(queries.astype(f32)).astype(bf16)
    value_vectors = jnp.einsum(
        "psd,de->pse", normed, full_value, preferred_element_type=f32
    ).astype(bf16)
    query_heads = heads_view(queries)
    stat_shape = (seqs_here, heads_here, rows_here)
    head_zero = jnp.zeros((rows_here, seqs_here, heads_here, DH), f32)

    def norm_fold(running, pieces, begin_row):
        key_piece = pieces[0]

        def advance(state_now, offset, extent):
            highest, summed = state_now
            key_heads = heads_view(lax.dynamic_slice_in_dim(key_piece, offset, extent, 0))
            shifted, counts, _ = block_weights(
                query_heads, local_labels, key_heads, label_rows(all_labels, offset, extent)
            )
            usable = counts > 0
            new_high = jnp.maximum(highest, jnp.max(jnp.where(usable, shifted, NEG_FILL), -1))
            summed = summed * jnp.exp(highest - new_high) + jnp.sum(
                jnp.where(usable, counts * jnp.exp(shifted - new_high[..., None]), 0.0), -1
            )
            return (new_high, summed)

        return blockwise(advance, running, key_piece.shape[0])

    highest, summed = over_keys(
        key_vectors,
        value_vectors,
        norm_fold,
        (jnp.full(stat_shape, NEG_FILL, f32), jnp.zeros(stat_shape, f32)),
    )
    log_total = highest + jnp.log(summed)

    def key_block(pieces, offset, extent):
        key_heads = heads_view(lax.dynamic_slice_in_dim(pieces[0], offset, extent, 0))
        value_heads = heads_view(lax.dynamic_slice_in_dim(pieces[1], offset, extent, 0))
        shifted, counts, itself = block_weights(
            query_heads, local_labels, key_heads, label_rows(all_labels, offset, extent)
        )
        return (key_heads, value_heads, weights_of(shifted, counts, log_total), itself)

    def mix_fold(running, pieces, begin_row):

        def advance(state_now, offset, extent):
            key_heads, value_heads, weights, itself = key_block(pieces, offset, extent)
            return state_now + jnp.einsum(
                "shpk,kshd->pshd", weights.astype(bf16), value_heads, preferred_element_type=f32
            )

        return blockwise(advance, running, pieces[0].shape[0])

    head_mix = over_keys(key_vectors, value_vectors, mix_fold, head_zero)
    attention = head_mix.reshape(rows_here, seqs_here, width_heads).astype(bf16)
    branch = branch_sum(
        jnp.einsum("pse,ed->psd", attention, full_output, preferred_element_type=f32)
    )
    first_out = (first_half.astype(f32) + branch).astype(bf16)
    first_wide = full_rows(first_out)
    ffn_in, ffn_scaled, ffn_inverse = norm_rows(first_wide.astype(f32), forward_gain, forward_shift)
    ffn_in = ffn_in.astype(bf16)
    pre_act = (
        jnp.einsum("psd,df->psf", ffn_in, full_expand, preferred_element_type=f32) + expand_bias
    )
    hidden_exact, unit_pull = jax.vjp(smooth_unit, pre_act)
    hidden = hidden_exact.astype(bf16)
    second_branch = (
        branch_sum(jnp.einsum("psf,fd->psd", hidden, full_shrink, preferred_element_type=f32))
        + shrink_bias
    )
    second_out = (second_half.astype(f32) + second_branch).astype(bf16)
    cotangent_wide = full_rows(second_cotangent)
    hidden_grad = jnp.einsum("psd,fd->psf", cotangent_wide, full_shrink, preferred_element_type=f32)
    pre_grad = unit_pull(hidden_grad)[0].astype(bf16)
    shrink_grad = jnp.einsum("psf,psd->fd", hidden, cotangent_wide, preferred_element_type=f32)
    shrink_bias_grad = jnp.sum(second_cotangent.astype(f32), (0, 1))
    expand_grad = jnp.einsum("psd,psf->df", ffn_in, pre_grad, preferred_element_type=f32)
    expand_bias_grad = jnp.sum(pre_grad.astype(f32), (0, 1))
    ffn_grad = branch_sum(
        jnp.einsum("psf,df->psd", pre_grad, full_expand, preferred_element_type=f32)
    )
    ffn_back, forward_gain_grad, forward_shift_grad = norm_back(
        ffn_grad, columns(ffn_scaled), ffn_inverse, columns(forward_gain)
    )
    first_grad = (first_cotangent.astype(f32) + ffn_back).astype(bf16)
    grad_wide = full_rows(first_grad)
    output_grad = jnp.einsum("pse,psd->ed", attention, grad_wide, preferred_element_type=f32)
    attention_grad = jnp.einsum(
        "psd,ed->pse", grad_wide, full_output, preferred_element_type=f32
    ).astype(bf16)
    grad_heads = heads_view(attention_grad)

    def delta_fold(running, pieces, begin_row):

        def advance(state_now, offset, extent):
            key_heads, value_heads, weights, itself = key_block(pieces, offset, extent)
            upstream = jnp.einsum(
                "pshd,kshd->shpk", grad_heads, value_heads, preferred_element_type=f32
            )
            return state_now + jnp.sum(weights * upstream, -1)

        return blockwise(advance, running, pieces[0].shape[0])

    row_delta = over_keys(key_vectors, value_vectors, delta_fold, jnp.zeros(stat_shape, f32))

    def query_fold(running, pieces, begin_row):

        def advance(state_now, offset, extent):
            key_heads, value_heads, weights, itself = key_block(pieces, offset, extent)
            upstream = jnp.einsum(
                "pshd,kshd->shpk", grad_heads, value_heads, preferred_element_type=f32
            )
            score_grad = jnp.where(itself, 0.0, weights * (upstream - row_delta[..., None])).astype(
                bf16
            )
            return state_now + jnp.einsum(
                "shpk,kshd->pshd", score_grad, key_heads, preferred_element_type=f32
            )

        return blockwise(advance, running, pieces[0].shape[0])

    query_part = over_keys(key_vectors, value_vectors, query_fold, head_zero)
    query_lse, query_delta = (
        lax.all_gather(log_total, "ctx", axis=2, tiled=True),
        lax.all_gather(row_delta, "ctx", axis=2, tiled=True),
    )
    local_keys = heads_view(key_vectors)
    local_values = heads_view(value_vectors)
    query_piece = lax.all_gather(queries, "ctx", axis=0, tiled=True)
    grad_piece = lax.all_gather(attention_grad, "ctx", axis=0, tiled=True)

    def advance(state_now, offset, extent):
        remote_queries = heads_view(lax.dynamic_slice_in_dim(query_piece, offset, extent, 0))
        remote_grads = heads_view(lax.dynamic_slice_in_dim(grad_piece, offset, extent, 0))
        lse_rows = lax.dynamic_slice_in_dim(query_lse, offset, extent, 2)
        delta_rows = lax.dynamic_slice_in_dim(query_delta, offset, extent, 2)
        shifted, counts, itself = block_weights(
            remote_queries, label_rows(all_labels, offset, extent), local_keys, local_labels
        )
        weights = weights_of(shifted, counts, lse_rows)
        upstream = jnp.einsum(
            "pshd,kshd->shpk", remote_grads, local_values, preferred_element_type=f32
        )
        score_grad = jnp.where(itself, 0.0, weights * (upstream - delta_rows[..., None])).astype(
            bf16
        )
        key_now = state_now[0] + jnp.einsum(
            "shpk,pshd->kshd", score_grad, remote_queries, preferred_element_type=f32
        )
        value_now = state_now[1] + jnp.einsum(
            "shpk,pshd->kshd", weights.astype(bf16), remote_grads, preferred_element_type=f32
        )
        return (key_now, value_now)

    key_part, value_part = blockwise(advance, (head_zero, head_zero), query_piece.shape[0])
    keys_grad = key_part.reshape(rows_here, seqs_here, width_heads).astype(bf16)
    values_grad = value_part.reshape(rows_here, seqs_here, width_heads).astype(bf16)
    unit_back = jax.vjp(unit_keys, queries.astype(f32))[1]
    queries_total = (
        query_part.reshape(rows_here, seqs_here, width_heads) + unit_back(keys_grad.astype(f32))[0]
    ).astype(bf16)
    query_grad = jnp.einsum("psd,pse->de", normed, queries_total, preferred_element_type=f32)
    value_grad = jnp.einsum("psd,pse->de", normed, values_grad, preferred_element_type=f32)
    normed_grad = branch_sum(
        jnp.einsum("pse,de->psd", queries_total, full_query, preferred_element_type=f32)
        + jnp.einsum("pse,de->psd", values_grad, full_value, preferred_element_type=f32)
    )
    attn_back, attention_gain_grad, attention_shift_grad = norm_back(
        normed_grad, columns(attn_scaled), attn_inverse, columns(attention_gain)
    )
    second_grad = (second_cotangent.astype(f32) + attn_back).astype(bf16)
    expand_bias_sum, shrink_bias_sum, attn_gain_sum, attn_shift_sum, ffn_gain_sum, ffn_shift_sum = (
        lax.psum(
            (
                expand_bias_grad,
                shrink_bias_grad,
                attention_gain_grad,
                attention_shift_grad,
                forward_gain_grad,
                forward_shift_grad,
            ),
            ("shard", "ctx"),
        )
    )
    query_sum, value_sum, expand_sum, output_sum, shrink_sum = over_context(
        query_grad, value_grad, expand_grad, output_grad, shrink_grad
    )
    query_own, value_own, expand_own = to_row_owners(query_sum, value_sum, expand_sum)
    output_own, shrink_own = to_col_owners(output_sum, shrink_sum)
    return (
        first_out,
        second_out,
        first_grad,
        second_grad,
        query_own,
        value_own,
        output_own,
        expand_own,
        expand_bias_sum,
        shrink_own,
        shrink_bias_sum,
        attn_gain_sum,
        attn_shift_sum,
        ffn_gain_sum,
        ffn_shift_sum,
    )


def swap(vectors, axis, bits):
    size = lax.axis_size(axis)
    return lax.ppermute(vectors, axis, [(at, at ^ bits) for at in range(size)])


def where_am_i():
    return lax.axis_index("shard"), lax.axis_index("ctx"), lax.axis_index("tp")


def plane_pairs(step, inverse):
    shards, planes = lax.axis_size("shard"), lax.axis_size("tp")
    local_seqs = planes // shards
    pairs = []
    for shard in range(shards):
        for plane in range(planes):
            chunk = step ^ plane
            there = (chunk % shards) * planes + shard * local_seqs + chunk // shards
            here = shard * planes + plane
            pairs.append((there, here) if inverse else (here, there))
    return pairs


def rows_in(sliced, beside=(), extra=None):
    shard, _, plane = where_am_i()
    shards, planes = lax.axis_size("shard"), lax.axis_size("tp")
    count, slots, seqs, width = sliced.shape
    extent = slots // shards
    by_seq = sliced.transpose(2, 0, 1, 3).reshape(seqs, count, shards, extent, width)
    by_seq = by_seq.transpose(0, 2, 1, 3, 4).reshape(seqs * shards, count * extent, width)
    if extra is not None:
        by_seq = jnp.concatenate([by_seq, jnp.concatenate([extra] * seqs, 0)], 1)
    mine = (plane % seqs) * shards + shard
    landed = []
    for step in range(planes):
        chunk = lax.dynamic_index_in_dim(by_seq, step ^ plane, 0, False)
        landed.append(lax.ppermute(chunk, ("shard", "tp"), plane_pairs(step, False)))
    landed, beside = lax.optimization_barrier((landed, beside))
    whole = jnp.zeros((count * extent, planes * width), sliced.dtype)
    for step in range(planes):
        piece = landed[step][: count * extent]
        whole = lax.dynamic_update_slice_in_dim(whole, piece, (step ^ mine) * width, 1)
    whole = whole.reshape(count, extent, planes * width)
    if extra is None:
        return whole, beside
    extras = jnp.zeros((planes,) + extra.shape[1:], extra.dtype)
    for step in range(planes):
        piece = landed[step][None, count * extent :]
        extras = lax.dynamic_update_slice_in_dim(extras, piece, step ^ mine, 0)
    return whole, beside, extras


def rows_out(whole, seqs, beside=(), first=None):
    shard, _, plane = where_am_i()
    shards, planes = lax.axis_size("shard"), lax.axis_size("tp")
    count, extent, features = whole.shape
    width = features // planes
    mine = (plane % seqs) * shards + shard
    flat = whole.reshape(count * extent, features)

    def send(step):
        piece = lax.dynamic_slice_in_dim(flat, (step ^ mine) * width, width, 1)
        return lax.ppermute(piece, ("shard", "tp"), plane_pairs(step, True))

    half = planes // 2 if first is not None else 0
    landed = [send(step) for step in range(half)]
    if first is not None:
        landed, beside, flat = lax.optimization_barrier((landed, beside, flat))
        beside = first(beside)
    rest = [send(step) for step in range(half, planes)]
    rest, beside = lax.optimization_barrier((rest, beside))
    landed = landed + rest
    by_seq = jnp.zeros((seqs * shards, count * extent, width), whole.dtype)
    for step in range(planes):
        by_seq = lax.dynamic_update_slice_in_dim(by_seq, landed[step][None], step ^ plane, 0)
    parts = by_seq.reshape(seqs, shards, count, extent, width).transpose(2, 1, 3, 0, 4)
    return parts.reshape(count, shards * extent, seqs, width), beside


def quarter_of(local, at):
    extent = local.shape[0] // lax.axis_size("ctx")
    return lax.dynamic_slice_in_dim(local, at * extent, extent, 0)


def by_half(own, other):
    first = lax.axis_index("shard") == 0
    return jnp.stack([jnp.where(first, own, other), jnp.where(first, other, own)])


def plain(vectors):
    return with_layout_constraint(vectors, Layout(major_to_minor=tuple(range(vectors.ndim))))


def core_parts(local):
    mine = quarter_of(local, lax.axis_index("ctx"))
    return by_half(mine, swap(mine, "shard", 1))


def split_bias(values):
    high = values.astype(jnp.bfloat16)
    rest = values - high.astype(jnp.float32)
    middle = rest.astype(jnp.bfloat16)
    return jnp.stack([high, middle, (rest - middle.astype(jnp.float32)).astype(jnp.bfloat16)])


def shard_half(wide, at):
    extent = wide.shape[1] // 2
    return lax.dynamic_slice_in_dim(wide, at * extent, extent, 1)


def chip_sums(rows_wide, columns_wide):
    shard = lax.axis_index("shard")

    def product(at):
        return lax.dot_general(
            shard_half(rows_wide, at),
            columns_wide,
            (((0,), (0,)), ((), ())),
            preferred_element_type=jnp.float32,
        )

    theirs = swap(product(1 - shard).astype(jnp.bfloat16), "shard", 1)
    return product(shard) + theirs.astype(jnp.float32)


def sum_parts(parts):
    return jnp.sum(parts.astype(jnp.float32), 0)


def send_ctx(sums):
    quarters = lax.axis_size("ctx")
    parts = sums.reshape(quarters, sums.shape[0] // quarters, sums.shape[1])
    return lax.all_to_all(parts, "ctx", 0, 0, tiled=True)


def scatter_ctx(sums):
    return sum_parts(send_ctx(sums))


def scatter_tp(sums):
    planes = lax.axis_size("tp")
    parts = sums.reshape(sums.shape[0], planes, -1).transpose(1, 0, 2)
    return sum_parts(lax.all_to_all(parts, "tp", 0, 0, tiled=True))


def collect_ctx(quarter):
    quarters = lax.axis_size("ctx")
    return in_order([quarter] + [swap(quarter, "ctx", j) for j in range(1, quarters)])


def in_order(pieces):
    ctx, extent = lax.axis_index("ctx"), pieces[0].shape[0]
    whole = jnp.zeros((len(pieces) * extent,) + pieces[0].shape[1:], pieces[0].dtype)
    for j, piece in enumerate(pieces):
        whole = lax.dynamic_update_slice_in_dim(whole, piece, (ctx ^ j) * extent, 0)
    return whole


def reduce_context_first(sums):
    bf16 = jnp.bfloat16
    quarter = scatter_ctx(sums.astype(bf16)).astype(bf16)
    return collect_ctx(scatter_tp(quarter).astype(bf16)).astype(jnp.float32)


def plane_part(parts, k):
    return lax.dynamic_index_in_dim(parts, lax.axis_index("tp") ^ k, 0, False)


def sum_in_plane(total):
    total = total + swap(total, "shard", 1)
    return sum(swap(total, "ctx", j) for j in range(1, lax.axis_size("ctx"))) + total


def after(values, ready):
    return lax.optimization_barrier((values, ready))[0]


def row_norm_back(grad, scaled, inverse, gain):
    weighted = grad * gain
    first = jnp.mean(weighted, -1, keepdims=True)
    second = jnp.mean(weighted * scaled, -1, keepdims=True)
    inner = inverse * (weighted - first - scaled * second)
    return inner, jnp.sum(grad * scaled, 0), jnp.sum(grad, 0)


def heads_out(vectors):
    heads = HEADS
    sent = vectors.reshape(vectors.shape[0], heads, -1).transpose(1, 0, 2)
    landed = lax.all_to_all(sent, ("ctx", "shard"), split_axis=0, concat_axis=0, tiled=True)
    return landed.reshape(-1, landed.shape[2])


def heads_back(vectors):
    sent = vectors.reshape(HEADS, -1, vectors.shape[1])
    landed = lax.all_to_all(sent, ("ctx", "shard"), split_axis=0, concat_axis=0, tiled=True)
    return landed.transpose(1, 0, 2).reshape(landed.shape[1], -1)


def plane_labels(segment_ids, bucket_ids, positions):
    shard, _, plane = where_am_i()
    seqs, slots = positions.shape
    packed = jnp.concatenate([positions[:, None], segment_ids[:, None], bucket_ids], 1)
    kinds = packed.shape[1]
    mine = lax.dynamic_index_in_dim(packed, plane % seqs, 0, False).reshape(-1, 128)
    mine = jnp.where(shard == plane // seqs, mine, swap(mine, "shard", 1))
    whole = collect_ctx(mine).reshape(-1, kinds, slots).transpose(1, 0, 2).reshape(kinds, -1)
    return whole[0], whole[1], whole[2:]


def pack_rows_kernel(code_ref, *refs):
    pieces, out_ref, sems = refs[:-2], refs[-2], refs[-1]
    extent = pieces[0].shape[0]
    copies = []
    for j, ref in enumerate(pieces):
        place = pl.multiple_of((code_ref[0] ^ j) * extent, extent)
        copies.append(pltpu.make_async_copy(ref, out_ref.at[pl.ds(place, extent), :], sems.at[j]))
        copies[-1].start()
    for copy in copies:
        copy.wait()


def pack_rows(pieces, code):
    extent, width = pieces[0].shape
    shape = (len(pieces) * extent, width)
    return pl.pallas_call(
        pack_rows_kernel,
        name="pack_rows",
        out_shape=jax.ShapeDtypeStruct(shape, pieces[0].dtype),
        grid_spec=pltpu.PrefetchScalarGridSpec(
            num_scalar_prefetch=1,
            grid=(1,),
            in_specs=[pl.BlockSpec(memory_space=pl.ANY)] * len(pieces),
            out_specs=pl.BlockSpec(shape, lambda i, *_: (0, 0)),
            scratch_shapes=[pltpu.SemaphoreType.DMA((len(pieces),))],
        ),
        compiler_params=pltpu.CompilerParams(vmem_limit_bytes=24 * 2**20),
        cost_estimate=pl.CostEstimate(flops=0, bytes_accessed=4 * len(pieces) * extent * width, transcendentals=0),
    )(jnp.reshape(code, (1,)).astype(jnp.int32), *pieces)


def pack_weights_kernel(code_ref, near_ref, far_ref, *refs):
    out_ref = refs[-1]
    units = near_ref.shape[1] // 2
    out_ref[:, :units] = near_ref[:, :units]
    out_ref[:, units : 2 * units] = far_ref[:, :units]
    out_ref[:, 2 * units : 3 * units] = near_ref[:, units:]
    out_ref[:, 3 * units : 4 * units] = far_ref[:, units:]
    width = refs[0].shape[1]
    for k, ref in enumerate(refs[:-1]):
        place = pl.multiple_of(4 * units + (code_ref[0] ^ k) * width, width)
        out_ref[:, pl.ds(place, width)] = ref[...]


def pack_weights(near, far, outs, code):
    extent, units = near.shape
    width = outs[0].shape[1]
    columns = 2 * units + len(outs) * width
    whole = lambda shape: pl.BlockSpec(shape, lambda i, *_: (0, 0))
    return pl.pallas_call(
        pack_weights_kernel,
        name="pack_weights",
        out_shape=jax.ShapeDtypeStruct((extent, columns), near.dtype),
        grid_spec=pltpu.PrefetchScalarGridSpec(
            num_scalar_prefetch=1,
            grid=(1,),
            in_specs=[whole((extent, units))] * 2 + [whole((extent, width)) for _ in outs],
            out_specs=whole((extent, columns)),
        ),
        compiler_params=pltpu.CompilerParams(vmem_limit_bytes=24 * 2**20),
        cost_estimate=pl.CostEstimate(flops=0, bytes_accessed=4 * extent * columns, transcendentals=0),
    )(jnp.reshape(code, (1,)).astype(jnp.int32), near, far, *outs)


def row_device(
    first_half,
    second_half,
    first_cotangent,
    second_cotangent,
    segment_ids,
    bucket_ids,
    positions,
    query_weight,
    value_weight,
    output_weight,
    expand_weight,
    expand_bias,
    shrink_weight,
    shrink_bias,
    attention_gain,
    attention_shift,
    forward_gain,
    forward_shift,
):
    bf16, f32 = jnp.bfloat16, jnp.float32
    planes = lax.axis_size("tp")
    shard, ctx, plane = where_am_i()
    seqs_here, width = first_half.shape[1:]
    units = expand_bias.shape[0]
    split = query_weight.shape[0]

    local_pair = jnp.stack(
        [query_weight.reshape(split, -1, DH), value_weight.reshape(split, -1, DH)], 2
    ).reshape(split, -1)
    pair_parts = core_parts(local_pair)
    pair_rows = pair_parts.shape[1] * pair_parts.shape[2] // width
    biases = split_bias(jnp.concatenate([expand_bias, shrink_bias])).reshape(-1, width)
    bias_rows = biases.shape[0]
    biases = jnp.pad(biases, ((0, -bias_rows % 16), (0, 0)))
    extra = jnp.concatenate(
        [pair_parts.reshape(-1, pair_rows, width), jnp.stack([biases] * pair_parts.shape[0])], 1
    )
    (second_rows,), _, extras = rows_in(second_half[None], (), extra)
    biases = extras[:, pair_rows : pair_rows + bias_rows].astype(f32).reshape(planes, 3, -1)
    biases = (biases[:, 0] + biases[:, 1]) + biases[:, 2]
    unit_bias = jnp.concatenate(
        [
            lax.dynamic_index_in_dim(biases, plane, 0, False)[:units],
            lax.dynamic_index_in_dim(biases, plane ^ 2, 0, False)[:units],
        ]
    )
    row_bias = biases[:, units:].reshape(-1)

    pair_wide = extras[:, :pair_rows].reshape((planes,) + pair_parts.shape[1:]).transpose(1, 0, 2)
    pair_wide = plain(pair_wide.reshape(pair_parts.shape[1], -1))
    up, down, out = (
        quarter_of(item, ctx) for item in (expand_weight, shrink_weight.T, output_weight.T)
    )
    quarters = lax.axis_size("ctx")
    pair_pieces, (normed, attn_scaled, attn_inverse), labels, stacked = lax.optimization_barrier(
        (
            [swap(pair_wide, "ctx", j) for j in range(1, quarters)],
            norm_rows(second_rows.astype(f32), attention_gain, attention_shift),
            plane_labels(*after((segment_ids, bucket_ids, positions), second_rows)),
            jnp.stack([first_half, second_cotangent]),
        )
    )
    places, segments, buckets = labels
    normed = normed.astype(bf16)
    pair_mine = pack_rows([pair_wide] + pair_pieces, ctx)
    pair_other = swap(pair_mine, "shard", 1)
    pair = (
        dot(shard_half(normed, shard), pair_mine, NN)
        + dot(shard_half(normed, 1 - shard), pair_other, NN)
    ).astype(bf16)
    sent, out = after((plain(jnp.concatenate([up, down], 1)), plain(out)), pair_mine)
    landed, far, outs_near, hot, bounds = lax.optimization_barrier(
        (
            heads_out(pair),
            swap(sent, "tp", 2),
            [swap(out, "tp", k) for k in range(1, planes)],
            into_places(places, bucket_hot(buckets)),
            doc_bounds(segments),
        )
    )
    wide = pack_weights(sent, far, [out] + outs_near, plane)
    whole = lax.all_gather(after(wide, landed), ("shard", "ctx"), axis=0, tiled=True)
    up_full, down_full, output_full = (
        whole[:, : 2 * units],
        whole[:, 2 * units : 4 * units],
        whole[:, 4 * units :],
    )

    sorted_pair = into_places(places, landed)
    query_sorted, value_sorted = sorted_pair[:, :DH], sorted_pair[:, DH:]
    bounds = with_bound(bounds, query_sorted)
    (first_rows, second_grad_rows), (mix, logs) = rows_in(
        after(stacked, landed),
        attend(bounds, query_sorted, value_sorted, hot),
    )
    far_grad_rows = swap(after(second_grad_rows, mix), "tp", 1)
    attention = heads_back(out_of_places(places, mix.T.astype(bf16)))

    first_out = (first_rows.astype(f32) + dot(attention, output_full, NT)).astype(bf16)
    ffn_in, ffn_scaled, ffn_inverse = norm_rows(first_out.astype(f32), forward_gain, forward_shift)
    ffn_in, far_grad_rows = lax.optimization_barrier((ffn_in.astype(bf16), far_grad_rows))

    def units_of(rows, grad_rows):
        pre_act = dot(rows, up_full, NN) + unit_bias
        below = 0.5 * (1.0 + lax.erf(pre_act * 2**-0.5))
        slope = below + pre_act * (jnp.exp(-0.5 * pre_act * pre_act) * (2 * jnp.pi) ** -0.5)
        pre_grad = (dot(grad_rows, down_full, NN) * slope).astype(bf16)
        return (pre_act * below).astype(bf16), pre_grad

    normed_all = lax.all_gather(after(normed, first_out), ("ctx", "shard"), axis=0, tiled=True)
    far_in, (hidden, pre_grad) = lax.optimization_barrier(
        (swap(ffn_in, "tp", 1), units_of(ffn_in, second_grad_rows))
    )
    (first_grad_rows,), (far_hidden, far_pre_grad) = rows_in(
        after(first_cotangent, far_in)[None], units_of(far_in, far_grad_rows)
    )
    far_ffn_grad = dot(far_pre_grad, up_full, NT).astype(bf16)
    all_rows = jnp.concatenate([ffn_in, far_in], 0)
    all_grad_rows = jnp.concatenate([second_grad_rows, far_grad_rows], 0)
    all_pre_grad = jnp.concatenate([pre_grad, far_pre_grad], 0)
    all_hidden = jnp.concatenate([hidden, far_hidden], 0)
    all_rows, all_grad_rows, pre_grad = after((all_rows, all_grad_rows, pre_grad), far_ffn_grad)
    theirs, far_branch, own_branch, ffn_grad, expand_sums, shrink_sums = lax.optimization_barrier(
        (
            swap(far_ffn_grad, "tp", 1),
            dot(far_hidden, down_full, NT).astype(bf16),
            second_rows.astype(f32) + dot(hidden, down_full, NT) + row_bias,
            dot(pre_grad, up_full, NT),
            chip_sums(all_rows, all_pre_grad).astype(bf16),
            chip_sums(all_grad_rows, all_hidden).astype(bf16),
        )
    )
    ffn_back, ffn_gain_grad, ffn_shift_grad = row_norm_back(
        ffn_grad + theirs.astype(f32), ffn_scaled, ffn_inverse, forward_gain
    )
    first_grad = (first_grad_rows.astype(f32) + ffn_back).astype(bf16)
    attention_grad = dot(first_grad, output_full, NN).astype(bf16)
    shrink_bias_grad = jnp.sum(second_grad_rows.astype(f32), 0)
    expand_bias_grad = jnp.sum(all_pre_grad.astype(f32), 0)
    far_branch = swap(far_branch, "tp", 1)

    spread = jnp.arange(planes, dtype=jnp.int32)[:, None]
    unit_grads = jnp.where(spread == plane, expand_bias_grad[None, :units], 0.0)
    unit_grads = jnp.where(spread == plane ^ 2, expand_bias_grad[None, units:], unit_grads)
    packed = jnp.concatenate(
        [unit_grads]
        + [item.reshape(planes, width) for item in (shrink_bias_grad, ffn_gain_grad, ffn_shift_grad)],
        1,
    )
    packed = (packed + swap(packed, "shard", 1)).astype(bf16).reshape(planes, quarters, -1)
    vector_width = packed.shape[2]
    packed = jnp.pad(packed, ((0, 0), (0, 0), (0, 16 * width - vector_width)))
    packed = packed.reshape(planes, quarters, 16, width).transpose(1, 2, 0, 3)
    packed = jnp.pad(packed.reshape(quarters, 16, -1), ((0, 0), (0, 0), (4 * units, 0)))
    early = jnp.concatenate(
        [expand_sums, shrink_sums, chip_sums(first_grad, attention).astype(bf16)], 1
    )
    early = jnp.concatenate([early.reshape(quarters, split // quarters, -1), packed], 1)
    early = early.reshape(-1, early.shape[2])
    grad_heads, early, normed_all = lax.optimization_barrier(
        (heads_out(attention_grad), early, normed_all)
    )
    early_mine = lax.psum_scatter(early, "ctx", scatter_dimension=0, tiled=True)
    outs_sliced, parts = rows_out(
        after(jnp.stack([first_out, first_grad]), grad_heads),
        seqs_here,
        attend_back(
            bounds, query_sorted, value_sorted, hot, into_places(places, grad_heads), mix, logs
        ),
    )
    far_branch, own_branch = after((far_branch, own_branch), parts)
    second_out = (own_branch + far_branch.astype(f32)).astype(bf16)
    def with_far(pair_grad_heads):
        sums = after(early_mine, pair_grad_heads)
        held = sums[: split // quarters]
        far = jnp.concatenate([held[:, units : 2 * units], held[:, 3 * units : 4 * units]], 1)
        pair_sums = lax.dot_general(
            normed_all, pair_grad_heads, (((0,), (0,)), ((), ())), preferred_element_type=f32
        ).astype(bf16)
        late = sums[:, 4 * units :].reshape(-1, planes, width).transpose(1, 0, 2)
        late = jnp.concatenate([pair_sums.reshape(planes, -1, 2 * DH), late], 1)
        return late, sums, heads_back(pair_grad_heads), swap(far, "tp", 2)

    second_out_sliced, (late, early_mine, pair_grad, far_sums) = rows_out(
        second_out[None],
        seqs_here,
        out_of_places(places, jnp.concatenate(parts, 1)),
        with_far,
    )
    held = early_mine[: split // quarters]
    near_sums = jnp.concatenate([held[:, :units], held[:, 2 * units : 3 * units]], 1)

    grad_mine, grad_other = dot(pair_grad, pair_mine, NT), dot(pair_grad, pair_other, NT)
    normed_grad = jnp.concatenate(
        [
            jnp.where(shard == 0, grad_mine, grad_other),
            jnp.where(shard == 0, grad_other, grad_mine),
        ],
        1,
    )
    attn_back, attn_gain_grad, attn_shift_grad = row_norm_back(
        normed_grad, attn_scaled, attn_inverse, attention_gain
    )
    second_grad = (second_grad_rows.astype(f32) + attn_back).astype(bf16)

    early_own = (near_sums.astype(f32) + far_sums.astype(f32)).astype(bf16)
    pieces = [swap(plane_part(late, k), "tp", k) for k in range(1, planes)]
    late = sum((piece.astype(f32) for piece in pieces), plane_part(late, 0).astype(f32)).astype(bf16)
    split_at = width
    turned = lax.ppermute(
        late[:split_at],
        ("ctx", "tp"),
        [(at * planes + to, to * planes + at) for at in range(quarters) for to in range(planes)],
    )
    norm_grads = jnp.concatenate(
        [attn_gain_grad.reshape(planes, width), attn_shift_grad.reshape(planes, width)], 1
    )
    second_grad_sliced, (early_pieces, turned, norm_pieces) = rows_out(
        second_grad[None],
        seqs_here,
        (
            [swap(early_own, "ctx", j) for j in range(1, quarters)],
            turned,
            [swap(plane_part(norm_grads, k), "tp", k) for k in range(1, planes)],
        ),
    )
    early_own = pack_rows([early_own] + early_pieces, ctx).astype(f32)
    expand_own, shrink_own = early_own[:, :units], early_own[:, units:].T
    norm_own = sum_in_plane(sum(norm_pieces, plane_part(norm_grads, 0))).reshape(2, width)
    late_own = collect_ctx(jnp.concatenate([turned, late[split_at:]], 0)[None])
    pair_head = late_own[:, :split_at].reshape(-1, width)
    late_own = late_own[:, split_at:].astype(f32)
    output_own = late_own[:, : split // quarters].reshape(split, width).T
    owned = late_own[:, split // quarters :].reshape(quarters, -1)[:, :vector_width].reshape(-1)
    row_own = owned[units:].reshape(3, width)
    near = lax.dynamic_slice_in_dim(pair_head, shard * split, split, 0)
    other = swap(lax.dynamic_slice_in_dim(pair_head, (1 - shard) * split, split, 0), "shard", 1)
    pair_own = by_half(near, other).astype(f32)
    query_own = jnp.concatenate([pair_own[0, :, :DH], pair_own[1, :, :DH]], 1)
    value_own = jnp.concatenate([pair_own[0, :, DH:], pair_own[1, :, DH:]], 1)

    return (
        outs_sliced[0],
        second_out_sliced[0],
        outs_sliced[1],
        second_grad_sliced[0],
        query_own,
        value_own,
        output_own,
        expand_own,
        owned[:units],
        shrink_own,
        row_own[0],
        norm_own[0],
        norm_own[1],
        row_own[1],
        row_own[2],
    )


def row_planes(mesh):
    sizes = mesh.shape
    return sizes["tp"] == SEQS and sizes["shard"] == 2 and sizes["ctx"] == 4 and HEADS == 8


def solution(mesh):
    return jax.shard_map(
        row_device if row_planes(mesh) else general_device,
        mesh=mesh,
        in_specs=(
            P("ctx", "shard", "tp"),
            P("ctx", "shard", "tp"),
            P("ctx", "shard", "tp"),
            P("ctx", "shard", "tp"),
            P("shard", "ctx"),
            P("shard", None, "ctx"),
            P("shard", "ctx"),
            P("shard", "tp"),
            P("shard", "tp"),
            P("tp", "shard"),
            P("shard", "tp"),
            P("tp"),
            P("tp", "shard"),
            P("tp"),
            P(),
            P(),
            P(),
            P(),
        ),
        out_specs=(
            P("ctx", "shard", "tp"),
            P("ctx", "shard", "tp"),
            P("ctx", "shard", "tp"),
            P("ctx", "shard", "tp"),
            P("shard", "tp"),
            P("shard", "tp"),
            P("tp", "shard"),
            P("shard", "tp"),
            P("tp"),
            P("tp", "shard"),
            P("tp"),
            P("tp"),
            P("tp"),
            P("tp"),
            P("tp"),
        ),
        check_vma=False,
    )
```

```python
import jax
import jax.numpy as jnp
from jax import lax
from jax.experimental import pallas as pl
from jax.experimental.layout import Layout, with_layout_constraint
from jax.experimental.pallas import tpu as pltpu
from jax.sharding import PartitionSpec as P

D = 1024
DH = 128
ROUNDS = 4


SELF_SCORE = -10.0
NEG_FILL = -1e30
BLOCK_ROWS = 512


BUCKETS = 64
HEADS = 8
SEQS = 4
TILE = 512
GROUP = 1
BOUND = 38.0
NT = (((1,), (1,)), ((), ()))
NN = (((1,), (0,)), ((), ()))


def dot(left, right, dims):
    return lax.dot_general(left, right, dims, preferred_element_type=jnp.float32)


def start_of(place, bounds_ref):
    start = jnp.where(place >= bounds_ref[0], bounds_ref[0], 0)
    start = jnp.where(place >= bounds_ref[1], bounds_ref[1], start)
    return jnp.where(place >= bounds_ref[2], bounds_ref[2], start)


def tile_masks(begin_row, bounds_ref):
    query_lane = lax.broadcasted_iota(jnp.int32, (1, TILE), 1)
    doc_start = start_of(query_lane + begin_row, bounds_ref)
    first = start_of(begin_row, bounds_ref) // TILE
    last_start = start_of(begin_row + TILE - 1, bounds_ref)
    full = jnp.minimum((last_start + TILE - 1) // TILE, begin_row // TILE)
    return doc_start, first, full


def rows_at(ref, block, tiles=1):
    return ref[pl.ds(pl.multiple_of(block * TILE, TILE), tiles * TILE), :]


def norm_factor(q):
    return lax.rsqrt(jnp.mean(q * q, -1, keepdims=True) + 1e-06)


def attend_kernel(bounds_ref, q_ref, v_ref, hot_ref, out_ref, log_ref, key_sc, vt_sc):
    block = pl.program_id(0)
    blocks = pl.num_programs(0)

    @pl.when(block == 0)
    def _():
        def prep(at, carry):
            q = rows_at(q_ref, at).astype(jnp.float32)
            begin = pl.multiple_of(at * TILE, TILE)
            key_sc[pl.ds(begin, TILE), :] = (q * (norm_factor(q) * DH ** (-0.5))).astype(jnp.bfloat16)
            v = rows_at(v_ref, at).astype(jnp.float32)
            vt_sc[:, pl.ds(begin, TILE)] = v.T.astype(jnp.bfloat16)
            return carry

        lax.fori_loop(0, blocks, prep, 0)

    begin_row = block * TILE
    doc_start, first, full = tile_masks(begin_row, bounds_ref)
    q = rows_at(q_ref, block)
    hot = rows_at(hot_ref, block)
    key_row = lax.broadcasted_iota(jnp.int32, (TILE, 1), 0)
    lane = lax.broadcasted_iota(jnp.int32, (1, TILE), 1)

    def scores(at, tiles):
        return dot(rows_at(key_sc, at, tiles), q, NT), dot(rows_at(hot_ref, at, tiles), hot, NT)

    def vt(at, tiles):
        return vt_sc[:, pl.ds(pl.multiple_of(at * TILE, TILE), tiles * TILE)]

    itself = key_row == lane

    def diagonal():
        s, c = scores(block, 1)
        c = jnp.where((key_row < lane) & (key_row + begin_row >= doc_start), c, 0.0)
        return jnp.where(itself, SELF_SCORE, s), jnp.where(itself, float(ROUNDS), c)

    def in_document(c, at):
        return jnp.where(key_row + at * TILE >= doc_start, c, 0.0)

    def mixed(at, tiles, p):
        return dot(vt(at, tiles), p.astype(jnp.bfloat16), NN)

    @pl.when(bounds_ref[3] == 1)
    def _():
        def fold(at, tiles, carry, masked):
            total, acc = carry
            s, c = scores(at, tiles)
            if masked:
                c = in_document(c, at)
            p = c * jnp.exp(s)
            return total + jnp.sum(p, 0, keepdims=True), acc + mixed(at, tiles, p)

        s, c = diagonal()
        p = c * jnp.exp(s)
        carry = jnp.sum(p, 0, keepdims=True), mixed(block, 1, p)
        carry = lax.fori_loop(first, full, lambda at, x: fold(at, 1, x, True), carry)
        rest = (block - full) % GROUP
        carry = lax.fori_loop(full, full + rest, lambda at, x: fold(at, 1, x, False), carry)
        total, acc = lax.fori_loop(
            0,
            (block - full) // GROUP,
            lambda at, x: fold(full + rest + GROUP * at, GROUP, x, False),
            carry,
        )
        out_ref[...] = acc / total
        log_ref[pl.ds(block, 1), :] = jnp.log(total)

    @pl.when(bounds_ref[3] == 0)
    def _():
        def fold(at, carry):
            high, total, acc = carry
            s, c = scores(at, 1)
            c = in_document(c, at)
            s = jnp.where(c > 0, s, NEG_FILL)
            new_high = jnp.maximum(high, jnp.max(s, 0, keepdims=True))
            fade = jnp.exp(high - new_high)
            p = c * jnp.exp(s - new_high)
            total = total * fade + jnp.sum(p, 0, keepdims=True)
            return new_high, total, acc * fade + mixed(at, 1, p)

        s, c = diagonal()
        s = jnp.where(c > 0, s, NEG_FILL)
        high = jnp.max(s, 0, keepdims=True)
        p = c * jnp.exp(s - high)
        carry = high, jnp.sum(p, 0, keepdims=True), mixed(block, 1, p)
        high, total, acc = lax.fori_loop(first, block, fold, carry)
        out_ref[...] = acc / total
        log_ref[pl.ds(block, 1), :] = high + jnp.log(total)


def attend(bounds, q, v, hot):
    rows = q.shape[0]
    blocks = rows // TILE
    whole = lambda shape: pl.BlockSpec(shape, lambda i, *_: (0,) * len(shape))
    return pl.pallas_call(
        attend_kernel,
        name="attend",
        out_shape=(
            jax.ShapeDtypeStruct((DH, rows), jnp.float32),
            jax.ShapeDtypeStruct((blocks, TILE), jnp.float32),
        ),
        grid_spec=pltpu.PrefetchScalarGridSpec(
            num_scalar_prefetch=1,
            grid=(blocks,),
            in_specs=[whole((rows, DH)), whole((rows, DH)), whole((rows, ROUNDS * BUCKETS))],
            out_specs=[pl.BlockSpec((DH, TILE), lambda i, *_: (0, i)), whole((blocks, TILE))],
            scratch_shapes=[pltpu.VMEM((rows, DH), jnp.bfloat16), pltpu.VMEM((DH, rows), jnp.bfloat16)],
        ),
        compiler_params=pltpu.CompilerParams(
            dimension_semantics=("arbitrary",), vmem_limit_bytes=40 * 2**20
        ),
        cost_estimate=pl.CostEstimate(
            flops=rows * DH, bytes_accessed=rows * DH, transcendentals=0
        ),
    )(bounds, q, v, hot)


def attend_back_kernel(
    bounds_ref, q_ref, v_ref, hot_ref, grad_ref, out_ref, log_ref,
    q_grad_ref, v_grad_ref, key_sc, kt_sc, dk_sc, dv_sc, dq_sc,
):
    block = pl.program_id(0)
    blocks = pl.num_programs(0)

    @pl.when(block == 0)
    def _():
        def prep(at, carry):
            begin = pl.multiple_of(at * TILE, TILE)
            q = rows_at(q_ref, at).astype(jnp.float32)
            k = q * (norm_factor(q) * DH ** (-0.5))
            key_sc[pl.ds(begin, TILE), :] = k.astype(jnp.bfloat16)
            kt_sc[:, pl.ds(begin, TILE)] = k.T.astype(jnp.bfloat16)
            dk_sc[pl.ds(begin, TILE), :] = jnp.zeros((TILE, DH), jnp.float32)
            dv_sc[pl.ds(begin, TILE), :] = jnp.zeros((TILE, DH), jnp.float32)
            return carry

        lax.fori_loop(0, blocks, prep, 0)

    begin_row = block * TILE
    doc_start, first, full = tile_masks(begin_row, bounds_ref)
    q = rows_at(q_ref, block)
    hot = rows_at(hot_ref, block)
    grad = rows_at(grad_ref, block)
    log_row = log_ref[pl.ds(block, 1), :]
    delta = jnp.sum(grad.astype(jnp.float32).T * out_ref[...], 0, keepdims=True)
    key_row = lax.broadcasted_iota(jnp.int32, (TILE, 1), 0)
    lane = lax.broadcasted_iota(jnp.int32, (1, TILE), 1)

    itself = key_row == lane

    def fold(at, tiles, acc, masked, bounded, diagonal=False):
        rows = pl.ds(pl.multiple_of(at * TILE, TILE), tiles * TILE)
        s = dot(key_sc[rows, :], q, NT)
        c = dot(hot_ref[rows, :], hot, NT)
        up = dot(v_ref[rows, :], grad, NT)
        if diagonal:
            c = jnp.where((key_row < lane) & (key_row + begin_row >= doc_start), c, 0.0)
            c = jnp.where(itself, float(ROUNDS), c)
            s = jnp.where(itself, SELF_SCORE, s)
        elif masked:
            c = jnp.where(key_row + at * TILE >= doc_start, c, 0.0)
        if not bounded:
            s = jnp.where(c > 0, s, NEG_FILL)
        w = c * jnp.exp(s - log_row)
        ds = w * (up - delta)
        if diagonal:
            ds = jnp.where(itself, 0.0, ds)
        w = w.astype(jnp.bfloat16)
        ds = ds.astype(jnp.bfloat16)
        dv_sc[rows, :] += dot(w, grad, NN)
        dk_sc[rows, :] += dot(ds, q, NN)
        return acc + dot(kt_sc[:, rows], ds, NN)

    def store(acc):
        dq_sc[pl.ds(pl.multiple_of(begin_row, TILE), TILE), :] = acc.T

    nothing = jnp.zeros((DH, TILE), jnp.float32)

    @pl.when(bounds_ref[3] == 1)
    def _():
        acc = fold(block, 1, nothing, True, True, True)
        acc = lax.fori_loop(first, full, lambda at, x: fold(at, 1, x, True, True), acc)
        rest = (block - full) % GROUP
        acc = lax.fori_loop(full, full + rest, lambda at, x: fold(at, 1, x, False, True), acc)
        store(
            lax.fori_loop(
                0,
                (block - full) // GROUP,
                lambda at, x: fold(full + rest + GROUP * at, GROUP, x, False, True),
                acc,
            )
        )

    @pl.when(bounds_ref[3] == 0)
    def _():
        acc = fold(block, 1, nothing, True, False, True)
        store(lax.fori_loop(first, block, lambda at, x: fold(at, 1, x, True, False), acc))

    @pl.when(block == blocks - 1)
    def _():
        def finish(at, carry):
            begin = pl.multiple_of(at * TILE, TILE)
            q = rows_at(q_ref, at).astype(jnp.float32)
            r = norm_factor(q)
            g = rows_at(dk_sc, at).astype(jnp.bfloat16).astype(jnp.float32)
            back = (r * DH ** (-0.5)) * (g - q * (r * r * jnp.mean(q * g, -1, keepdims=True)))
            q_grad_ref[pl.ds(begin, TILE), :] = (rows_at(dq_sc, at) + back).astype(jnp.bfloat16)
            v_grad_ref[pl.ds(begin, TILE), :] = rows_at(dv_sc, at).astype(jnp.bfloat16)
            return carry

        lax.fori_loop(0, blocks, finish, 0)


def attend_back(bounds, q, v, hot, grad, out, logs):
    rows = q.shape[0]
    blocks = rows // TILE
    whole = lambda shape: pl.BlockSpec(shape, lambda i, *_: (0,) * len(shape))
    return pl.pallas_call(
        attend_back_kernel,
        name="attend_back",
        out_shape=(jax.ShapeDtypeStruct((rows, DH), jnp.bfloat16),) * 2,
        grid_spec=pltpu.PrefetchScalarGridSpec(
            num_scalar_prefetch=1,
            grid=(blocks,),
            in_specs=[
                whole((rows, DH)), whole((rows, DH)), whole((rows, ROUNDS * BUCKETS)), whole((rows, DH)),
                pl.BlockSpec((DH, TILE), lambda i, *_: (0, i)), whole((blocks, TILE)),
            ],
            out_specs=[whole((rows, DH))] * 2,
            scratch_shapes=[
                pltpu.VMEM((rows, DH), jnp.bfloat16),
                pltpu.VMEM((DH, rows), jnp.bfloat16),
                pltpu.VMEM((rows, DH), jnp.float32),
                pltpu.VMEM((rows, DH), jnp.float32),
                pltpu.VMEM((rows, DH), jnp.float32),
            ],
        ),
        compiler_params=pltpu.CompilerParams(
            dimension_semantics=("arbitrary",), vmem_limit_bytes=48 * 2**20
        ),
        cost_estimate=pl.CostEstimate(
            flops=rows * DH, bytes_accessed=rows * DH, transcendentals=0
        ),
    )(bounds, q, v, hot, grad, out, logs)


def place_matrix(places):
    rows = places.shape[0]
    return (jnp.arange(rows, dtype=jnp.int32)[:, None] == places[None, :]).astype(jnp.bfloat16)


def into_places(places, vectors):
    return jnp.einsum("pa,ad->pd", place_matrix(places), vectors, preferred_element_type=jnp.float32).astype(jnp.bfloat16)


def out_of_places(places, vectors):
    rows = places.shape[0]
    picks = (places[:, None] == jnp.arange(rows, dtype=jnp.int32)[None, :]).astype(jnp.bfloat16)
    return dot(picks, vectors, NN).astype(jnp.bfloat16)


def bucket_hot(buckets):
    hot = buckets.T[:, :, None] == jnp.arange(BUCKETS, dtype=jnp.int32)
    return hot.astype(jnp.bfloat16).reshape(buckets.shape[1], ROUNDS * BUCKETS)


def doc_bounds(segments):
    return jnp.sum((segments[None, :] < jnp.arange(1, 4, dtype=jnp.int32)[:, None]).astype(jnp.int32), 1)


def with_bound(bounds, queries):
    squares = jnp.sum(queries.astype(jnp.float32) ** 2, -1)
    return jnp.concatenate([bounds, (jnp.max(squares) <= BOUND**2).astype(jnp.int32)[None]])


def smooth_unit(values_in):
    return jax.nn.gelu(values_in, approximate=False)


def norm_rows(rows_wide, gain_row, shift_row):
    centre = jnp.mean(rows_wide, -1, keepdims=True)
    offset = rows_wide - centre
    inverse = lax.rsqrt(jnp.mean(offset * offset, -1, keepdims=True) + 1e-05)
    scaled = offset * inverse
    return (scaled * gain_row + shift_row, scaled, inverse)


def unit_keys(queries):
    shaped = queries.reshape(queries.shape[:-1] + (queries.shape[-1] // DH, DH))
    factor = lax.rsqrt(jnp.mean(shaped * shaped, -1, keepdims=True) + 1e-06) * DH ** (-0.5)
    return (shaped * factor).reshape(queries.shape)


def heads_view(vectors):
    return vectors.reshape(vectors.shape[0], vectors.shape[1], vectors.shape[2] // DH, DH)


def full_rows(sliced):
    return lax.all_gather(sliced, "tp", axis=2, tiled=True)


def branch_sum(partial_value):
    return lax.psum_scatter(partial_value, "tp", scatter_dimension=2, tiled=True)


def norm_back(grad_slice, scaled_slice, inverse, gain_slice):
    weighted = grad_slice * gain_slice
    first_sum, second_sum = lax.psum(
        (jnp.sum(weighted, -1, keepdims=True), jnp.sum(weighted * scaled_slice, -1, keepdims=True)),
        "tp",
    )
    inner = inverse * (weighted - first_sum / D - scaled_slice * (second_sum / D))
    return (inner, jnp.sum(grad_slice * scaled_slice, (0, 1)), jnp.sum(grad_slice, (0, 1)))


def label_rows(all_labels, begin_row, extent):
    all_segments, all_buckets, all_positions = all_labels
    return (
        lax.dynamic_slice_in_dim(all_segments, begin_row, extent, 1),
        lax.dynamic_slice_in_dim(all_buckets, begin_row, extent, 2),
        lax.dynamic_slice_in_dim(all_positions, begin_row, extent, 1),
    )


def block_weights(query_heads, query_labels, key_heads, key_labels):
    query_seg, query_buck, query_pos = query_labels
    key_seg, key_buck, key_pos = key_labels
    scores = jnp.einsum(
        "pshd,kshd->shpk", query_heads, key_heads, preferred_element_type=jnp.float32
    )
    matches = jnp.sum((query_buck[:, :, :, None] == key_buck[:, :, None, :]).astype(jnp.int32), 1)
    same_doc = query_seg[:, :, None] == key_seg[:, None, :]
    earlier = key_pos[:, None, :] < query_pos[:, :, None]
    itself = key_pos[:, None, :] == query_pos[:, :, None]
    counts = jnp.where(itself, ROUNDS, jnp.where(earlier & same_doc, matches, 0)).astype(
        jnp.float32
    )[:, None]
    shifted = jnp.where(itself[:, None], SELF_SCORE, scores)
    return (shifted, counts, itself[:, None])


def weights_of(shifted, counts, log_total):
    return jnp.where(counts > 0, counts * jnp.exp(shifted - log_total[..., None]), 0.0)


def blockwise(advance, running, row_count):
    extent = BLOCK_ROWS

    def turn(state_now, block_index):
        return (advance(state_now, block_index * extent, extent), None)

    return lax.scan(turn, running, jnp.arange(row_count // extent, dtype=jnp.int32))[0]


def over_keys(key_vectors, value_vectors, folder, initial):
    return folder(
        initial,
        (
            lax.all_gather(key_vectors, "ctx", axis=0, tiled=True),
            lax.all_gather(value_vectors, "ctx", axis=0, tiled=True),
        ),
        jnp.int32(0),
    )


def over_context(first_part, second_part, third_part, fourth_part, fifth_part):
    return (
        lax.psum(first_part.astype(jnp.bfloat16), "ctx").astype(jnp.float32),
        lax.psum(second_part.astype(jnp.bfloat16), "ctx").astype(jnp.float32),
        lax.psum(third_part.astype(jnp.bfloat16), "ctx").astype(jnp.float32),
        lax.psum(fourth_part.astype(jnp.bfloat16), "ctx").astype(jnp.float32),
        lax.psum(fifth_part.astype(jnp.bfloat16), "ctx").astype(jnp.float32),
    )


def to_row_owners(first_part, second_part, third_part):
    return (
        lax.psum_scatter(
            first_part.astype(jnp.bfloat16), "shard", scatter_dimension=0, tiled=True
        ).astype(jnp.float32),
        lax.psum_scatter(
            second_part.astype(jnp.bfloat16), "shard", scatter_dimension=0, tiled=True
        ).astype(jnp.float32),
        lax.psum_scatter(
            third_part.astype(jnp.bfloat16), "shard", scatter_dimension=0, tiled=True
        ).astype(jnp.float32),
    )


def to_col_owners(first_part, second_part):
    return (
        lax.psum_scatter(
            first_part.astype(jnp.bfloat16), "shard", scatter_dimension=1, tiled=True
        ).astype(jnp.float32),
        lax.psum_scatter(
            second_part.astype(jnp.bfloat16), "shard", scatter_dimension=1, tiled=True
        ).astype(jnp.float32),
    )


def general_device(
    first_half,
    second_half,
    first_cotangent,
    second_cotangent,
    segment_ids,
    bucket_ids,
    positions,
    query_weight,
    value_weight,
    output_weight,
    expand_weight,
    expand_bias,
    shrink_weight,
    shrink_bias,
    attention_gain,
    attention_shift,
    forward_gain,
    forward_shift,
):
    rows_here, seqs_here, slice_width = first_half.shape
    width_heads = query_weight.shape[1]
    heads_here = width_heads // DH
    tp_start = lax.axis_index("tp") * slice_width
    ctx_start = lax.axis_index("ctx") * rows_here
    bf16 = jnp.bfloat16
    f32 = jnp.float32

    def columns(wide):
        return lax.dynamic_slice_in_dim(wide, tp_start, slice_width, wide.ndim - 1)

    full_query, full_value, full_expand = (
        lax.all_gather(query_weight, "shard", axis=0, tiled=True),
        lax.all_gather(value_weight, "shard", axis=0, tiled=True),
        lax.all_gather(expand_weight, "shard", axis=0, tiled=True),
    )
    full_output, full_shrink = (
        lax.all_gather(output_weight, "shard", axis=1, tiled=True),
        lax.all_gather(shrink_weight, "shard", axis=1, tiled=True),
    )
    all_labels = (
        lax.all_gather(segment_ids, "ctx", axis=1, tiled=True),
        lax.all_gather(bucket_ids, "ctx", axis=2, tiled=True),
        lax.all_gather(positions, "ctx", axis=1, tiled=True),
    )
    local_labels = label_rows(all_labels, ctx_start, rows_here)
    second_wide = full_rows(second_half)
    normed, attn_scaled, attn_inverse = norm_rows(
        second_wide.astype(f32), attention_gain, attention_shift
    )
    normed = normed.astype(bf16)
    queries = jnp.einsum("psd,de->pse", normed, full_query, preferred_element_type=f32).astype(bf16)
    key_vectors = unit_keys(queries.astype(f32)).astype(bf16)
    value_vectors = jnp.einsum(
        "psd,de->pse", normed, full_value, preferred_element_type=f32
    ).astype(bf16)
    query_heads = heads_view(queries)
    stat_shape = (seqs_here, heads_here, rows_here)
    head_zero = jnp.zeros((rows_here, seqs_here, heads_here, DH), f32)

    def norm_fold(running, pieces, begin_row):
        key_piece = pieces[0]

        def advance(state_now, offset, extent):
            highest, summed = state_now
            key_heads = heads_view(lax.dynamic_slice_in_dim(key_piece, offset, extent, 0))
            shifted, counts, _ = block_weights(
                query_heads, local_labels, key_heads, label_rows(all_labels, offset, extent)
            )
            usable = counts > 0
            new_high = jnp.maximum(highest, jnp.max(jnp.where(usable, shifted, NEG_FILL), -1))
            summed = summed * jnp.exp(highest - new_high) + jnp.sum(
                jnp.where(usable, counts * jnp.exp(shifted - new_high[..., None]), 0.0), -1
            )
            return (new_high, summed)

        return blockwise(advance, running, key_piece.shape[0])

    highest, summed = over_keys(
        key_vectors,
        value_vectors,
        norm_fold,
        (jnp.full(stat_shape, NEG_FILL, f32), jnp.zeros(stat_shape, f32)),
    )
    log_total = highest + jnp.log(summed)

    def key_block(pieces, offset, extent):
        key_heads = heads_view(lax.dynamic_slice_in_dim(pieces[0], offset, extent, 0))
        value_heads = heads_view(lax.dynamic_slice_in_dim(pieces[1], offset, extent, 0))
        shifted, counts, itself = block_weights(
            query_heads, local_labels, key_heads, label_rows(all_labels, offset, extent)
        )
        return (key_heads, value_heads, weights_of(shifted, counts, log_total), itself)

    def mix_fold(running, pieces, begin_row):

        def advance(state_now, offset, extent):
            key_heads, value_heads, weights, itself = key_block(pieces, offset, extent)
            return state_now + jnp.einsum(
                "shpk,kshd->pshd", weights.astype(bf16), value_heads, preferred_element_type=f32
            )

        return blockwise(advance, running, pieces[0].shape[0])

    head_mix = over_keys(key_vectors, value_vectors, mix_fold, head_zero)
    attention = head_mix.reshape(rows_here, seqs_here, width_heads).astype(bf16)
    branch = branch_sum(
        jnp.einsum("pse,ed->psd", attention, full_output, preferred_element_type=f32)
    )
    first_out = (first_half.astype(f32) + branch).astype(bf16)
    first_wide = full_rows(first_out)
    ffn_in, ffn_scaled, ffn_inverse = norm_rows(first_wide.astype(f32), forward_gain, forward_shift)
    ffn_in = ffn_in.astype(bf16)
    pre_act = (
        jnp.einsum("psd,df->psf", ffn_in, full_expand, preferred_element_type=f32) + expand_bias
    )
    hidden_exact, unit_pull = jax.vjp(smooth_unit, pre_act)
    hidden = hidden_exact.astype(bf16)
    second_branch = (
        branch_sum(jnp.einsum("psf,fd->psd", hidden, full_shrink, preferred_element_type=f32))
        + shrink_bias
    )
    second_out = (second_half.astype(f32) + second_branch).astype(bf16)
    cotangent_wide = full_rows(second_cotangent)
    hidden_grad = jnp.einsum("psd,fd->psf", cotangent_wide, full_shrink, preferred_element_type=f32)
    pre_grad = unit_pull(hidden_grad)[0].astype(bf16)
    shrink_grad = jnp.einsum("psf,psd->fd", hidden, cotangent_wide, preferred_element_type=f32)
    shrink_bias_grad = jnp.sum(second_cotangent.astype(f32), (0, 1))
    expand_grad = jnp.einsum("psd,psf->df", ffn_in, pre_grad, preferred_element_type=f32)
    expand_bias_grad = jnp.sum(pre_grad.astype(f32), (0, 1))
    ffn_grad = branch_sum(
        jnp.einsum("psf,df->psd", pre_grad, full_expand, preferred_element_type=f32)
    )
    ffn_back, forward_gain_grad, forward_shift_grad = norm_back(
        ffn_grad, columns(ffn_scaled), ffn_inverse, columns(forward_gain)
    )
    first_grad = (first_cotangent.astype(f32) + ffn_back).astype(bf16)
    grad_wide = full_rows(first_grad)
    output_grad = jnp.einsum("pse,psd->ed", attention, grad_wide, preferred_element_type=f32)
    attention_grad = jnp.einsum(
        "psd,ed->pse", grad_wide, full_output, preferred_element_type=f32
    ).astype(bf16)
    grad_heads = heads_view(attention_grad)

    def delta_fold(running, pieces, begin_row):

        def advance(state_now, offset, extent):
            key_heads, value_heads, weights, itself = key_block(pieces, offset, extent)
            upstream = jnp.einsum(
                "pshd,kshd->shpk", grad_heads, value_heads, preferred_element_type=f32
            )
            return state_now + jnp.sum(weights * upstream, -1)

        return blockwise(advance, running, pieces[0].shape[0])

    row_delta = over_keys(key_vectors, value_vectors, delta_fold, jnp.zeros(stat_shape, f32))

    def query_fold(running, pieces, begin_row):

        def advance(state_now, offset, extent):
            key_heads, value_heads, weights, itself = key_block(pieces, offset, extent)
            upstream = jnp.einsum(
                "pshd,kshd->shpk", grad_heads, value_heads, preferred_element_type=f32
            )
            score_grad = jnp.where(itself, 0.0, weights * (upstream - row_delta[..., None])).astype(
                bf16
            )
            return state_now + jnp.einsum(
                "shpk,kshd->pshd", score_grad, key_heads, preferred_element_type=f32
            )

        return blockwise(advance, running, pieces[0].shape[0])

    query_part = over_keys(key_vectors, value_vectors, query_fold, head_zero)
    query_lse, query_delta = (
        lax.all_gather(log_total, "ctx", axis=2, tiled=True),
        lax.all_gather(row_delta, "ctx", axis=2, tiled=True),
    )
    local_keys = heads_view(key_vectors)
    local_values = heads_view(value_vectors)
    query_piece = lax.all_gather(queries, "ctx", axis=0, tiled=True)
    grad_piece = lax.all_gather(attention_grad, "ctx", axis=0, tiled=True)

    def advance(state_now, offset, extent):
        remote_queries = heads_view(lax.dynamic_slice_in_dim(query_piece, offset, extent, 0))
        remote_grads = heads_view(lax.dynamic_slice_in_dim(grad_piece, offset, extent, 0))
        lse_rows = lax.dynamic_slice_in_dim(query_lse, offset, extent, 2)
        delta_rows = lax.dynamic_slice_in_dim(query_delta, offset, extent, 2)
        shifted, counts, itself = block_weights(
            remote_queries, label_rows(all_labels, offset, extent), local_keys, local_labels
        )
        weights = weights_of(shifted, counts, lse_rows)
        upstream = jnp.einsum(
            "pshd,kshd->shpk", remote_grads, local_values, preferred_element_type=f32
        )
        score_grad = jnp.where(itself, 0.0, weights * (upstream - delta_rows[..., None])).astype(
            bf16
        )
        key_now = state_now[0] + jnp.einsum(
            "shpk,pshd->kshd", score_grad, remote_queries, preferred_element_type=f32
        )
        value_now = state_now[1] + jnp.einsum(
            "shpk,pshd->kshd", weights.astype(bf16), remote_grads, preferred_element_type=f32
        )
        return (key_now, value_now)

    key_part, value_part = blockwise(advance, (head_zero, head_zero), query_piece.shape[0])
    keys_grad = key_part.reshape(rows_here, seqs_here, width_heads).astype(bf16)
    values_grad = value_part.reshape(rows_here, seqs_here, width_heads).astype(bf16)
    unit_back = jax.vjp(unit_keys, queries.astype(f32))[1]
    queries_total = (
        query_part.reshape(rows_here, seqs_here, width_heads) + unit_back(keys_grad.astype(f32))[0]
    ).astype(bf16)
    query_grad = jnp.einsum("psd,pse->de", normed, queries_total, preferred_element_type=f32)
    value_grad = jnp.einsum("psd,pse->de", normed, values_grad, preferred_element_type=f32)
    normed_grad = branch_sum(
        jnp.einsum("pse,de->psd", queries_total, full_query, preferred_element_type=f32)
        + jnp.einsum("pse,de->psd", values_grad, full_value, preferred_element_type=f32)
    )
    attn_back, attention_gain_grad, attention_shift_grad = norm_back(
        normed_grad, columns(attn_scaled), attn_inverse, columns(attention_gain)
    )
    second_grad = (second_cotangent.astype(f32) + attn_back).astype(bf16)
    expand_bias_sum, shrink_bias_sum, attn_gain_sum, attn_shift_sum, ffn_gain_sum, ffn_shift_sum = (
        lax.psum(
            (
                expand_bias_grad,
                shrink_bias_grad,
                attention_gain_grad,
                attention_shift_grad,
                forward_gain_grad,
                forward_shift_grad,
            ),
            ("shard", "ctx"),
        )
    )
    query_sum, value_sum, expand_sum, output_sum, shrink_sum = over_context(
        query_grad, value_grad, expand_grad, output_grad, shrink_grad
    )
    query_own, value_own, expand_own = to_row_owners(query_sum, value_sum, expand_sum)
    output_own, shrink_own = to_col_owners(output_sum, shrink_sum)
    return (
        first_out,
        second_out,
        first_grad,
        second_grad,
        query_own,
        value_own,
        output_own,
        expand_own,
        expand_bias_sum,
        shrink_own,
        shrink_bias_sum,
        attn_gain_sum,
        attn_shift_sum,
        ffn_gain_sum,
        ffn_shift_sum,
    )


def swap(vectors, axis, bits):
    size = lax.axis_size(axis)
    return lax.ppermute(vectors, axis, [(at, at ^ bits) for at in range(size)])


def where_am_i():
    return lax.axis_index("shard"), lax.axis_index("ctx"), lax.axis_index("tp")


def plane_pairs(step, inverse):
    shards, planes = lax.axis_size("shard"), lax.axis_size("tp")
    local_seqs = planes // shards
    pairs = []
    for shard in range(shards):
        for plane in range(planes):
            chunk = step ^ plane
            there = (chunk % shards) * planes + shard * local_seqs + chunk // shards
            here = shard * planes + plane
            pairs.append((there, here) if inverse else (here, there))
    return pairs


def rows_in(sliced, beside=(), extra=None):
    shard, _, plane = where_am_i()
    shards, planes = lax.axis_size("shard"), lax.axis_size("tp")
    count, slots, seqs, width = sliced.shape
    extent = slots // shards
    by_seq = sliced.transpose(2, 0, 1, 3).reshape(seqs, count, shards, extent, width)
    by_seq = by_seq.transpose(0, 2, 1, 3, 4).reshape(seqs * shards, count * extent, width)
    if extra is not None:
        by_seq = jnp.concatenate([by_seq, jnp.concatenate([extra] * seqs, 0)], 1)
    mine = (plane % seqs) * shards + shard
    landed = []
    for step in range(planes):
        chunk = lax.dynamic_index_in_dim(by_seq, step ^ plane, 0, False)
        landed.append(lax.ppermute(chunk, ("shard", "tp"), plane_pairs(step, False)))
    landed, beside = lax.optimization_barrier((landed, beside))
    whole = jnp.zeros((count * extent, planes * width), sliced.dtype)
    for step in range(planes):
        piece = landed[step][: count * extent]
        whole = lax.dynamic_update_slice_in_dim(whole, piece, (step ^ mine) * width, 1)
    whole = whole.reshape(count, extent, planes * width)
    if extra is None:
        return whole, beside
    extras = jnp.zeros((planes,) + extra.shape[1:], extra.dtype)
    for step in range(planes):
        piece = landed[step][None, count * extent :]
        extras = lax.dynamic_update_slice_in_dim(extras, piece, step ^ mine, 0)
    return whole, beside, extras


def rows_out(whole, seqs, beside=(), first=None):
    shard, _, plane = where_am_i()
    shards, planes = lax.axis_size("shard"), lax.axis_size("tp")
    count, extent, features = whole.shape
    width = features // planes
    mine = (plane % seqs) * shards + shard
    flat = whole.reshape(count * extent, features)

    def send(step):
        piece = lax.dynamic_slice_in_dim(flat, (step ^ mine) * width, width, 1)
        return lax.ppermute(piece, ("shard", "tp"), plane_pairs(step, True))

    half = planes // 2 if first is not None else 0
    landed = [send(step) for step in range(half)]
    if first is not None:
        landed, beside, flat = lax.optimization_barrier((landed, beside, flat))
        beside = first(beside)
    rest = [send(step) for step in range(half, planes)]
    rest, beside = lax.optimization_barrier((rest, beside))
    landed = landed + rest
    by_seq = jnp.zeros((seqs * shards, count * extent, width), whole.dtype)
    for step in range(planes):
        by_seq = lax.dynamic_update_slice_in_dim(by_seq, landed[step][None], step ^ plane, 0)
    parts = by_seq.reshape(seqs, shards, count, extent, width).transpose(2, 1, 3, 0, 4)
    return parts.reshape(count, shards * extent, seqs, width), beside


def quarter_of(local, at):
    extent = local.shape[0] // lax.axis_size("ctx")
    return lax.dynamic_slice_in_dim(local, at * extent, extent, 0)


def by_half(own, other):
    first = lax.axis_index("shard") == 0
    return jnp.stack([jnp.where(first, own, other), jnp.where(first, other, own)])


def plain(vectors):
    return with_layout_constraint(vectors, Layout(major_to_minor=tuple(range(vectors.ndim))))


def core_parts(local):
    mine = quarter_of(local, lax.axis_index("ctx"))
    return by_half(mine, swap(mine, "shard", 1))


def split_bias(values):
    high = values.astype(jnp.bfloat16)
    rest = values - high.astype(jnp.float32)
    middle = rest.astype(jnp.bfloat16)
    return jnp.stack([high, middle, (rest - middle.astype(jnp.float32)).astype(jnp.bfloat16)])


def shard_half(wide, at):
    extent = wide.shape[1] // 2
    return lax.dynamic_slice_in_dim(wide, at * extent, extent, 1)


def chip_sums(rows_wide, columns_wide):
    shard = lax.axis_index("shard")

    def product(at):
        return lax.dot_general(
            shard_half(rows_wide, at),
            columns_wide,
            (((0,), (0,)), ((), ())),
            preferred_element_type=jnp.float32,
        )

    theirs = swap(product(1 - shard).astype(jnp.bfloat16), "shard", 1)
    return product(shard) + theirs.astype(jnp.float32)


def sum_parts(parts):
    return jnp.sum(parts.astype(jnp.float32), 0)


def send_ctx(sums):
    quarters = lax.axis_size("ctx")
    parts = sums.reshape(quarters, sums.shape[0] // quarters, sums.shape[1])
    return lax.all_to_all(parts, "ctx", 0, 0, tiled=True)


def scatter_ctx(sums):
    return sum_parts(send_ctx(sums))


def scatter_tp(sums):
    planes = lax.axis_size("tp")
    parts = sums.reshape(sums.shape[0], planes, -1).transpose(1, 0, 2)
    return sum_parts(lax.all_to_all(parts, "tp", 0, 0, tiled=True))


def collect_ctx(quarter):
    quarters = lax.axis_size("ctx")
    return in_order([quarter] + [swap(quarter, "ctx", j) for j in range(1, quarters)])


def in_order(pieces):
    ctx, extent = lax.axis_index("ctx"), pieces[0].shape[0]
    whole = jnp.zeros((len(pieces) * extent,) + pieces[0].shape[1:], pieces[0].dtype)
    for j, piece in enumerate(pieces):
        whole = lax.dynamic_update_slice_in_dim(whole, piece, (ctx ^ j) * extent, 0)
    return whole


def reduce_context_first(sums):
    bf16 = jnp.bfloat16
    quarter = scatter_ctx(sums.astype(bf16)).astype(bf16)
    return collect_ctx(scatter_tp(quarter).astype(bf16)).astype(jnp.float32)


def plane_part(parts, k):
    return lax.dynamic_index_in_dim(parts, lax.axis_index("tp") ^ k, 0, False)


def sum_in_plane(total):
    total = total + swap(total, "shard", 1)
    return sum(swap(total, "ctx", j) for j in range(1, lax.axis_size("ctx"))) + total


def after(values, ready):
    return lax.optimization_barrier((values, ready))[0]


def row_norm_back(grad, scaled, inverse, gain):
    weighted = grad * gain
    first = jnp.mean(weighted, -1, keepdims=True)
    second = jnp.mean(weighted * scaled, -1, keepdims=True)
    inner = inverse * (weighted - first - scaled * second)
    return inner, jnp.sum(grad * scaled, 0), jnp.sum(grad, 0)


def heads_out(vectors):
    heads = HEADS
    sent = vectors.reshape(vectors.shape[0], heads, -1).transpose(1, 0, 2)
    landed = lax.all_to_all(sent, ("ctx", "shard"), split_axis=0, concat_axis=0, tiled=True)
    return landed.reshape(-1, landed.shape[2])


def heads_back(vectors):
    sent = vectors.reshape(HEADS, -1, vectors.shape[1])
    landed = lax.all_to_all(sent, ("ctx", "shard"), split_axis=0, concat_axis=0, tiled=True)
    return landed.transpose(1, 0, 2).reshape(landed.shape[1], -1)


def plane_labels(segment_ids, bucket_ids, positions):
    shard, _, plane = where_am_i()
    seqs, slots = positions.shape
    packed = jnp.concatenate([positions[:, None], segment_ids[:, None], bucket_ids], 1)
    kinds = packed.shape[1]
    mine = lax.dynamic_index_in_dim(packed, plane % seqs, 0, False).reshape(-1, 128)
    mine = jnp.where(shard == plane // seqs, mine, swap(mine, "shard", 1))
    whole = collect_ctx(mine).reshape(-1, kinds, slots).transpose(1, 0, 2).reshape(kinds, -1)
    return whole[0], whole[1], whole[2:]


def pack_rows_kernel(code_ref, *refs):
    pieces, out_ref, sems = refs[:-2], refs[-2], refs[-1]
    extent = pieces[0].shape[0]
    copies = []
    for j, ref in enumerate(pieces):
        place = pl.multiple_of((code_ref[0] ^ j) * extent, extent)
        copies.append(pltpu.make_async_copy(ref, out_ref.at[pl.ds(place, extent), :], sems.at[j]))
        copies[-1].start()
    for copy in copies:
        copy.wait()


def pack_rows(pieces, code):
    extent, width = pieces[0].shape
    shape = (len(pieces) * extent, width)
    return pl.pallas_call(
        pack_rows_kernel,
        name="pack_rows",
        out_shape=jax.ShapeDtypeStruct(shape, pieces[0].dtype),
        grid_spec=pltpu.PrefetchScalarGridSpec(
            num_scalar_prefetch=1,
            grid=(1,),
            in_specs=[pl.BlockSpec(memory_space=pl.ANY)] * len(pieces),
            out_specs=pl.BlockSpec(shape, lambda i, *_: (0, 0)),
            scratch_shapes=[pltpu.SemaphoreType.DMA((len(pieces),))],
        ),
        compiler_params=pltpu.CompilerParams(vmem_limit_bytes=24 * 2**20),
        cost_estimate=pl.CostEstimate(flops=0, bytes_accessed=4 * len(pieces) * extent * width, transcendentals=0),
    )(jnp.reshape(code, (1,)).astype(jnp.int32), *pieces)


def pack_weights_kernel(code_ref, near_ref, far_ref, *refs):
    out_ref = refs[-1]
    units = near_ref.shape[1] // 2
    out_ref[:, :units] = near_ref[:, :units]
    out_ref[:, units : 2 * units] = far_ref[:, :units]
    out_ref[:, 2 * units : 3 * units] = near_ref[:, units:]
    out_ref[:, 3 * units : 4 * units] = far_ref[:, units:]
    width = refs[0].shape[1]
    for k, ref in enumerate(refs[:-1]):
        place = pl.multiple_of(4 * units + (code_ref[0] ^ k) * width, width)
        out_ref[:, pl.ds(place, width)] = ref[...]


def pack_weights(near, far, outs, code):
    extent, units = near.shape
    width = outs[0].shape[1]
    columns = 2 * units + len(outs) * width
    whole = lambda shape: pl.BlockSpec(shape, lambda i, *_: (0, 0))
    return pl.pallas_call(
        pack_weights_kernel,
        name="pack_weights",
        out_shape=jax.ShapeDtypeStruct((extent, columns), near.dtype),
        grid_spec=pltpu.PrefetchScalarGridSpec(
            num_scalar_prefetch=1,
            grid=(1,),
            in_specs=[whole((extent, units))] * 2 + [whole((extent, width)) for _ in outs],
            out_specs=whole((extent, columns)),
        ),
        compiler_params=pltpu.CompilerParams(vmem_limit_bytes=24 * 2**20),
        cost_estimate=pl.CostEstimate(flops=0, bytes_accessed=4 * extent * columns, transcendentals=0),
    )(jnp.reshape(code, (1,)).astype(jnp.int32), near, far, *outs)


def row_device(
    first_half,
    second_half,
    first_cotangent,
    second_cotangent,
    segment_ids,
    bucket_ids,
    positions,
    query_weight,
    value_weight,
    output_weight,
    expand_weight,
    expand_bias,
    shrink_weight,
    shrink_bias,
    attention_gain,
    attention_shift,
    forward_gain,
    forward_shift,
):
    bf16, f32 = jnp.bfloat16, jnp.float32
    planes = lax.axis_size("tp")
    shard, ctx, plane = where_am_i()
    seqs_here, width = first_half.shape[1:]
    units = expand_bias.shape[0]
    split = query_weight.shape[0]

    local_pair = jnp.stack(
        [query_weight.reshape(split, -1, DH), value_weight.reshape(split, -1, DH)], 2
    ).reshape(split, -1)
    pair_parts = core_parts(local_pair)
    pair_rows = pair_parts.shape[1] * pair_parts.shape[2] // width
    biases = split_bias(jnp.concatenate([expand_bias, shrink_bias])).reshape(-1, width)
    bias_rows = biases.shape[0]
    biases = jnp.pad(biases, ((0, -bias_rows % 16), (0, 0)))
    extra = jnp.concatenate(
        [pair_parts.reshape(-1, pair_rows, width), jnp.stack([biases] * pair_parts.shape[0])], 1
    )
    (second_rows,), _, extras = rows_in(second_half[None], (), extra)
    biases = extras[:, pair_rows : pair_rows + bias_rows].astype(f32).reshape(planes, 3, -1)
    biases = (biases[:, 0] + biases[:, 1]) + biases[:, 2]
    unit_bias = jnp.concatenate(
        [
            lax.dynamic_index_in_dim(biases, plane, 0, False)[:units],
            lax.dynamic_index_in_dim(biases, plane ^ 2, 0, False)[:units],
        ]
    )
    row_bias = biases[:, units:].reshape(-1)

    pair_wide = extras[:, :pair_rows].reshape((planes,) + pair_parts.shape[1:]).transpose(1, 0, 2)
    pair_wide = plain(pair_wide.reshape(pair_parts.shape[1], -1))
    up, down, out = (
        quarter_of(item, ctx) for item in (expand_weight, shrink_weight.T, output_weight.T)
    )
    quarters = lax.axis_size("ctx")
    pair_pieces, (normed, attn_scaled, attn_inverse), labels, stacked = lax.optimization_barrier(
        (
            [swap(pair_wide, "ctx", j) for j in range(1, quarters)],
            norm_rows(second_rows.astype(f32), attention_gain, attention_shift),
            plane_labels(*after((segment_ids, bucket_ids, positions), second_rows)),
            jnp.stack([first_half, second_cotangent]),
        )
    )
    places, segments, buckets = labels
    normed = normed.astype(bf16)
    pair_mine = pack_rows([pair_wide] + pair_pieces, ctx)
    pair_other = swap(pair_mine, "shard", 1)
    pair = (
        dot(shard_half(normed, shard), pair_mine, NN)
        + dot(shard_half(normed, 1 - shard), pair_other, NN)
    ).astype(bf16)
    sent, out = after((plain(jnp.concatenate([up, down], 1)), plain(out)), pair_mine)
    landed, far, outs_near, hot, bounds = lax.optimization_barrier(
        (
            heads_out(pair),
            swap(sent, "tp", 2),
            [swap(out, "tp", k) for k in range(1, planes)],
            into_places(places, bucket_hot(buckets)),
            doc_bounds(segments),
        )
    )
    wide = pack_weights(sent, far, [out] + outs_near, plane)
    whole = lax.all_gather(after(wide, landed), ("shard", "ctx"), axis=0, tiled=True)
    up_full, down_full, output_full = (
        whole[:, : 2 * units],
        whole[:, 2 * units : 4 * units],
        whole[:, 4 * units :],
    )

    sorted_pair = into_places(places, landed)
    query_sorted, value_sorted = sorted_pair[:, :DH], sorted_pair[:, DH:]
    bounds = with_bound(bounds, landed[:, :DH])
    (first_rows, second_grad_rows), (mix, logs) = rows_in(
        after(stacked, landed),
        attend(bounds, query_sorted, value_sorted, hot),
    )
    far_grad_rows = swap(after(second_grad_rows, mix), "tp", 1)
    attention = heads_back(out_of_places(places, mix.T.astype(bf16)))

    first_out = (first_rows.astype(f32) + dot(attention, output_full, NT)).astype(bf16)
    ffn_in, ffn_scaled, ffn_inverse = norm_rows(first_out.astype(f32), forward_gain, forward_shift)
    ffn_in, far_grad_rows = lax.optimization_barrier((ffn_in.astype(bf16), far_grad_rows))

    def units_of(rows, grad_rows):
        pre_act = dot(rows, up_full, NN) + unit_bias
        below = 0.5 * (1.0 + lax.erf(pre_act * 2**-0.5))
        slope = below + pre_act * (jnp.exp(-0.5 * pre_act * pre_act) * (2 * jnp.pi) ** -0.5)
        pre_grad = (dot(grad_rows, down_full, NN) * slope).astype(bf16)
        return (pre_act * below).astype(bf16), pre_grad

    normed_all = lax.all_gather(after(normed, first_out), ("ctx", "shard"), axis=0, tiled=True)
    far_in, (hidden, pre_grad) = lax.optimization_barrier(
        (swap(ffn_in, "tp", 1), units_of(ffn_in, second_grad_rows))
    )
    (first_grad_rows,), (far_hidden, far_pre_grad) = rows_in(
        after(first_cotangent, far_in)[None], units_of(far_in, far_grad_rows)
    )
    far_ffn_grad = dot(far_pre_grad, up_full, NT).astype(bf16)
    all_rows = jnp.concatenate([ffn_in, far_in], 0)
    all_grad_rows = jnp.concatenate([second_grad_rows, far_grad_rows], 0)
    all_pre_grad = jnp.concatenate([pre_grad, far_pre_grad], 0)
    all_hidden = jnp.concatenate([hidden, far_hidden], 0)
    all_rows, all_grad_rows, pre_grad = after((all_rows, all_grad_rows, pre_grad), far_ffn_grad)
    theirs, far_branch, own_branch, ffn_grad, expand_sums, shrink_sums = lax.optimization_barrier(
        (
            swap(far_ffn_grad, "tp", 1),
            dot(far_hidden, down_full, NT).astype(bf16),
            second_rows.astype(f32) + dot(hidden, down_full, NT) + row_bias,
            dot(pre_grad, up_full, NT),
            chip_sums(all_rows, all_pre_grad).astype(bf16),
            chip_sums(all_grad_rows, all_hidden).astype(bf16),
        )
    )
    ffn_back, ffn_gain_grad, ffn_shift_grad = row_norm_back(
        ffn_grad + theirs.astype(f32), ffn_scaled, ffn_inverse, forward_gain
    )
    first_grad = (first_grad_rows.astype(f32) + ffn_back).astype(bf16)
    attention_grad = dot(first_grad, output_full, NN).astype(bf16)
    shrink_bias_grad = jnp.sum(second_grad_rows.astype(f32), 0)
    expand_bias_grad = jnp.sum(all_pre_grad.astype(f32), 0)
    far_branch = swap(far_branch, "tp", 1)

    spread = jnp.arange(planes, dtype=jnp.int32)[:, None]
    unit_grads = jnp.where(spread == plane, expand_bias_grad[None, :units], 0.0)
    unit_grads = jnp.where(spread == plane ^ 2, expand_bias_grad[None, units:], unit_grads)
    packed = jnp.concatenate(
        [unit_grads]
        + [item.reshape(planes, width) for item in (shrink_bias_grad, ffn_gain_grad, ffn_shift_grad)],
        1,
    )
    packed = (packed + swap(packed, "shard", 1)).astype(bf16).reshape(planes, quarters, -1)
    vector_width = packed.shape[2]
    packed = jnp.pad(packed, ((0, 0), (0, 0), (0, 16 * width - vector_width)))
    packed = packed.reshape(planes, quarters, 16, width).transpose(1, 2, 0, 3)
    packed = jnp.pad(packed.reshape(quarters, 16, -1), ((0, 0), (0, 0), (4 * units, 0)))
    early = jnp.concatenate(
        [expand_sums, shrink_sums, chip_sums(first_grad, attention).astype(bf16)], 1
    )
    early = jnp.concatenate([early.reshape(quarters, split // quarters, -1), packed], 1)
    early = early.reshape(-1, early.shape[2])
    grad_heads, early, normed_all = lax.optimization_barrier(
        (heads_out(attention_grad), early, normed_all)
    )
    early_mine = lax.psum_scatter(early, "ctx", scatter_dimension=0, tiled=True)
    outs_sliced, parts = rows_out(
        after(jnp.stack([first_out, first_grad]), grad_heads),
        seqs_here,
        attend_back(
            bounds, query_sorted, value_sorted, hot, into_places(places, grad_heads), mix, logs
        ),
    )
    far_branch, own_branch = after((far_branch, own_branch), parts)
    second_out = (own_branch + far_branch.astype(f32)).astype(bf16)
    def with_far(pair_grad_heads):
        sums = after(early_mine, pair_grad_heads)
        held = sums[: split // quarters]
        far = jnp.concatenate([held[:, units : 2 * units], held[:, 3 * units : 4 * units]], 1)
        pair_sums = lax.dot_general(
            normed_all, pair_grad_heads, (((0,), (0,)), ((), ())), preferred_element_type=f32
        ).astype(bf16)
        late = sums[:, 4 * units :].reshape(-1, planes, width).transpose(1, 0, 2)
        late = jnp.concatenate([pair_sums.reshape(planes, -1, 2 * DH), late], 1)
        return late, sums, heads_back(pair_grad_heads), swap(far, "tp", 2)

    second_out_sliced, (late, early_mine, pair_grad, far_sums) = rows_out(
        second_out[None],
        seqs_here,
        out_of_places(places, jnp.concatenate(parts, 1)),
        with_far,
    )
    held = early_mine[: split // quarters]
    near_sums = jnp.concatenate([held[:, :units], held[:, 2 * units : 3 * units]], 1)

    grad_mine, grad_other = dot(pair_grad, pair_mine, NT), dot(pair_grad, pair_other, NT)
    normed_grad = jnp.concatenate(
        [
            jnp.where(shard == 0, grad_mine, grad_other),
            jnp.where(shard == 0, grad_other, grad_mine),
        ],
        1,
    )
    attn_back, attn_gain_grad, attn_shift_grad = row_norm_back(
        normed_grad, attn_scaled, attn_inverse, attention_gain
    )
    second_grad = (second_grad_rows.astype(f32) + attn_back).astype(bf16)

    early_own = (near_sums.astype(f32) + far_sums.astype(f32)).astype(bf16)
    pieces = [swap(plane_part(late, k), "tp", k) for k in range(1, planes)]
    late = sum((piece.astype(f32) for piece in pieces), plane_part(late, 0).astype(f32)).astype(bf16)
    split_at = width
    turned = lax.ppermute(
        late[:split_at],
        ("ctx", "tp"),
        [(at * planes + to, to * planes + at) for at in range(quarters) for to in range(planes)],
    )
    norm_grads = jnp.concatenate(
        [attn_gain_grad.reshape(planes, width), attn_shift_grad.reshape(planes, width)], 1
    )
    second_grad_sliced, (early_pieces, turned, norm_pieces) = rows_out(
        second_grad[None],
        seqs_here,
        (
            [swap(early_own, "ctx", j) for j in range(1, quarters)],
            turned,
            [swap(plane_part(norm_grads, k), "tp", k) for k in range(1, planes)],
        ),
    )
    early_own = pack_rows([early_own] + early_pieces, ctx).astype(f32)
    expand_own, shrink_own = early_own[:, :units], early_own[:, units:].T
    norm_own = sum_in_plane(sum(norm_pieces, plane_part(norm_grads, 0))).reshape(2, width)
    late_own = collect_ctx(jnp.concatenate([turned, late[split_at:]], 0)[None])
    pair_head = late_own[:, :split_at].reshape(-1, width)
    late_own = late_own[:, split_at:].astype(f32)
    output_own = late_own[:, : split // quarters].reshape(split, width).T
    owned = late_own[:, split // quarters :].reshape(quarters, -1)[:, :vector_width].reshape(-1)
    row_own = owned[units:].reshape(3, width)
    near = lax.dynamic_slice_in_dim(pair_head, shard * split, split, 0)
    other = swap(lax.dynamic_slice_in_dim(pair_head, (1 - shard) * split, split, 0), "shard", 1)
    pair_own = by_half(near, other).astype(f32)
    query_own = jnp.concatenate([pair_own[0, :, :DH], pair_own[1, :, :DH]], 1)
    value_own = jnp.concatenate([pair_own[0, :, DH:], pair_own[1, :, DH:]], 1)

    return (
        outs_sliced[0],
        second_out_sliced[0],
        outs_sliced[1],
        second_grad_sliced[0],
        query_own,
        value_own,
        output_own,
        expand_own,
        owned[:units],
        shrink_own,
        row_own[0],
        norm_own[0],
        norm_own[1],
        row_own[1],
        row_own[2],
    )


def row_planes(mesh):
    sizes = mesh.shape
    return sizes["tp"] == SEQS and sizes["shard"] == 2 and sizes["ctx"] == 4 and HEADS == 8


def solution(mesh):
    return jax.shard_map(
        row_device if row_planes(mesh) else general_device,
        mesh=mesh,
        in_specs=(
            P("ctx", "shard", "tp"),
            P("ctx", "shard", "tp"),
            P("ctx", "shard", "tp"),
            P("ctx", "shard", "tp"),
            P("shard", "ctx"),
            P("shard", None, "ctx"),
            P("shard", "ctx"),
            P("shard", "tp"),
            P("shard", "tp"),
            P("tp", "shard"),
            P("shard", "tp"),
            P("tp"),
            P("tp", "shard"),
            P("tp"),
            P(),
            P(),
            P(),
            P(),
        ),
        out_specs=(
            P("ctx", "shard", "tp"),
            P("ctx", "shard", "tp"),
            P("ctx", "shard", "tp"),
            P("ctx", "shard", "tp"),
            P("shard", "tp"),
            P("shard", "tp"),
            P("tp", "shard"),
            P("shard", "tp"),
            P("tp"),
            P("tp", "shard"),
            P("tp"),
            P("tp"),
            P("tp"),
            P("tp"),
            P("tp"),
        ),
        check_vma=False,
    )
```
